256 devices in a mesh: tiles: 64 (over y, x_lo, z), probes: 4 (over x_hi, core).
Axes of the slice: x: 4 (x_hi: 2, x_lo: 2; x = x_hi * 2 + x_lo), y: 4, z: 8, core: 2. Of those that a mesh axis runs over, the one named last changes fastest.
Arguments:
- blocks: bfloat16 [4096, 192, 192], P('tiles'), may hold values from -0.21875 to 0.21875
- connectivity: int32 [4096, 64], P('tiles'), may hold values from 0 to 4607, as said below
- basal_map: int32 [4096, 64], P('tiles'), may hold values from 0 to 383
- friction: float32 [4096, 64, 3], P('tiles'), may hold values from 0.2 to 2
- elem_counts: int32 [64], P('tiles'), may hold values from 1 to 64, 3072 in all
- obs_weight: float32 [262144, 3], P('tiles'), may hold values from 0.2 to 2
- sign_bits: int32 [16384, 32], P('tiles', 'probes'), may hold values from 0 to 1
- cluster_ids: int32 [16384], P('tiles'), may hold values from 0 to 63, never falling along the last dimension, each value on 1 to 512 neighbouring positions
Outputs:
- samples: float32 [16384, 32], P('tiles', 'probes')
- refined: float32 [16384, 32], P('tiles', 'probes')
- gram: float32 [64, 32, 32], P(None, 'probes')
The draws below stay inside these ranges and needn't reach their ends.
Inputs may be any that keep to these rules, and one draw needn't show every extreme that they name: `connectivity`: about one reference in eight names a node of the next tile. `elem_counts`: some tile has all 64 slots live. `cluster_ids`: never falling along the cells; each cluster holds 1 to 512 cells.
All inputs are finite; a program needn't handle non-finite values. No bound on the sum of `elem_counts` on one device may be relied on, other than what follows from the above.
Results may differ from the reference program's by a relative error of at most 0.004.
Values may be sent and summed in bfloat16 or wider, within the bound.
A program may use at most 64 MiB of HBM per device.

```python
import math
import jax
import jax.numpy as jnp
import numpy as np
from jax import lax

NPE = 64
DOF = 192
PROBES = 32
E_DEV = 64
NODE = 4096
HALO = 512
POWER = 2
BC = 256
RIM = 64
TILES = 64
ELEMS = 4096
NNODE = 262144
NBAS = 16384
NCL = 64
N_TILES = 64


def draw_connectivity(key, part):
    key_pick = jax.random.fold_in(key, 11)
    key_own = jax.random.fold_in(key, 12)
    key_next = jax.random.fold_in(key, 13)
    choose = jax.random.randint(key_pick, (ELEMS, NPE), 0, 8)
    own_nodes = jax.random.randint(key_own, (ELEMS, NPE), 0, NODE)
    next_nodes = NODE + jax.random.randint(key_next, (ELEMS, NPE), 0, HALO)
    result = jnp.where(choose == 0, next_nodes, own_nodes).astype(jnp.int32)
    result = result.at[0, 0].set(NODE + HALO - 1)
    result = result.at[0, 1].set(0)
    return result


def place_ends(array, stream_key, low, largest):
    spot = [jax.random.randint(jax.random.fold_in(stream_key, axis), (), 0, length) for axis, length in enumerate(array.shape)]
    main_axis = array.shape.index(max(array.shape))
    beside = spot[:main_axis] + [(spot[main_axis] + 1) % array.shape[main_axis]] + spot[main_axis + 1:]
    return array.at[tuple(spot)].set(low).at[tuple(beside)].set(largest)


def shard_levels(key, extent, pieces, least, largest):
    level, own = 1.0, jax.random.fold_in(key, 6)
    for axis_at, blocks in pieces:
        steps = jnp.exp(jax.random.uniform(jax.random.fold_in(own, axis_at), (blocks,), jnp.float32, least / len(pieces), largest / len(pieces)))
        level = level * jnp.repeat(steps, extent[axis_at] // blocks).reshape([-1 if axis == axis_at else 1 for axis in range(len(extent))])
    return level


def split_up(count, total, limit, skew):
    weights = [(1 << 20) // math.isqrt(rank ** skew) + 1 for rank in range(2, count + 1)]
    spare, given = total - limit - (count - 1), [1] * (count - 1)
    while spare > 0:
        candidates = [i for i in range(count - 1) if given[i] < limit]
        whole, left = sum([weights[i] for i in candidates]), spare
        for i in candidates:
            extra = min(limit - given[i], max(1, left * weights[i] // whole), spare)
            given[i] = given[i] + extra
            spare = spare - extra
    return np.array([limit] + given)


def ragged(stream_key, count, total, reach, lean):
    if count == 2:
        one = jax.random.randint(stream_key, (), max(1, total - reach), min(reach, total - 1) + 1)
        return jnp.stack([one, total - one])
    tallies = jnp.asarray(split_up(count, total, reach, lean), jnp.int32)
    couples = (count - 1) // 2
    source_of, sink = tallies[1:1 + 2 * couples:2], tallies[2:2 + 2 * couples:2]
    slack = jnp.minimum(source_of - 1, reach - sink)
    shifted = jax.random.randint(jax.random.fold_in(stream_key, 1), (couples,), 0, 1 << 20) % (slack + 1)
    tallies = tallies.at[1:1 + 2 * couples:2].set(source_of - shifted).at[2:2 + 2 * couples:2].set(sink + shifted)
    return tallies[jax.random.permutation(jax.random.fold_in(stream_key, 2), count)]


def centred(key, extent, scale, reach, pieces=(), kind=jnp.bfloat16):
    factor_of = shard_levels(key, extent, pieces, -0.22, 0.18) if pieces else 1.0
    entries = jax.random.normal(key, extent, jnp.float32) * scale * factor_of
    return jnp.minimum(jnp.maximum(entries, -reach), reach).astype(kind)


def setup_inputs(seed: int = 0) -> dict:
    seeds = jax.random.split(jax.random.key(seed), 9)
    return {
        "blocks": centred(seeds[0], (ELEMS, DOF, DOF), (DOF * 4) ** -0.5, 0.21875, ((0, 64),)),
        "connectivity": draw_connectivity(jax.random.fold_in(seeds[8], 71), 0),
        "basal_map": place_ends(jax.random.randint(seeds[2], (ELEMS, NPE), 0, BC + 2 * RIM), jax.random.fold_in(seeds[2], 1), 0, (BC + 2 * RIM) - 1).astype(jnp.int32),
        "friction": jnp.clip(jnp.exp(math.log(2.0) - 2.3025851 * jax.random.uniform(seeds[3], (ELEMS, NPE, 3), jnp.float32) ** shard_levels(seeds[3], (ELEMS, NPE, 3), ((0, 64),), -0.2, 0.2)), 0.2, 2.0),
        "elem_counts": ragged(seeds[4], TILES, 3 * E_DEV * N_TILES // 4, E_DEV, 2).astype(jnp.int32),
        "obs_weight": jnp.clip(jnp.exp(math.log(2.0) - 2.3025851 * jax.random.uniform(seeds[5], (NNODE, 3), jnp.float32) ** shard_levels(seeds[5], (NNODE, 3), ((0, 64),), -0.2, 0.2)), 0.2, 2.0),
        "sign_bits": place_ends(jax.random.randint(seeds[6], (NBAS, PROBES), 0, 2), jax.random.fold_in(seeds[6], 1), 0, 1).astype(jnp.int32),
        "cluster_ids": jnp.searchsorted(jnp.cumsum(ragged(seeds[7], NCL, NBAS, 2 * BC, 1)), jnp.arange(NBAS), side="right").astype(jnp.int32),
    }


def reference(blocks, connectivity, basal_map, friction, elem_counts, obs_weight, sign_bits, cluster_ids):
    slot_range = jnp.arange(ELEMS, dtype=jnp.int32)
    tile_of = (slot_range // E_DEV).astype(jnp.int32)
    slot_of = (slot_range % E_DEV).astype(jnp.int32)
    alive_slots = slot_of < elem_counts[tile_of]
    node_global = tile_of[:, None] * NODE + connectivity
    node_valid = node_global < NNODE
    node_clip = jnp.clip(node_global, 0, NNODE - 1)
    node_target = jnp.where(node_valid, node_global, NNODE).reshape(-1)
    cell_global = tile_of[:, None] * BC + basal_map - RIM
    cell_valid = (cell_global >= 0) & (cell_global < NBAS)
    cell_clip = jnp.clip(cell_global, 0, NBAS - 1)
    cell_target = jnp.where(cell_valid, cell_global, NBAS).reshape(-1)
    tiled_blocks = blocks.reshape(N_TILES, E_DEV, DOF, DOF)

    def products(vectors, form):

        def one_tile(operands):
            return jnp.einsum(form, operands[0].astype(jnp.float32), operands[1].astype(jnp.float32), precision=lax.Precision.HIGHEST)
        result = lax.map(one_tile, (tiled_blocks, vectors.reshape(N_TILES, E_DEV, DOF, PROBES)))
        return result.reshape(ELEMS, DOF, PROBES)

    def hessian(field):
        gathered = jnp.where(cell_valid[:, :, None], field[cell_clip], jnp.float32(0.0))
        inputs = (friction[:, :, :, None] * gathered[:, :, None, :]).astype(jnp.bfloat16).reshape(ELEMS, DOF, PROBES)
        forward = products(inputs, 'eij,ejp->eip')
        forward = jnp.where(alive_slots[:, None, None], forward, jnp.float32(0.0))
        assembled = jax.ops.segment_sum(forward.reshape(ELEMS * NPE, 3 * PROBES), node_target, num_segments=NNODE + 1)[:NNODE]
        weighted = (obs_weight[:, :, None] * assembled.reshape(NNODE, 3, PROBES)).astype(jnp.bfloat16)
        adjoint_in = jnp.where(node_valid[:, :, None, None], weighted[node_clip], jnp.zeros((), jnp.bfloat16))
        adjoint_out = products(adjoint_in.reshape(ELEMS, DOF, PROBES), 'eji,ejp->eip')
        partials = lax.optimization_barrier(jnp.sum(friction[:, :, :, None] * adjoint_out.reshape(ELEMS, NPE, 3, PROBES), axis=2))
        partials = jnp.where(alive_slots[:, None, None], partials, jnp.float32(0.0))
        return jax.ops.segment_sum(partials.reshape(ELEMS * NPE, PROBES), cell_target, num_segments=NBAS + 1)[:NBAS]
    parity = jnp.arange(PROBES, dtype=jnp.int32) % 2
    same_colour = (cluster_ids % 2)[:, None] == parity[None, :]
    probe_start = jnp.where(same_colour, (2 * sign_bits - 1).astype(jnp.float32), jnp.float32(0.0))
    samples = jnp.where(same_colour, jnp.float32(0.0), hessian(probe_start))
    current = samples
    for power_step in range(POWER):
        rms_scale = jnp.sqrt(lax.optimization_barrier(jnp.sum(current * current, axis=0)) / NBAS + 1e-06)
        applied = hessian(current / rms_scale)
        if power_step % 2 == 0:
            current = jnp.where(same_colour, applied, jnp.float32(0.0))
        else:
            current = jnp.where(same_colour, jnp.float32(0.0), applied)
    refined = current
    onehot = (cluster_ids[:, None] == jnp.arange(NCL, dtype=jnp.int32)[None, :]).astype(jnp.float32)
    outer = refined[:, :, None] * refined[:, None, :]
    gram = jnp.dot(onehot.T, outer.reshape(NBAS, PROBES * PROBES), precision=lax.Precision.HIGHEST).reshape(NCL, PROBES, PROBES)
    return (samples, refined, gram)
```

```python
import functools

import jax
import jax.numpy as jnp
from jax import lax
from jax.experimental import pallas as pl
from jax.experimental.pallas import tpu as pltpu
from jax.sharding import PartitionSpec as P

F32 = jnp.float32
BF16 = jnp.bfloat16
I32 = jnp.int32
POWER = 2
ROUNDS = POWER + 1
RIM = 64
ELEMS = 64
DOF = 192
PAIRS = 32
CHUNKS = 16
ZS = 8
YXS = 8
GROUPS = 4
EDGE = (0, 1, 16, 17)
INNER = tuple(range(2, 16))
NT = (((1,), (1,)), ((), ()))
NN = (((1,), (0,)), ((), ()))
MESH = pl.DeviceIdType.MESH


def mo(x, n):
    return pl.multiple_of(x, n)


def split(x):
    hi = x.astype(BF16).astype(F32)
    return hi, x - hi


def dot(a, b, dims=NN):
    return lax.dot_general(a, b, dims, preferred_element_type=F32)


def kernel(
    blk_hbm, idx_ref, fr_ref, w_ref, qs_ref, cl_ref,
    samp_ref, refd_ref, gram_ref,
    blk, ohn, ohnt, ohc, ohct, an8, ac8, fr8, rep, sel, pm, pmt,
    gh, gl, xin, fw, fc, acce, acci, te, ti, ad1, ad, ain, yh, yl, pt,
    wn, qsp, qsn, renext, reprev, bs, rbn, rbp, pa, pb, cp, gk, ka, kb, kc,
    blk_sem, i_s, i_r, e_s, e_r, b_s, b_r, p_s, p_r, g_s, g_r, k_s, k_r,
):
    tile = lax.axis_index("tiles")
    group = lax.axis_index("probes")
    tiles = lax.axis_size("tiles")
    nxt = lax.rem(tile + 1, tiles)
    prv = lax.rem(tile + tiles - 1, tiles)
    my_z = lax.rem(tile, ZS)
    my_yx = lax.div(tile, ZS)
    has_prev = jnp.where(tile > 0, 1.0, 0.0).astype(F32)
    has_next = jnp.where(tile < tiles - 1, 1.0, 0.0).astype(F32)

    def z_peer(d):
        return lax.rem(my_z + d, ZS)

    def yx_peer(d):
        return lax.rem(my_yx + d, YXS)

    def z_device(z):
        return (my_yx * ZS + z, group)

    def yx_device(yx):
        return (yx * ZS + my_z, group)

    def rcopy(src, dst, ss, rs, dev):
        return pltpu.make_async_remote_copy(
            src_ref=src, dst_ref=dst, send_sem=ss, recv_sem=rs, device_id=dev, device_id_type=MESH
        )

    load = pltpu.make_async_copy(blk_hbm, blk, blk_sem)
    load.start()

    barrier = pltpu.get_barrier_semaphore()

    def greet(dev):
        pl.semaphore_signal(barrier, inc=1, device_id=dev, device_id_type=MESH)

    greet((nxt, group))
    greet((prv, group))
    for d in range(1, ZS):
        greet(z_device(z_peer(d)))
    for d in range(1, YXS):
        greet(yx_device(yx_peer(d)))
    for d in range(1, GROUPS):
        greet((tile, lax.rem(group + d, GROUPS)))

    def one(cond):
        return jnp.where(cond, 1.0, 0.0).astype(BF16)

    def pair_col(lane):
        half = lane >> 8
        j = lane & 255
        k = (j * 171) >> 9
        return half, k, j - 3 * k, j < DOF

    r = lax.broadcasted_iota(I32, (128, 512), 0)
    half, k, c, ok = pair_col(lax.broadcasted_iota(I32, (128, 512), 1))
    rep[...] = one((r == half * 64 + k) & ok)
    half, k, c, ok = pair_col(lax.broadcasted_iota(I32, (512, 128), 0))
    r = lax.broadcasted_iota(I32, (512, 128), 1)
    sel[...] = one((r == half * 64 + k) & ok)
    r = lax.broadcasted_iota(I32, (384, 512), 0)
    half, k, c, ok = pair_col(lax.broadcasted_iota(I32, (384, 512), 1))
    pm[...] = one((r == c * 128 + half * 64 + k) & ok)
    half, k, c, ok = pair_col(lax.broadcasted_iota(I32, (512, 384), 0))
    r = lax.broadcasted_iota(I32, (512, 384), 1)
    pmt[...] = one((r == c * 128 + half * 64 + k) & ok)

    fw[...] = jnp.zeros(fw.shape, BF16)
    yh[...] = jnp.zeros(yh.shape, BF16)
    yl[...] = jnp.zeros(yl.shape, BF16)

    for i in range(PAIRS):
        rows = slice(i * 8, i * 8 + 8)
        fr8[rows, :] = jnp.broadcast_to(fr_ref[i : i + 1, :], (8, 512))
    for i in range(CHUNKS):
        rows = slice(i * 8, i * 8 + 8)
        for j in range(2):
            lanes = slice(j * 128, j * 128 + 128)
            n = 2 * i + j
            an8[rows, lanes] = jnp.broadcast_to(idx_ref[n : n + 1, :] >> 8, (8, 128))
            ac8[rows, lanes] = jnp.broadcast_to(idx_ref[PAIRS + n : PAIRS + n + 1, :] >> 7, (8, 128))

    low = jnp.where(
        lax.broadcasted_iota(I32, (64, 128), 0) < PAIRS, idx_ref[...] & 255, idx_ref[...] & 127
    ).astype(F32)
    cols = jnp.transpose(jnp.concatenate([low, jnp.zeros((64, 128), F32)], axis=0))
    sub_n = lax.broadcasted_iota(I32, (256, 128), 0)
    sub_c = lax.broadcasted_iota(I32, (128, 128), 0)
    lane_n = lax.broadcasted_iota(I32, (128, 256), 1).astype(F32)
    lane_c = lax.broadcasted_iota(I32, (128, 128), 1).astype(F32)
    for i in range(PAIRS):
        span = slice(i * 128, i * 128 + 128)
        ohn[:, span] = one(sub_n == (idx_ref[i : i + 1, :] & 255))
        ohc[:, span] = one(sub_c == (idx_ref[PAIRS + i : PAIRS + i + 1, :] & 127))
        ohnt[span, :] = one(lane_n == cols[:, i : i + 1])
        ohct[span, :] = one(lane_c == cols[:, PAIRS + i : PAIRS + i + 1])

    pl.semaphore_wait(barrier, 2 + ZS - 1 + YXS - 1 + GROUPS - 1)

    first = [
        rcopy(qs_ref.at[:, pl.ds(256, 128)], qsp, i_s.at[0], i_r.at[0], (nxt, group)),
        rcopy(qs_ref.at[:, pl.ds(0, 128)], qsn, i_s.at[1], i_r.at[1], (prv, group)),
        rcopy(w_ref.at[pl.ds(0, 8), :], wn, i_s.at[2], i_r.at[2], (prv, group)),
    ]
    for cpy in first:
        cpy.start()
    for cpy in first:
        cpy.wait()
    load.wait()

    lane = lax.broadcasted_iota(I32, (8, 128), 1)
    upper = jnp.where(lane >= RIM, 1.0, 0.0).astype(F32)
    own = [upper, jnp.ones((8, 128), F32), 1.0 - upper]
    exist = [
        upper + (1.0 - upper) * has_prev,
        jnp.ones((8, 128), F32),
        (1.0 - upper) + upper * has_next,
    ]
    q = [
        qs_ref[0:8, 0:128] + qsp[0:8, :] * has_prev,
        qs_ref[0:8, 128:256],
        qs_ref[0:8, 256:384] + qsn[0:8, :] * has_next,
    ]
    same = [
        qs_ref[8:16, 0:128] + qsp[8:16, :] * has_prev,
        qs_ref[8:16, 128:256],
        qs_ref[8:16, 256:384] + qsn[8:16, :] * has_next,
    ]

    def square_start(i, cur):
        total = cur[0] * cur[0] * own[0] + cur[1] * cur[1] + cur[2] * cur[2] * own[2]
        pa[i, my_z] = total
        for d in range(1, ZS):
            rcopy(
                pa.at[i, my_z], pa.at[i, my_z], p_s.at[i, 0, d], p_r.at[i, 0, my_z],
                z_device(z_peer(d)),
            ).start()

    def square_mid(i):
        for d in range(1, ZS):
            z = z_peer(d)
            got = rcopy(pa.at[i, z], pa.at[i, z], p_s.at[i, 0, d], p_r.at[i, 0, z], z_device(z))
            got.wait_recv()
            got.wait_send()
        total = pa[i, 0]
        for z in range(1, ZS):
            total = total + pa[i, z]
        pb[i, my_yx] = total
        for d in range(1, YXS):
            rcopy(
                pb.at[i, my_yx], pb.at[i, my_yx], p_s.at[i, 1, d], p_r.at[i, 1, my_yx],
                yx_device(yx_peer(d)),
            ).start()

    def square_end(i):
        for d in range(1, YXS):
            yx = yx_peer(d)
            got = rcopy(
                pb.at[i, yx], pb.at[i, yx], p_s.at[i, 1, d], p_r.at[i, 1, yx], yx_device(yx)
            )
            got.wait_recv()
            got.wait_send()
        total = pb[i, 0]
        for yx in range(1, YXS):
            total = total + pb[i, yx]
        mean = jnp.sum(total, axis=1, keepdims=True) / (256 * tiles)
        return 1.0 / jnp.sqrt(mean + 1e-06)

    row16 = lax.broadcasted_iota(I32, (16, DOF), 0) < 8

    def scatter_nodes(m, levels):
        r0 = mo(m * 16, 16)
        parts = []
        for c in range(3):
            span = slice(c * 128, c * 128 + 128)
            parts.append(
                jnp.concatenate([fc[pl.ds(r0, 8), span], fc[pl.ds(r0 + 8, 8), span]], axis=1)
            )
        a = an8[pl.ds(mo(m * 8, 8), 8), :]
        spread = jnp.concatenate(
            [jnp.where(a == lv, parts[c], 0.0) for lv in levels for c in range(3)], axis=0
        )
        return dot(spread.astype(BF16), ohnt[pl.ds(mo(m * 256, 256), 256), :])

    def gather_nodes(m, table, levels, base):
        got = dot(table[...], ohn[:, pl.ds(mo(m * 256, 256), 256)])
        a = an8[pl.ds(mo(m * 8, 8), 8), :]
        out = list(base)
        for n, lv in enumerate(levels):
            hit = a == lv
            for c in range(3):
                row = (n * 3 + c) * 8
                out[c] = jnp.where(hit, got[row : row + 8], out[c])
        return out

    def hessian(h, q):
        parts = []
        for b in q:
            parts += list(split(b))
        cells = jnp.concatenate(parts, axis=0).astype(BF16)

        @pl.loop(0, CHUNKS)
        def _(m):
            got = dot(cells, ohc[:, pl.ds(mo(m * 256, 256), 256)])
            a = ac8[pl.ds(mo(m * 8, 8), 8), :]
            g = jnp.where(
                a == 0,
                got[0:8] + got[8:16],
                jnp.where(a == 1, got[16:24] + got[24:32], got[32:40] + got[40:48]),
            )
            hi, lo = split(g)
            rows = pl.ds(mo(m * 16, 16), 16)
            gh[rows, :] = jnp.concatenate([hi[:, :128], hi[:, 128:]], axis=0).astype(BF16)
            gl[rows, :] = jnp.concatenate([lo[:, :128], lo[:, 128:]], axis=0).astype(BF16)

        for i in range(4):
            rows = slice(i * 64, i * 64 + 64)
            wide = dot(gh[rows, :], rep[...]) + dot(gl[rows, :], rep[...])
            xin[rows, :] = (wide * fr8[rows, :]).astype(BF16)

        @pl.loop(0, CHUNKS)
        def _(m):
            rows = pl.ds(mo(m * 16, 16), 16)
            for half in range(2):
                span = slice(half * 256, half * 256 + DOF)
                x = xin[rows, span]
                o0 = dot(x, blk[4 * m + half], NT)
                o1 = dot(x, blk[4 * m + 2 + half], NT)
                fw[rows, span] = jnp.where(row16, o0, o1).astype(BF16)

        for i in range(4):
            rows = slice(i * 64, i * 64 + 64)
            fc[rows, :] = dot(fw[rows, :], pmt[...])

        acce[...] = jnp.zeros(acce.shape, F32)
        acci[...] = jnp.zeros(acci.shape, F32)

        @pl.loop(0, CHUNKS)
        def _(m):
            acce[...] += scatter_nodes(m, EDGE)

        swap = [
            rcopy(acce.at[pl.ds(0, 48), :], renext.at[h], e_s.at[h, 0], e_r.at[h, 0], (prv, group)),
            rcopy(acce.at[pl.ds(48, 48), :], reprev.at[h], e_s.at[h, 1], e_r.at[h, 1], (nxt, group)),
        ]
        for cpy in swap:
            cpy.start()

        @pl.loop(0, CHUNKS)
        def _(m):
            acci[...] += scatter_nodes(m, INNER)

        if h > 0:
            square_mid(h - 1)

        for i in range(21):
            pair = []
            for j in range(2):
                n = 2 * i + j
                pair.append(acci[n * 8 : n * 8 + 8, :] * w_ref[6 + n : 7 + n, :])
            ti[i * 16 : i * 16 + 16, :] = jnp.concatenate(pair, axis=0).astype(BF16)

        @pl.loop(0, CHUNKS)
        def _(m):
            zero = jnp.zeros((8, 256), F32)
            out = gather_nodes(m, ti, INNER, [zero] * 3)
            r0 = mo(m * 16, 16)
            for c in range(3):
                span = slice(c * 128, c * 128 + 128)
                ad1[pl.ds(r0, 8), span] = out[c][:, :128]
                ad1[pl.ds(r0 + 8, 8), span] = out[c][:, 128:]

        for cpy in swap:
            cpy.wait()
        for i in range(6):
            pair = []
            for j in range(2):
                n = 2 * i + j
                if n < 6:
                    total = acce[n * 8 : n * 8 + 8, :] + reprev[h, n * 8 : n * 8 + 8, :] * has_prev
                    pair.append(total * w_ref[n : n + 1, :])
                else:
                    o = (n - 6) * 8
                    total = acce[n * 8 : n * 8 + 8, :] + renext[h, o : o + 8, :]
                    pair.append(total * (wn[n - 6 : n - 5, :] * has_next))
            te[i * 16 : i * 16 + 16, :] = jnp.concatenate(pair, axis=0).astype(BF16)

        @pl.loop(0, CHUNKS)
        def _(m):
            r0 = mo(m * 16, 16)
            base = []
            for c in range(3):
                span = slice(c * 128, c * 128 + 128)
                base.append(
                    jnp.concatenate([ad1[pl.ds(r0, 8), span], ad1[pl.ds(r0 + 8, 8), span]], axis=1)
                )
            out = gather_nodes(m, te, EDGE, base)
            for c in range(3):
                span = slice(c * 128, c * 128 + 128)
                ad[pl.ds(r0, 16), span] = jnp.concatenate(
                    [out[c][:, :128], out[c][:, 128:]], axis=0
                ).astype(BF16)

        for i in range(4):
            rows = slice(i * 64, i * 64 + 64)
            ain[rows, :] = dot(ad[rows, :], pm[...]).astype(BF16)

        @pl.loop(0, CHUNKS)
        def _(m):
            rows = pl.ds(mo(m * 16, 16), 16)
            for half in range(2):
                span = slice(half * 256, half * 256 + DOF)
                x = ain[rows, span]
                o0 = dot(x, blk[4 * m + half])
                o1 = dot(x, blk[4 * m + 2 + half])
                hi, lo = split(jnp.where(row16, o0, o1) * fr8[rows, span])
                yh[rows, span] = hi.astype(BF16)
                yl[rows, span] = lo.astype(BF16)

        for i in range(4):
            rows = slice(i * 64, i * 64 + 64)
            pt[rows, :] = dot(yh[rows, :], sel[...]) + dot(yl[rows, :], sel[...])

        def scatter_cells(m, acc):
            r0 = mo(m * 16, 16)
            v = jnp.concatenate([pt[pl.ds(r0, 8), :], pt[pl.ds(r0 + 8, 8), :]], axis=1)
            a = ac8[pl.ds(mo(m * 8, 8), 8), :]
            spread = jnp.concatenate(
                [jnp.where(a == lv, s, 0.0) for lv in range(3) for s in split(v)], axis=0
            )
            return acc + dot(spread.astype(BF16), ohct[pl.ds(mo(m * 256, 256), 256), :])

        acc = lax.fori_loop(0, CHUNKS, scatter_cells, jnp.zeros((48, 128), F32))
        sums = [acc[n * 16 : n * 16 + 8] + acc[n * 16 + 8 : n * 16 + 16] for n in range(3)]
        bs[h, 0] = sums[0]
        bs[h, 1] = sums[2]
        swap = [
            rcopy(bs.at[h, 0], rbn.at[h], b_s.at[h, 0], b_r.at[h, 0], (prv, group)),
            rcopy(bs.at[h, 1], rbp.at[h], b_s.at[h, 1], b_r.at[h, 1], (nxt, group)),
        ]
        for cpy in swap:
            cpy.start()
        scale = square_end(h - 1) if h > 0 else None
        for cpy in swap:
            cpy.wait()
        sums[0] = sums[0] + rbp[h] * has_prev
        sums[2] = sums[2] + rbn[h] * has_next
        keep = same if h % 2 == 1 else [exist[n] - same[n] for n in range(3)]
        out = []
        for n in range(3):
            v = sums[n] * keep[n]
            out.append(v if scale is None else v * scale)
        return out

    for h in range(ROUNDS):
        q = hessian(h, q)
        if h < POWER:
            square_start(h, q)
        if h == 0:
            for n in range(3):
                samp_ref[:, n * 128 : n * 128 + 128] = q[n]
    for n in range(3):
        refd_ref[:, n * 128 : n * 128 + 128] = q[n]

    mine = pltpu.roll(refd_ref[...], 384 - RIM, 1)[:, :256]
    cp[group] = mine
    for d in range(1, GROUPS):
        rcopy(
            cp.at[group], cp.at[group], g_s.at[d], g_r.at[group], (tile, lax.rem(group + d, GROUPS))
        ).start()
    for d in range(1, GROUPS):
        g = lax.rem(group + d, GROUPS)
        got = rcopy(cp.at[g], cp.at[g], g_s.at[d], g_r.at[g], (tile, g))
        got.wait_recv()
        got.wait_send()
    every = jnp.concatenate([cp[g] for g in range(GROUPS)], axis=0)
    outer = jnp.concatenate([every * mine[i : i + 1, :] for i in range(8)], axis=0)
    hi, lo = split(outer)
    member = one(lax.broadcasted_iota(I32, (64, 256), 0) == cl_ref[...])
    gk[...] = dot(member, hi.astype(BF16), NT) + dot(member, lo.astype(BF16), NT)

    ka[my_z] = gk[pl.ds(mo(my_z * 8, 8), 8), :]
    for d in range(1, ZS):
        z = z_peer(d)
        rcopy(
            gk.at[pl.ds(mo(z * 8, 8), 8), :], ka.at[my_z], k_s.at[0, d], k_r.at[0, my_z],
            z_device(z),
        ).start()
    for d in range(1, ZS):
        z = z_peer(d)
        got = rcopy(ka.at[z], ka.at[z], k_s.at[0, d], k_r.at[0, z], z_device(z))
        got.wait_recv()
        got.wait_send()
    total = ka[0]
    for z in range(1, ZS):
        total = total + ka[z]
    kb[my_yx] = total
    for d in range(1, YXS):
        rcopy(
            kb.at[my_yx], kb.at[my_yx], k_s.at[1, d], k_r.at[1, my_yx], yx_device(yx_peer(d))
        ).start()
    for d in range(1, YXS):
        yx = yx_peer(d)
        got = rcopy(kb.at[yx], kb.at[yx], k_s.at[1, d], k_r.at[1, yx], yx_device(yx))
        got.wait_recv()
        got.wait_send()
    total = kb[0]
    for yx in range(1, YXS):
        total = total + kb[yx]
    kc[my_z] = total
    for d in range(1, ZS):
        rcopy(
            kc.at[my_z], kc.at[my_z], k_s.at[2, d], k_r.at[2, my_z], z_device(z_peer(d))
        ).start()
    for d in range(1, ZS):
        z = z_peer(d)
        got = rcopy(kc.at[z], kc.at[z], k_s.at[2, d], k_r.at[2, z], z_device(z))
        got.wait_recv()
        got.wait_send()
    for z in range(ZS):
        gram_ref[z * 8 : z * 8 + 8, :] = kc[z]


def shards(
    blocks, connectivity, basal_map, friction, elem_counts, obs_weight, sign_bits, cluster_ids
):
    live = jnp.arange(ELEMS, dtype=I32) < elem_counts[0]
    fr = jnp.where(live[:, None], friction.reshape(ELEMS, DOF), 0.0)
    fr = jnp.pad(fr, ((0, 0), (0, 256 - DOF))).reshape(PAIRS, 512)
    idx = jnp.concatenate([connectivity.reshape(PAIRS, 128), basal_map.reshape(PAIRS, 128)], axis=0)
    w = obs_weight.reshape(16, 256, 3).transpose(0, 2, 1).reshape(48, 256)
    parity = jnp.arange(8, dtype=I32)[:, None] % 2
    same = (cluster_ids % 2)[None, :] == parity
    start = jnp.where(same, (2 * sign_bits.T - 1).astype(F32), 0.0)
    qs = jnp.pad(jnp.concatenate([start, same.astype(F32)], axis=0), ((0, 0), (RIM, RIM)))
    cl = cluster_ids.reshape(1, 256)

    vmem = pl.BlockSpec(memory_space=pltpu.VMEM)
    dma = pltpu.SemaphoreType.DMA
    samp, refd, gram = pl.pallas_call(
        kernel,
        out_shape=(
            jax.ShapeDtypeStruct((8, 384), F32),
            jax.ShapeDtypeStruct((8, 384), F32),
            jax.ShapeDtypeStruct((64, 256), F32),
        ),
        in_specs=[pl.BlockSpec(memory_space=pl.ANY)] + [vmem] * 5,
        out_specs=(vmem, vmem, vmem),
        scratch_shapes=[
            pltpu.VMEM((ELEMS, DOF, DOF), BF16),
            pltpu.VMEM((256, 4096), BF16),
            pltpu.VMEM((4096, 256), BF16),
            pltpu.VMEM((128, 4096), BF16),
            pltpu.VMEM((4096, 128), BF16),
            pltpu.VMEM((128, 256), I32),
            pltpu.VMEM((128, 256), I32),
            pltpu.VMEM((256, 512), F32),
            pltpu.VMEM((128, 512), BF16),
            pltpu.VMEM((512, 128), BF16),
            pltpu.VMEM((384, 512), BF16),
            pltpu.VMEM((512, 384), BF16),
            pltpu.VMEM((256, 128), BF16),
            pltpu.VMEM((256, 128), BF16),
            pltpu.VMEM((256, 512), BF16),
            pltpu.VMEM((256, 512), BF16),
            pltpu.VMEM((256, 384), F32),
            pltpu.VMEM((96, 256), F32),
            pltpu.VMEM((336, 256), F32),
            pltpu.VMEM((96, 256), BF16),
            pltpu.VMEM((336, 256), BF16),
            pltpu.VMEM((256, 384), F32),
            pltpu.VMEM((256, 384), BF16),
            pltpu.VMEM((256, 512), BF16),
            pltpu.VMEM((256, 512), BF16),
            pltpu.VMEM((256, 512), BF16),
            pltpu.VMEM((256, 128), F32),
            pltpu.VMEM((8, 256), F32),
            pltpu.VMEM((16, 128), F32),
            pltpu.VMEM((16, 128), F32),
            pltpu.VMEM((ROUNDS, 48, 256), F32),
            pltpu.VMEM((ROUNDS, 48, 256), F32),
            pltpu.VMEM((ROUNDS, 2, 8, 128), F32),
            pltpu.VMEM((ROUNDS, 8, 128), F32),
            pltpu.VMEM((ROUNDS, 8, 128), F32),
            pltpu.VMEM((POWER, ZS, 8, 128), F32),
            pltpu.VMEM((POWER, YXS, 8, 128), F32),
            pltpu.VMEM((GROUPS, 8, 256), F32),
            pltpu.VMEM((64, 256), F32),
            pltpu.VMEM((ZS, 8, 256), F32),
            pltpu.VMEM((YXS, 8, 256), F32),
            pltpu.VMEM((ZS, 8, 256), F32),
            dma,
            dma((3,)),
            dma((3,)),
            dma((ROUNDS, 2)),
            dma((ROUNDS, 2)),
            dma((ROUNDS, 2)),
            dma((ROUNDS, 2)),
            dma((POWER, 2, 8)),
            dma((POWER, 2, 8)),
            dma((GROUPS,)),
            dma((GROUPS,)),
            dma((3, 8)),
            dma((3, 8)),
        ],
        compiler_params=pltpu.CompilerParams(
            collective_id=0, has_side_effects=True, vmem_limit_bytes=48 * 1024 * 1024
        ),
    )(blocks, idx, fr, w, qs, cl)
    samples = samp[:, RIM : RIM + 256].T
    refined = refd[:, RIM : RIM + 256].T
    return samples, refined, gram.reshape(64, 8, 32)


def solution(mesh):
    in_specs = (
        P("tiles", None, None),
        P("tiles", None),
        P("tiles", None),
        P("tiles", None, None),
        P("tiles"),
        P("tiles", None),
        P("tiles", "probes"),
        P("tiles"),
    )
    out_specs = (P("tiles", "probes"), P("tiles", "probes"), P(None, "probes", None))
    return jax.shard_map(shards, mesh=mesh, in_specs=in_specs, out_specs=out_specs, check_vma=False)
```

```python
import functools

import jax
import jax.numpy as jnp
from jax import lax
from jax.experimental import pallas as pl
from jax.experimental.pallas import tpu as pltpu
from jax.sharding import PartitionSpec as P

F32 = jnp.float32
BF16 = jnp.bfloat16
I32 = jnp.int32
POWER = 2
ROUNDS = POWER + 1
RIM = 64
ELEMS = 64
DOF = 192
PAIRS = 32
CHUNKS = 16
U_IN = 16
U_PROD = 16
U_EDGE = 16
U_INNER = 16
U_GET = 16
U_PUT = 16
ZS = 8
YXS = 8
GROUPS = 4
EDGE = (0, 1, 16, 17)
INNER = tuple(range(2, 16))
NT = (((1,), (1,)), ((), ()))
NN = (((1,), (0,)), ((), ()))
MESH = pl.DeviceIdType.MESH


def mo(x, n):
    return pl.multiple_of(x, n)


def each(unroll, body):
    @pl.loop(0, CHUNKS // unroll)
    def _(n):
        for j in range(unroll):
            body(n * unroll + j)


def split(x):
    hi = x.astype(BF16).astype(F32)
    return hi, x - hi


def dot(a, b, dims=NN):
    return lax.dot_general(a, b, dims, preferred_element_type=F32)


def kernel(
    blk_hbm, conn_hbm, cell_hbm, fr_hbm, count_ref, w_hbm, sign_hbm, cl_hbm,
    samp_ref, refd_ref, gram_ref,
    conn, cell, fr3, w3, sign, cl_ref, idx_ref, qs_ref,
    blk, ohn, ohnt, ohc, ohct, an8, ac8, fr8, rep, sel, pm, pmt,
    gh, gl, xin, fw, fc, acce, acci, te, ti, ad1, ad, ain, yh, yl, pt,
    wn, qsp, qsn, renext, reprev, bs, rbn, rbp, pa, pb, cp, gk, ka, kb, kc,
    blk_sem, in_sem, i_s, i_r, e_s, e_r, b_s, b_r, p_s, p_r, g_s, g_r, k_s, k_r,
):
    tile = lax.axis_index("tiles")
    group = lax.axis_index("probes")
    tiles = lax.axis_size("tiles")
    nxt = lax.rem(tile + 1, tiles)
    prv = lax.rem(tile + tiles - 1, tiles)
    my_z = lax.rem(tile, ZS)
    my_yx = lax.div(tile, ZS)
    has_prev = jnp.where(tile > 0, 1.0, 0.0).astype(F32)
    has_next = jnp.where(tile < tiles - 1, 1.0, 0.0).astype(F32)

    def z_peer(d):
        return lax.rem(my_z + d, ZS)

    def yx_peer(d):
        return lax.rem(my_yx + d, YXS)

    def z_device(z):
        return (my_yx * ZS + z, group)

    def yx_device(yx):
        return (yx * ZS + my_z, group)

    def rcopy(src, dst, ss, rs, dev):
        return pltpu.make_async_remote_copy(
            src_ref=src, dst_ref=dst, send_sem=ss, recv_sem=rs, device_id=dev, device_id_type=MESH
        )

    small = [
        pltpu.make_async_copy(src, dst, in_sem.at[n])
        for n, (src, dst) in enumerate(
            [(sign_hbm, sign), (cl_hbm, cl_ref), (w_hbm, w3), (conn_hbm, conn), (cell_hbm, cell), (fr_hbm, fr3)]
        )
    ]
    for cpy in small:
        cpy.start()
    load = pltpu.make_async_copy(blk_hbm, blk, blk_sem)
    load.start()

    barrier = pltpu.get_barrier_semaphore()

    def greet(dev):
        pl.semaphore_signal(barrier, inc=1, device_id=dev, device_id_type=MESH)

    greet((nxt, group))
    greet((prv, group))
    for d in range(1, ZS):
        greet(z_device(z_peer(d)))
    for d in range(1, YXS):
        greet(yx_device(yx_peer(d)))
    for d in range(1, GROUPS):
        greet((tile, lax.rem(group + d, GROUPS)))

    def one(cond):
        return jnp.where(cond, 1.0, 0.0).astype(BF16)

    def pair_col(lane):
        half = lane >> 8
        j = lane & 255
        k = (j * 171) >> 9
        return half, k, j - 3 * k, j < DOF

    r = lax.broadcasted_iota(I32, (128, 512), 0)
    half, k, c, ok = pair_col(lax.broadcasted_iota(I32, (128, 512), 1))
    rep[...] = one((r == half * 64 + k) & ok)
    half, k, c, ok = pair_col(lax.broadcasted_iota(I32, (512, 128), 0))
    r = lax.broadcasted_iota(I32, (512, 128), 1)
    sel[...] = one((r == half * 64 + k) & ok)
    r = lax.broadcasted_iota(I32, (384, 512), 0)
    half, k, c, ok = pair_col(lax.broadcasted_iota(I32, (384, 512), 1))
    pm[...] = one((r == c * 128 + half * 64 + k) & ok)
    half, k, c, ok = pair_col(lax.broadcasted_iota(I32, (512, 384), 0))
    r = lax.broadcasted_iota(I32, (512, 384), 1)
    pmt[...] = one((r == c * 128 + half * 64 + k) & ok)

    fw[...] = jnp.zeros(fw.shape, BF16)
    yh[...] = jnp.zeros(yh.shape, BF16)
    yl[...] = jnp.zeros(yl.shape, BF16)

    for cpy in small:
        cpy.wait()

    same_own = (cl_ref[...] & 1) == (lax.broadcasted_iota(I32, (8, 256), 0) & 1)
    start = jnp.where(same_own, (2 * sign[...] - 1).astype(F32), 0.0)
    both = jnp.concatenate([start, jnp.where(same_own, 1.0, 0.0).astype(F32)], axis=0)
    qs_ref[...] = pltpu.roll(
        jnp.concatenate([both, jnp.zeros((16, 128), F32)], axis=1), RIM, 1
    )
    first = [
        rcopy(qs_ref.at[:, pl.ds(256, 128)], qsp, i_s.at[0], i_r.at[0], (nxt, group)),
        rcopy(qs_ref.at[:, pl.ds(0, 128)], qsn, i_s.at[1], i_r.at[1], (prv, group)),
        rcopy(w3.at[:, pl.ds(0, 512)], wn, i_s.at[2], i_r.at[2], (prv, group)),
    ]
    pl.semaphore_wait(barrier, 2 + ZS - 1 + YXS - 1 + GROUPS - 1)
    for cpy in first:
        cpy.start()

    idx_ref[0:PAIRS, :] = jnp.concatenate([conn[0:PAIRS, :], conn[PAIRS:ELEMS, :]], axis=1)
    idx_ref[PAIRS:ELEMS, :] = jnp.concatenate([cell[0:PAIRS, :], cell[PAIRS:ELEMS, :]], axis=1)
    element = lax.broadcasted_iota(I32, (PAIRS, 128), 0) + jnp.where(
        lax.broadcasted_iota(I32, (PAIRS, 128), 1) < 64, 0, PAIRS
    )
    live = element < count_ref[0]
    wide = []
    for c in range(3):
        f = jnp.concatenate([fr3[c, 0:PAIRS, :], fr3[c, PAIRS:ELEMS, :]], axis=1)
        wide.append(jnp.where(live, f, 0.0))
    wide = jnp.concatenate(wide, axis=1)
    hi, rest = split(wide)
    mid, lo = split(rest)
    third = dot(jnp.concatenate([hi, mid, lo], axis=0).astype(BF16), pm[...])
    fr = third[0:PAIRS] + third[PAIRS : 2 * PAIRS] + third[2 * PAIRS :]
    for i in range(PAIRS):
        rows = slice(i * 8, i * 8 + 8)
        fr8[rows, :] = jnp.broadcast_to(fr[i : i + 1, :], (8, 512))
    for i in range(CHUNKS):
        rows = slice(i * 8, i * 8 + 8)
        for j in range(2):
            lanes = slice(j * 128, j * 128 + 128)
            n = 2 * i + j
            an8[rows, lanes] = jnp.broadcast_to(idx_ref[n : n + 1, :] >> 8, (8, 128))
            ac8[rows, lanes] = jnp.broadcast_to(idx_ref[PAIRS + n : PAIRS + n + 1, :] >> 7, (8, 128))

    low = jnp.where(
        lax.broadcasted_iota(I32, (64, 128), 0) < PAIRS, idx_ref[...] & 255, idx_ref[...] & 127
    ).astype(F32)
    cols = jnp.transpose(jnp.concatenate([low, jnp.zeros((64, 128), F32)], axis=0))
    sub_n = lax.broadcasted_iota(I32, (256, 128), 0)
    sub_c = lax.broadcasted_iota(I32, (128, 128), 0)
    lane_n = lax.broadcasted_iota(I32, (128, 256), 1).astype(F32)
    lane_c = lax.broadcasted_iota(I32, (128, 128), 1).astype(F32)
    for i in range(PAIRS):
        span = slice(i * 128, i * 128 + 128)
        ohn[:, span] = one(sub_n == (idx_ref[i : i + 1, :] & 255))
        ohc[:, span] = one(sub_c == (idx_ref[PAIRS + i : PAIRS + i + 1, :] & 127))
        ohnt[span, :] = one(lane_n == cols[:, i : i + 1])
        ohct[span, :] = one(lane_c == cols[:, PAIRS + i : PAIRS + i + 1])

    for cpy in first:
        cpy.wait()
    load.wait()

    lane = lax.broadcasted_iota(I32, (8, 128), 1)
    upper = jnp.where(lane >= RIM, 1.0, 0.0).astype(F32)
    own = [upper, jnp.ones((8, 128), F32), 1.0 - upper]
    exist = [
        upper + (1.0 - upper) * has_prev,
        jnp.ones((8, 128), F32),
        (1.0 - upper) + upper * has_next,
    ]
    q = [
        qs_ref[0:8, 0:128] + qsp[0:8, :] * has_prev,
        qs_ref[0:8, 128:256],
        qs_ref[0:8, 256:384] + qsn[0:8, :] * has_next,
    ]
    same = [
        qs_ref[8:16, 0:128] + qsp[8:16, :] * has_prev,
        qs_ref[8:16, 128:256],
        qs_ref[8:16, 256:384] + qsn[8:16, :] * has_next,
    ]

    def square_start(i, cur):
        total = cur[0] * cur[0] * own[0] + cur[1] * cur[1] + cur[2] * cur[2] * own[2]
        pa[i, my_z] = total
        for d in range(1, ZS):
            rcopy(
                pa.at[i, my_z], pa.at[i, my_z], p_s.at[i, 0, d], p_r.at[i, 0, my_z],
                z_device(z_peer(d)),
            ).start()

    def square_mid(i):
        for d in range(1, ZS):
            z = z_peer(d)
            got = rcopy(pa.at[i, z], pa.at[i, z], p_s.at[i, 0, d], p_r.at[i, 0, z], z_device(z))
            got.wait_recv()
            got.wait_send()
        total = pa[i, 0]
        for z in range(1, ZS):
            total = total + pa[i, z]
        pb[i, my_yx] = total
        for d in range(1, YXS):
            rcopy(
                pb.at[i, my_yx], pb.at[i, my_yx], p_s.at[i, 1, d], p_r.at[i, 1, my_yx],
                yx_device(yx_peer(d)),
            ).start()

    def square_end(i):
        for d in range(1, YXS):
            yx = yx_peer(d)
            got = rcopy(
                pb.at[i, yx], pb.at[i, yx], p_s.at[i, 1, d], p_r.at[i, 1, yx], yx_device(yx)
            )
            got.wait_recv()
            got.wait_send()
        total = pb[i, 0]
        for yx in range(1, YXS):
            total = total + pb[i, yx]
        mean = jnp.sum(total, axis=1, keepdims=True) / (256 * tiles)
        return 1.0 / jnp.sqrt(mean + 1e-06)

    def weight(ref, n):
        c = n % 3
        return ref[c : c + 1, n // 3 * 256 : n // 3 * 256 + 256]

    row16 = lax.broadcasted_iota(I32, (16, DOF), 0) < 8

    def scatter_nodes(n, unroll, levels):
        spreads = []
        for j in range(unroll):
            m = n * unroll + j
            r0 = mo(m * 16, 16)
            parts = []
            for c in range(3):
                span = slice(c * 128, c * 128 + 128)
                parts.append(
                    jnp.concatenate([fc[pl.ds(r0, 8), span], fc[pl.ds(r0 + 8, 8), span]], axis=1)
                )
            a = an8[pl.ds(mo(m * 8, 8), 8), :]
            spread = jnp.concatenate(
                [jnp.where(a == lv, parts[c], 0.0) for lv in levels for c in range(3)], axis=0
            )
            spreads.append(spread.astype(BF16))
        size = unroll * 256
        return dot(jnp.concatenate(spreads, axis=1), ohnt[pl.ds(mo(n * size, size), size), :])

    def gather_nodes(m, table, levels, base):
        got = dot(table[...], ohn[:, pl.ds(mo(m * 256, 256), 256)])
        a = an8[pl.ds(mo(m * 8, 8), 8), :]
        out = list(base)
        for n, lv in enumerate(levels):
            hit = a == lv
            for c in range(3):
                row = (n * 3 + c) * 8
                out[c] = jnp.where(hit, got[row : row + 8], out[c])
        return out

    def hessian(h, q):
        parts = []
        for b in q:
            parts += list(split(b))
        cells = jnp.concatenate(parts, axis=0).astype(BF16)

        def gather_cells(m):
            got = dot(cells, ohc[:, pl.ds(mo(m * 256, 256), 256)])
            a = ac8[pl.ds(mo(m * 8, 8), 8), :]
            g = jnp.where(
                a == 0,
                got[0:8] + got[8:16],
                jnp.where(a == 1, got[16:24] + got[24:32], got[32:40] + got[40:48]),
            )
            hi, lo = split(g)
            rows = pl.ds(mo(m * 16, 16), 16)
            gh[rows, :] = jnp.concatenate([hi[:, :128], hi[:, 128:]], axis=0).astype(BF16)
            gl[rows, :] = jnp.concatenate([lo[:, :128], lo[:, 128:]], axis=0).astype(BF16)

        each(U_IN, gather_cells)

        for i in range(4):
            rows = slice(i * 64, i * 64 + 64)
            wide = dot(gh[rows, :], rep[...]) + dot(gl[rows, :], rep[...])
            xin[rows, :] = (wide * fr8[rows, :]).astype(BF16)

        def forward(m):
            rows = pl.ds(mo(m * 16, 16), 16)
            for half in range(2):
                span = slice(half * 256, half * 256 + DOF)
                x = xin[rows, span]
                o0 = dot(x, blk[2 * m + PAIRS * half], NT)
                o1 = dot(x, blk[2 * m + 1 + PAIRS * half], NT)
                fw[rows, span] = jnp.where(row16, o0, o1).astype(BF16)

        each(U_PROD, forward)

        for i in range(4):
            rows = slice(i * 64, i * 64 + 64)
            fc[rows, :] = dot(fw[rows, :], pmt[...])

        acce[...] = jnp.zeros(acce.shape, F32)
        acci[...] = jnp.zeros(acci.shape, F32)

        @pl.loop(0, CHUNKS // U_EDGE)
        def _(n):
            acce[...] += scatter_nodes(n, U_EDGE, EDGE)

        swap = [
            rcopy(acce.at[pl.ds(0, 48), :], renext.at[h], e_s.at[h, 0], e_r.at[h, 0], (prv, group)),
            rcopy(acce.at[pl.ds(48, 48), :], reprev.at[h], e_s.at[h, 1], e_r.at[h, 1], (nxt, group)),
        ]
        for cpy in swap:
            cpy.start()

        @pl.loop(0, CHUNKS // U_INNER)
        def _(n):
            acci[...] += scatter_nodes(n, U_INNER, INNER)

        if h > 0:
            square_mid(h - 1)

        for i in range(21):
            pair = []
            for j in range(2):
                n = 2 * i + j
                pair.append(acci[n * 8 : n * 8 + 8, :] * weight(w3, 6 + n))
            ti[i * 16 : i * 16 + 16, :] = jnp.concatenate(pair, axis=0).astype(BF16)

        def gather_inner(m):
            zero = jnp.zeros((8, 256), F32)
            out = gather_nodes(m, ti, INNER, [zero] * 3)
            r0 = mo(m * 16, 16)
            for c in range(3):
                span = slice(c * 128, c * 128 + 128)
                ad1[pl.ds(r0, 8), span] = out[c][:, :128]
                ad1[pl.ds(r0 + 8, 8), span] = out[c][:, 128:]

        each(U_GET, gather_inner)

        for cpy in swap:
            cpy.wait()
        for i in range(6):
            pair = []
            for j in range(2):
                n = 2 * i + j
                if n < 6:
                    total = acce[n * 8 : n * 8 + 8, :] + reprev[h, n * 8 : n * 8 + 8, :] * has_prev
                    pair.append(total * weight(w3, n))
                else:
                    o = (n - 6) * 8
                    total = acce[n * 8 : n * 8 + 8, :] + renext[h, o : o + 8, :]
                    pair.append(total * (weight(wn, n - 6) * has_next))
            te[i * 16 : i * 16 + 16, :] = jnp.concatenate(pair, axis=0).astype(BF16)

        def gather_edge(m):
            r0 = mo(m * 16, 16)
            base = []
            for c in range(3):
                span = slice(c * 128, c * 128 + 128)
                base.append(
                    jnp.concatenate([ad1[pl.ds(r0, 8), span], ad1[pl.ds(r0 + 8, 8), span]], axis=1)
                )
            out = gather_nodes(m, te, EDGE, base)
            for c in range(3):
                span = slice(c * 128, c * 128 + 128)
                ad[pl.ds(r0, 16), span] = jnp.concatenate(
                    [out[c][:, :128], out[c][:, 128:]], axis=0
                ).astype(BF16)

        each(U_GET, gather_edge)

        for i in range(4):
            rows = slice(i * 64, i * 64 + 64)
            ain[rows, :] = dot(ad[rows, :], pm[...]).astype(BF16)

        def adjoint(m):
            rows = pl.ds(mo(m * 16, 16), 16)
            for half in range(2):
                span = slice(half * 256, half * 256 + DOF)
                x = ain[rows, span]
                o0 = dot(x, blk[2 * m + PAIRS * half])
                o1 = dot(x, blk[2 * m + 1 + PAIRS * half])
                hi, lo = split(jnp.where(row16, o0, o1) * fr8[rows, span])
                yh[rows, span] = hi.astype(BF16)
                yl[rows, span] = lo.astype(BF16)

        each(U_PROD, adjoint)

        for i in range(4):
            rows = slice(i * 64, i * 64 + 64)
            pt[rows, :] = dot(yh[rows, :], sel[...]) + dot(yl[rows, :], sel[...])

        def scatter_cells(n, acc):
            spreads = []
            for j in range(U_PUT):
                m = n * U_PUT + j
                r0 = mo(m * 16, 16)
                v = jnp.concatenate([pt[pl.ds(r0, 8), :], pt[pl.ds(r0 + 8, 8), :]], axis=1)
                a = ac8[pl.ds(mo(m * 8, 8), 8), :]
                spread = jnp.concatenate(
                    [jnp.where(a == lv, s, 0.0) for lv in range(3) for s in split(v)], axis=0
                )
                spreads.append(spread.astype(BF16))
            size = U_PUT * 256
            return acc + dot(
                jnp.concatenate(spreads, axis=1), ohct[pl.ds(mo(n * size, size), size), :]
            )

        acc = lax.fori_loop(0, CHUNKS // U_PUT, scatter_cells, jnp.zeros((48, 128), F32))
        sums = [acc[n * 16 : n * 16 + 8] + acc[n * 16 + 8 : n * 16 + 16] for n in range(3)]
        bs[h, 0] = sums[0]
        bs[h, 1] = sums[2]
        swap = [
            rcopy(bs.at[h, 0], rbn.at[h], b_s.at[h, 0], b_r.at[h, 0], (prv, group)),
            rcopy(bs.at[h, 1], rbp.at[h], b_s.at[h, 1], b_r.at[h, 1], (nxt, group)),
        ]
        for cpy in swap:
            cpy.start()
        scale = square_end(h - 1) if h > 0 else None
        for cpy in swap:
            cpy.wait()
        sums[0] = sums[0] + rbp[h] * has_prev
        sums[2] = sums[2] + rbn[h] * has_next
        keep = same if h % 2 == 1 else [exist[n] - same[n] for n in range(3)]
        out = []
        for n in range(3):
            v = sums[n] * keep[n]
            out.append(v if scale is None else v * scale)
        return out

    for h in range(ROUNDS):
        q = hessian(h, q)
        if h < POWER:
            square_start(h, q)
        if h == 0:
            for n in range(3):
                samp_ref[:, n * 128 : n * 128 + 128] = q[n]
    for n in range(3):
        refd_ref[:, n * 128 : n * 128 + 128] = q[n]

    mine = pltpu.roll(refd_ref[...], 384 - RIM, 1)[:, :256]
    cp[group] = mine
    for d in range(1, GROUPS):
        rcopy(
            cp.at[group], cp.at[group], g_s.at[d], g_r.at[group], (tile, lax.rem(group + d, GROUPS))
        ).start()
    for d in range(1, GROUPS):
        g = lax.rem(group + d, GROUPS)
        got = rcopy(cp.at[g], cp.at[g], g_s.at[d], g_r.at[g], (tile, g))
        got.wait_recv()
        got.wait_send()
    every = jnp.concatenate([cp[g] for g in range(GROUPS)], axis=0)
    outer = jnp.concatenate([every * mine[i : i + 1, :] for i in range(8)], axis=0)
    hi, lo = split(outer)
    member = one(lax.broadcasted_iota(I32, (64, 256), 0) == cl_ref[...])
    gk[...] = dot(member, hi.astype(BF16), NT) + dot(member, lo.astype(BF16), NT)

    ka[my_yx] = gk[pl.ds(mo(my_yx * 8, 8), 8), :]
    for d in range(1, YXS):
        yx = yx_peer(d)
        rcopy(
            gk.at[pl.ds(mo(yx * 8, 8), 8), :], ka.at[my_yx], k_s.at[0, d], k_r.at[0, my_yx],
            yx_device(yx),
        ).start()
    for d in range(1, YXS):
        yx = yx_peer(d)
        got = rcopy(ka.at[yx], ka.at[yx], k_s.at[0, d], k_r.at[0, yx], yx_device(yx))
        got.wait_recv()
        got.wait_send()
    total = ka[0]
    for yx in range(1, YXS):
        total = total + ka[yx]
    kb[my_z] = total
    for d in range(1, ZS):
        rcopy(
            kb.at[my_z], kb.at[my_z], k_s.at[1, d], k_r.at[1, my_z], z_device(z_peer(d))
        ).start()
    for d in range(1, ZS):
        z = z_peer(d)
        got = rcopy(kb.at[z], kb.at[z], k_s.at[1, d], k_r.at[1, z], z_device(z))
        got.wait_recv()
        got.wait_send()
    total = kb[0]
    for z in range(1, ZS):
        total = total + kb[z]
    kc[my_yx] = total
    for d in range(1, YXS):
        rcopy(
            kc.at[my_yx], kc.at[my_yx], k_s.at[2, d], k_r.at[2, my_yx], yx_device(yx_peer(d))
        ).start()
    for d in range(1, YXS):
        yx = yx_peer(d)
        got = rcopy(kc.at[yx], kc.at[yx], k_s.at[2, d], k_r.at[2, yx], yx_device(yx))
        got.wait_recv()
        got.wait_send()
    for yx in range(YXS):
        gram_ref[yx * 8 : yx * 8 + 8, :] = kc[yx]


def shards(
    blocks, connectivity, basal_map, friction, elem_counts, obs_weight, sign_bits, cluster_ids
):
    vmem = pl.BlockSpec(memory_space=pltpu.VMEM)
    here = pl.BlockSpec(memory_space=pl.ANY)
    dma = pltpu.SemaphoreType.DMA
    samp, refd, gram = pl.pallas_call(
        kernel,
        out_shape=(
            jax.ShapeDtypeStruct((8, 384), F32),
            jax.ShapeDtypeStruct((8, 384), F32),
            jax.ShapeDtypeStruct((64, 256), F32),
        ),
        in_specs=[here] * 4 + [pl.BlockSpec(memory_space=pltpu.SMEM)] + [here] * 3,
        out_specs=(vmem, vmem, vmem),
        scratch_shapes=[
            pltpu.VMEM((ELEMS, 64), I32),
            pltpu.VMEM((ELEMS, 64), I32),
            pltpu.VMEM((3, ELEMS, 64), F32),
            pltpu.VMEM((3, 4096), F32),
            pltpu.VMEM((8, 256), I32),
            pltpu.VMEM((1, 256), I32),
            pltpu.VMEM((ELEMS, 128), I32),
            pltpu.VMEM((16, 384), F32),
            pltpu.VMEM((ELEMS, DOF, DOF), BF16),
            pltpu.VMEM((256, 4096), BF16),
            pltpu.VMEM((4096, 256), BF16),
            pltpu.VMEM((128, 4096), BF16),
            pltpu.VMEM((4096, 128), BF16),
            pltpu.VMEM((128, 256), I32),
            pltpu.VMEM((128, 256), I32),
            pltpu.VMEM((256, 512), F32),
            pltpu.VMEM((128, 512), BF16),
            pltpu.VMEM((512, 128), BF16),
            pltpu.VMEM((384, 512), BF16),
            pltpu.VMEM((512, 384), BF16),
            pltpu.VMEM((256, 128), BF16),
            pltpu.VMEM((256, 128), BF16),
            pltpu.VMEM((256, 512), BF16),
            pltpu.VMEM((256, 512), BF16),
            pltpu.VMEM((256, 384), F32),
            pltpu.VMEM((96, 256), F32),
            pltpu.VMEM((336, 256), F32),
            pltpu.VMEM((96, 256), BF16),
            pltpu.VMEM((336, 256), BF16),
            pltpu.VMEM((256, 384), F32),
            pltpu.VMEM((256, 384), BF16),
            pltpu.VMEM((256, 512), BF16),
            pltpu.VMEM((256, 512), BF16),
            pltpu.VMEM((256, 512), BF16),
            pltpu.VMEM((256, 128), F32),
            pltpu.VMEM((3, 512), F32),
            pltpu.VMEM((16, 128), F32),
            pltpu.VMEM((16, 128), F32),
            pltpu.VMEM((ROUNDS, 48, 256), F32),
            pltpu.VMEM((ROUNDS, 48, 256), F32),
            pltpu.VMEM((ROUNDS, 2, 8, 128), F32),
            pltpu.VMEM((ROUNDS, 8, 128), F32),
            pltpu.VMEM((ROUNDS, 8, 128), F32),
            pltpu.VMEM((POWER, ZS, 8, 128), F32),
            pltpu.VMEM((POWER, YXS, 8, 128), F32),
            pltpu.VMEM((GROUPS, 8, 256), F32),
            pltpu.VMEM((64, 256), F32),
            pltpu.VMEM((ZS, 8, 256), F32),
            pltpu.VMEM((YXS, 8, 256), F32),
            pltpu.VMEM((ZS, 8, 256), F32),
            dma,
            dma((6,)),
            dma((3,)),
            dma((3,)),
            dma((ROUNDS, 2)),
            dma((ROUNDS, 2)),
            dma((ROUNDS, 2)),
            dma((ROUNDS, 2)),
            dma((POWER, 2, 8)),
            dma((POWER, 2, 8)),
            dma((GROUPS,)),
            dma((GROUPS,)),
            dma((3, 8)),
            dma((3, 8)),
        ],
        compiler_params=pltpu.CompilerParams(
            collective_id=0, has_side_effects=True, vmem_limit_bytes=63 * 1024 * 1024
        ),
    )(
        blocks, connectivity, basal_map, friction.transpose(2, 0, 1), elem_counts,
        obs_weight.T, sign_bits.T, cluster_ids[None, :],
    )
    samples = samp[:, RIM : RIM + 256].T
    refined = refd[:, RIM : RIM + 256].T
    return samples, refined, gram.reshape(64, 8, 32)


def solution(mesh):
    in_specs = (
        P("tiles", None, None),
        P("tiles", None),
        P("tiles", None),
        P("tiles", None, None),
        P("tiles"),
        P("tiles", None),
        P("tiles", "probes"),
        P("tiles"),
    )
    out_specs = (P("tiles", "probes"), P("tiles", "probes"), P(None, "probes", None))
    return jax.shard_map(shards, mesh=mesh, in_specs=in_specs, out_specs=out_specs, check_vma=False)
```

```python
import functools

import jax
import jax.numpy as jnp
from jax import lax
from jax.experimental import pallas as pl
from jax.experimental.pallas import tpu as pltpu
from jax.sharding import PartitionSpec as P

F32 = jnp.float32
BF16 = jnp.bfloat16
I32 = jnp.int32
POWER = 2
ROUNDS = POWER + 1
RIM = 64
ELEMS = 64
DOF = 192
PAIRS = 32
CHUNKS = 16
U_IN = 16
U_PROD = 16
U_EDGE = 16
U_INNER = 16
U_GET = 8
U_PUT = 16
ZS = 8
YXS = 8
GROUPS = 4
EDGE = (0, 1, 16, 17)
INNER = tuple(range(2, 16))
NT = (((1,), (1,)), ((), ()))
NN = (((1,), (0,)), ((), ()))
MESH = pl.DeviceIdType.MESH


def mo(x, n):
    return pl.multiple_of(x, n)


def each(unroll, body, steps=CHUNKS):
    @pl.loop(0, steps // unroll)
    def _(n):
        for j in range(unroll):
            body(n * unroll + j)


def split(x):
    hi = x.astype(BF16).astype(F32)
    return hi, x - hi


def dot(a, b, dims=NN):
    return lax.dot_general(a, b, dims, preferred_element_type=F32)


def kernel(
    blk_hbm, conn_hbm, cell_hbm, fr_hbm, count_ref, w_hbm, sign_hbm, cl_hbm,
    samp_ref, refd_ref, gram_ref,
    conn, cell, fr3, w3, sign, cl_ref, idx_ref, qs_ref,
    blk, ohn, ohc, an8, ac8, fr8, rep, sel, pm, pmt,
    gh, gl, xin, fw, fc, acce, acci, te, ti, ad1, ad, ain, yh, yl, pt,
    wn, qsp, qsn, esend, renext, reprev, bs, rbn, rbp, pa, pb, fp, fpn, fpp, gk, ka, kb, kc,
    blk_sem, in_sem, i_s, i_r, e_s, e_r, b_s, b_r, p_s, p_r, g_s, g_r, k_s, k_r,
):
    tile = lax.axis_index("tiles")
    group = lax.axis_index("probes")
    tiles = lax.axis_size("tiles")
    nxt = lax.rem(tile + 1, tiles)
    prv = lax.rem(tile + tiles - 1, tiles)
    my_z = lax.rem(tile, ZS)
    my_yx = lax.div(tile, ZS)
    has_prev = jnp.where(tile > 0, 1.0, 0.0).astype(F32)
    has_next = jnp.where(tile < tiles - 1, 1.0, 0.0).astype(F32)

    def z_peer(d):
        return lax.rem(my_z + d, ZS)

    def yx_peer(d):
        return lax.rem(my_yx + d, YXS)

    def z_device(z):
        return (my_yx * ZS + z, group)

    def yx_device(yx):
        return (yx * ZS + my_z, group)

    def rcopy(src, dst, ss, rs, dev):
        return pltpu.make_async_remote_copy(
            src_ref=src, dst_ref=dst, send_sem=ss, recv_sem=rs, device_id=dev, device_id_type=MESH
        )

    small = [
        pltpu.make_async_copy(src, dst, in_sem.at[n])
        for n, (src, dst) in enumerate(
            [(sign_hbm, sign), (cl_hbm, cl_ref), (w_hbm, w3), (conn_hbm, conn), (cell_hbm, cell), (fr_hbm, fr3)]
        )
    ]
    for cpy in small:
        cpy.start()
    load = pltpu.make_async_copy(blk_hbm, blk, blk_sem)
    load.start()

    barrier = pltpu.get_barrier_semaphore()

    def greet(dev):
        pl.semaphore_signal(barrier, inc=1, device_id=dev, device_id_type=MESH)

    greet((nxt, group))
    greet((prv, group))
    for d in range(1, ZS):
        greet(z_device(z_peer(d)))
    for d in range(1, YXS):
        greet(yx_device(yx_peer(d)))
    for d in range(1, GROUPS):
        other = lax.rem(group + d, GROUPS)
        greet((tile, other))
        greet((nxt, other))
        greet((prv, other))

    def one(cond):
        return jnp.where(cond, 1.0, 0.0).astype(BF16)

    def pair_col(lane):
        half = lane >> 8
        j = lane & 255
        k = (j * 171) >> 9
        return half, k, j - 3 * k, j < DOF

    r = lax.broadcasted_iota(I32, (128, 512), 0)
    half, k, c, ok = pair_col(lax.broadcasted_iota(I32, (128, 512), 1))
    rep[...] = one((r == half * 64 + k) & ok)
    half, k, c, ok = pair_col(lax.broadcasted_iota(I32, (512, 128), 0))
    r = lax.broadcasted_iota(I32, (512, 128), 1)
    sel[...] = one((r == half * 64 + k) & ok)
    r = lax.broadcasted_iota(I32, (384, 512), 0)
    half, k, c, ok = pair_col(lax.broadcasted_iota(I32, (384, 512), 1))
    pm[...] = one((r == c * 128 + half * 64 + k) & ok)
    half, k, c, ok = pair_col(lax.broadcasted_iota(I32, (512, 384), 0))
    r = lax.broadcasted_iota(I32, (512, 384), 1)
    pmt[...] = one((r == c * 128 + half * 64 + k) & ok)

    fw[...] = jnp.zeros(fw.shape, BF16)
    yh[...] = jnp.zeros(yh.shape, BF16)
    yl[...] = jnp.zeros(yl.shape, BF16)

    for cpy in small:
        cpy.wait()

    same_own = (cl_ref[...] & 1) == (lax.broadcasted_iota(I32, (8, 256), 0) & 1)
    start = jnp.where(same_own, (2 * sign[...] - 1).astype(F32), 0.0)
    both = jnp.concatenate([start, jnp.where(same_own, 1.0, 0.0).astype(F32)], axis=0)
    qs_ref[...] = pltpu.roll(
        jnp.concatenate([both, jnp.zeros((16, 128), F32)], axis=1), RIM, 1
    )
    first = [
        rcopy(qs_ref.at[:, pl.ds(256, 128)], qsp, i_s.at[0], i_r.at[0], (nxt, group)),
        rcopy(qs_ref.at[:, pl.ds(0, 128)], qsn, i_s.at[1], i_r.at[1], (prv, group)),
        rcopy(w3.at[:, pl.ds(0, 512)], wn, i_s.at[2], i_r.at[2], (prv, group)),
    ]
    pl.semaphore_wait(barrier, 2 + ZS - 1 + YXS - 1 + 3 * (GROUPS - 1))
    for cpy in first:
        cpy.start()

    idx_ref[0:PAIRS, :] = jnp.concatenate([conn[0:PAIRS, :], conn[PAIRS:ELEMS, :]], axis=1)
    idx_ref[PAIRS:ELEMS, :] = jnp.concatenate([cell[0:PAIRS, :], cell[PAIRS:ELEMS, :]], axis=1)
    element = lax.broadcasted_iota(I32, (PAIRS, 128), 0) + jnp.where(
        lax.broadcasted_iota(I32, (PAIRS, 128), 1) < 64, 0, PAIRS
    )
    live = element < count_ref[0]
    wide = []
    for c in range(3):
        f = jnp.concatenate([fr3[c, 0:PAIRS, :], fr3[c, PAIRS:ELEMS, :]], axis=1)
        wide.append(jnp.where(live, f, 0.0))
    wide = jnp.concatenate(wide, axis=1)
    hi, rest = split(wide)
    mid, lo = split(rest)
    third = dot(jnp.concatenate([hi, mid, lo], axis=0).astype(BF16), pm[...])
    fr = third[0:PAIRS] + third[PAIRS : 2 * PAIRS] + third[2 * PAIRS :]
    for i in range(PAIRS):
        rows = slice(i * 8, i * 8 + 8)
        fr8[rows, :] = jnp.broadcast_to(fr[i : i + 1, :], (8, 512))
    for i in range(CHUNKS):
        rows = slice(i * 8, i * 8 + 8)
        for j in range(2):
            lanes = slice(j * 128, j * 128 + 128)
            n = 2 * i + j
            an8[rows, lanes] = jnp.broadcast_to(idx_ref[n : n + 1, :] >> 8, (8, 128))
            ac8[rows, lanes] = jnp.broadcast_to(idx_ref[PAIRS + n : PAIRS + n + 1, :] >> 7, (8, 128))

    sub_n = lax.broadcasted_iota(I32, (256, 128), 0)
    sub_c = lax.broadcasted_iota(I32, (128, 128), 0)
    for i in range(PAIRS):
        span = slice(i * 128, i * 128 + 128)
        ohn[:, span] = one(sub_n == (idx_ref[i : i + 1, :] & 255))
        ohc[:, span] = one(sub_c == (idx_ref[PAIRS + i : PAIRS + i + 1, :] & 127))

    for cpy in first:
        cpy.wait()
    load.wait()

    lane = lax.broadcasted_iota(I32, (8, 128), 1)
    upper = jnp.where(lane >= RIM, 1.0, 0.0).astype(F32)
    own = [upper, jnp.ones((8, 128), F32), 1.0 - upper]
    exist = [
        upper + (1.0 - upper) * has_prev,
        jnp.ones((8, 128), F32),
        (1.0 - upper) + upper * has_next,
    ]
    q = [
        qs_ref[0:8, 0:128] + qsp[0:8, :] * has_prev,
        qs_ref[0:8, 128:256],
        qs_ref[0:8, 256:384] + qsn[0:8, :] * has_next,
    ]
    same = [
        qs_ref[8:16, 0:128] + qsp[8:16, :] * has_prev,
        qs_ref[8:16, 128:256],
        qs_ref[8:16, 256:384] + qsn[8:16, :] * has_next,
    ]

    def square_start(i, cur):
        total = cur[0] * cur[0] * own[0] + cur[1] * cur[1] + cur[2] * cur[2] * own[2]
        pa[i, my_z] = total
        for d in range(1, ZS):
            rcopy(
                pa.at[i, my_z], pa.at[i, my_z], p_s.at[i, 0, d], p_r.at[i, 0, my_z],
                z_device(z_peer(d)),
            ).start()

    def square_mid(i):
        for d in range(1, ZS):
            z = z_peer(d)
            got = rcopy(pa.at[i, z], pa.at[i, z], p_s.at[i, 0, d], p_r.at[i, 0, z], z_device(z))
            got.wait_recv()
            got.wait_send()
        total = pa[i, 0]
        for z in range(1, ZS):
            total = total + pa[i, z]
        pb[i, my_yx] = total
        for d in range(1, YXS):
            rcopy(
                pb.at[i, my_yx], pb.at[i, my_yx], p_s.at[i, 1, d], p_r.at[i, 1, my_yx],
                yx_device(yx_peer(d)),
            ).start()

    def square_end(i):
        for d in range(1, YXS):
            yx = yx_peer(d)
            got = rcopy(
                pb.at[i, yx], pb.at[i, yx], p_s.at[i, 1, d], p_r.at[i, 1, yx], yx_device(yx)
            )
            got.wait_recv()
            got.wait_send()
        total = pb[i, 0]
        for yx in range(1, YXS):
            total = total + pb[i, yx]
        mean = jnp.sum(total, axis=1, keepdims=True) / (256 * tiles)
        return 1.0 / jnp.sqrt(mean + 1e-06)

    def weight(ref, n):
        c = n % 3
        return ref[c : c + 1, n // 3 * 256 : n // 3 * 256 + 256]

    row16 = lax.broadcasted_iota(I32, (16, DOF), 0) < 8

    def scatter_nodes(n, unroll, levels):
        spreads = []
        for j in range(unroll):
            m = n * unroll + j
            r0 = mo(m * 16, 16)
            parts = []
            for c in range(3):
                span = slice(c * 128, c * 128 + 128)
                parts.append(
                    jnp.concatenate([fc[pl.ds(r0, 8), span], fc[pl.ds(r0 + 8, 8), span]], axis=1)
                )
            a = an8[pl.ds(mo(m * 8, 8), 8), :]
            spread = jnp.concatenate(
                [jnp.where(a == lv, parts[c], 0.0) for lv in levels for c in range(3)], axis=0
            )
            spreads.append(spread.astype(BF16))
        size = unroll * 256
        return dot(jnp.concatenate(spreads, axis=1), ohn[:, pl.ds(mo(n * size, size), size)], NT)

    def gather_nodes(m, table, levels, base):
        got = dot(table[...], ohn[:, pl.ds(mo(m * 512, 512), 512)])
        r = mo(m * 16, 16)
        a = jnp.concatenate([an8[pl.ds(r, 8), :], an8[pl.ds(r + 8, 8), :]], axis=1)
        out = list(base)
        for n, lv in enumerate(levels):
            hit = a == lv
            for c in range(3):
                row = (n * 3 + c) * 8
                out[c] = jnp.where(hit, got[row : row + 8], out[c])
        return out

    def hessian(h, q):
        parts = []
        for b in q:
            parts += list(split(b))
        cells = jnp.concatenate(parts, axis=0).astype(BF16)

        def gather_cells(m):
            got = dot(cells, ohc[:, pl.ds(mo(m * 256, 256), 256)])
            a = ac8[pl.ds(mo(m * 8, 8), 8), :]
            g = jnp.where(
                a == 0,
                got[0:8] + got[8:16],
                jnp.where(a == 1, got[16:24] + got[24:32], got[32:40] + got[40:48]),
            )
            hi, lo = split(g)
            rows = pl.ds(mo(m * 16, 16), 16)
            gh[rows, :] = jnp.concatenate([hi[:, :128], hi[:, 128:]], axis=0).astype(BF16)
            gl[rows, :] = jnp.concatenate([lo[:, :128], lo[:, 128:]], axis=0).astype(BF16)

        each(U_IN, gather_cells)

        for i in range(4):
            rows = slice(i * 64, i * 64 + 64)
            wide = dot(gh[rows, :], rep[...]) + dot(gl[rows, :], rep[...])
            xin[rows, :] = (wide * fr8[rows, :]).astype(BF16)

        def forward(m):
            rows = pl.ds(mo(m * 16, 16), 16)
            for half in range(2):
                span = slice(half * 256, half * 256 + DOF)
                x = xin[rows, span]
                o0 = dot(x, blk[2 * m + PAIRS * half], NT)
                o1 = dot(x, blk[2 * m + 1 + PAIRS * half], NT)
                fw[rows, span] = jnp.where(row16, o0, o1).astype(BF16)

        each(U_PROD, forward)

        for i in range(4):
            rows = slice(i * 64, i * 64 + 64)
            fc[rows, :] = dot(fw[rows, :], pmt[...])

        acce[...] = jnp.zeros(acce.shape, F32)
        acci[...] = jnp.zeros(acci.shape, F32)

        @pl.loop(0, CHUNKS // U_EDGE)
        def _(n):
            acce[...] += scatter_nodes(n, U_EDGE, EDGE)

        esend[h] = acce[...].astype(BF16)
        swap = [
            rcopy(esend.at[h, pl.ds(0, 48), :], renext.at[h], e_s.at[h, 0], e_r.at[h, 0], (prv, group)),
            rcopy(esend.at[h, pl.ds(48, 48), :], reprev.at[h], e_s.at[h, 1], e_r.at[h, 1], (nxt, group)),
        ]
        for cpy in swap:
            cpy.start()

        @pl.loop(0, CHUNKS // U_INNER)
        def _(n):
            acci[...] += scatter_nodes(n, U_INNER, INNER)

        if h > 0:
            square_mid(h - 1)

        for i in range(21):
            pair = []
            for j in range(2):
                n = 2 * i + j
                pair.append(acci[n * 8 : n * 8 + 8, :] * weight(w3, 6 + n))
            ti[i * 16 : i * 16 + 16, :] = jnp.concatenate(pair, axis=0).astype(BF16)

        def gather_inner(m):
            zero = jnp.zeros((8, 512), F32)
            out = gather_nodes(m, ti, INNER, [zero] * 3)
            r0 = mo(m * 32, 32)
            for c in range(3):
                span = slice(c * 128, c * 128 + 128)
                for j in range(4):
                    ad1[pl.ds(r0 + 8 * j, 8), span] = out[c][:, j * 128 : j * 128 + 128]

        each(U_GET, gather_inner, CHUNKS // 2)

        for cpy in swap:
            cpy.wait()
        for i in range(6):
            if i < 3:
                theirs = reprev[h, i * 16 : i * 16 + 16, :].astype(F32) * has_prev
            else:
                theirs = renext[h, i * 16 - 48 : i * 16 - 32, :].astype(F32)
            total = acce[i * 16 : i * 16 + 16, :] + theirs
            pair = []
            for j in range(2):
                n = 2 * i + j
                scale = weight(w3, n) if n < 6 else weight(wn, n - 6) * has_next
                pair.append(total[j * 8 : j * 8 + 8] * scale)
            te[i * 16 : i * 16 + 16, :] = jnp.concatenate(pair, axis=0).astype(BF16)

        def gather_edge(m):
            r0 = mo(m * 32, 32)
            base = []
            for c in range(3):
                span = slice(c * 128, c * 128 + 128)
                base.append(
                    jnp.concatenate([ad1[pl.ds(r0 + 8 * j, 8), span] for j in range(4)], axis=1)
                )
            out = gather_nodes(m, te, EDGE, base)
            for c in range(3):
                span = slice(c * 128, c * 128 + 128)
                ad[pl.ds(r0, 32), span] = jnp.concatenate(
                    [out[c][:, j * 128 : j * 128 + 128] for j in range(4)], axis=0
                ).astype(BF16)

        each(U_GET, gather_edge, CHUNKS // 2)

        for i in range(4):
            rows = slice(i * 64, i * 64 + 64)
            ain[rows, :] = dot(ad[rows, :], pm[...]).astype(BF16)

        def adjoint(m):
            rows = pl.ds(mo(m * 16, 16), 16)
            for half in range(2):
                span = slice(half * 256, half * 256 + DOF)
                x = ain[rows, span]
                o0 = dot(x, blk[2 * m + PAIRS * half])
                o1 = dot(x, blk[2 * m + 1 + PAIRS * half])
                hi, lo = split(jnp.where(row16, o0, o1) * fr8[rows, span])
                yh[rows, span] = hi.astype(BF16)
                yl[rows, span] = lo.astype(BF16)

        each(U_PROD, adjoint)

        for i in range(4):
            rows = slice(i * 64, i * 64 + 64)
            pt[rows, :] = dot(yh[rows, :], sel[...]) + dot(yl[rows, :], sel[...])

        def scatter_cells(n, acc):
            spreads = []
            for j in range(U_PUT):
                m = n * U_PUT + j
                r0 = mo(m * 16, 16)
                v = jnp.concatenate([pt[pl.ds(r0, 8), :], pt[pl.ds(r0 + 8, 8), :]], axis=1)
                a = ac8[pl.ds(mo(m * 8, 8), 8), :]
                spread = jnp.concatenate(
                    [jnp.where(a == lv, s, 0.0) for lv in range(3) for s in split(v)], axis=0
                )
                spreads.append(spread.astype(BF16))
            size = U_PUT * 256
            return acc + dot(
                jnp.concatenate(spreads, axis=1), ohc[:, pl.ds(mo(n * size, size), size)], NT
            )

        acc = lax.fori_loop(0, CHUNKS // U_PUT, scatter_cells, jnp.zeros((48, 128), F32))
        sums = [acc[n * 16 : n * 16 + 8] + acc[n * 16 + 8 : n * 16 + 16] for n in range(3)]
        keep = same if h % 2 == 1 else [exist[n] - same[n] for n in range(3)]
        if h == POWER:
            scale = square_end(h - 1)
            for n in range(3):
                fp[group, :, n * 128 : n * 128 + 128] = sums[n] * keep[n] * scale
            return None
        bs[h, 0] = sums[0]
        bs[h, 1] = sums[2]
        swap = [
            rcopy(bs.at[h, 0], rbn.at[h], b_s.at[h, 0], b_r.at[h, 0], (prv, group)),
            rcopy(bs.at[h, 1], rbp.at[h], b_s.at[h, 1], b_r.at[h, 1], (nxt, group)),
        ]
        for cpy in swap:
            cpy.start()
        scale = square_end(h - 1) if h > 0 else None
        for cpy in swap:
            cpy.wait()
        sums[0] = sums[0] + rbp[h] * has_prev
        sums[2] = sums[2] + rbn[h] * has_next
        out = []
        for n in range(3):
            v = sums[n] * keep[n]
            out.append(v if scale is None else v * scale)
        return out

    for h in range(ROUNDS):
        q = hessian(h, q)
        if h < POWER:
            square_start(h, q)
        if h == 0:
            for n in range(3):
                samp_ref[:, n * 128 : n * 128 + 128] = q[n]
    def final(kind, d, source):
        other = lax.rem(group + d, GROUPS)
        device, landing, span = (
            ((prv, other), fpn, pl.ds(0, 128)),
            ((nxt, other), fpp, pl.ds(256, 128)),
            ((tile, other), fp, pl.ds(0, 384)),
        )[kind]
        return rcopy(
            fp.at[group, :, span], landing.at[source], g_s.at[kind, d], g_r.at[kind, source], device
        )

    order = [(kind, d) for d in range(GROUPS) for kind in range(3) if kind < 2 or d > 0]
    for kind, d in order:
        final(kind, d, group).start()
    for kind, d in order:
        final(kind, d, lax.rem(group + d, GROUPS)).wait_recv()
    for kind, d in order:
        final(kind, d, group).wait_send()

    def window(g):
        return jnp.concatenate(
            [
                fp[g, :, 0:128] + fpp[g] * has_prev,
                fp[g, :, 128:256],
                fp[g, :, 256:384] + fpn[g] * has_next,
            ],
            axis=1,
        )

    refd_ref[...] = window(group)
    mine = pltpu.roll(refd_ref[...], 384 - RIM, 1)[:, :256]
    every = jnp.concatenate([window(g) for g in range(GROUPS)], axis=0)
    every = pltpu.roll(every, 384 - RIM, 1)[:, :256]
    outer = jnp.concatenate([every * mine[i : i + 1, :] for i in range(8)], axis=0)
    hi, lo = split(outer)
    member = one(lax.broadcasted_iota(I32, (64, 256), 0) == cl_ref[...])
    grams = dot(member, hi.astype(BF16), NT) + dot(member, lo.astype(BF16), NT)
    for yx in range(YXS):
        rows = grams[yx * 8 : yx * 8 + 8]
        gk[yx] = jnp.concatenate([rows[:, :128], rows[:, 128:]], axis=0).astype(BF16)

    for d in range(1, YXS):
        yx = yx_peer(d)
        rcopy(
            gk.at[yx], ka.at[my_yx], k_s.at[0, d], k_r.at[0, my_yx],
            yx_device(yx),
        ).start()
    for d in range(1, YXS):
        yx = yx_peer(d)
        got = rcopy(ka.at[yx], ka.at[yx], k_s.at[0, d], k_r.at[0, yx], yx_device(yx))
        got.wait_recv()
        got.wait_send()
    ka[my_yx] = gk[my_yx]
    total = ka[0].astype(F32)
    for yx in range(1, YXS):
        total = total + ka[yx].astype(F32)
    kb[my_z] = total.astype(BF16)
    for d in range(1, ZS):
        rcopy(
            kb.at[my_z], kb.at[my_z], k_s.at[1, d], k_r.at[1, my_z], z_device(z_peer(d))
        ).start()
    for d in range(1, ZS):
        z = z_peer(d)
        got = rcopy(kb.at[z], kb.at[z], k_s.at[1, d], k_r.at[1, z], z_device(z))
        got.wait_recv()
        got.wait_send()
    total = kb[0].astype(F32)
    for z in range(1, ZS):
        total = total + kb[z].astype(F32)
    kc[my_yx] = total
    for d in range(1, YXS):
        rcopy(
            kc.at[my_yx], kc.at[my_yx], k_s.at[2, d], k_r.at[2, my_yx], yx_device(yx_peer(d))
        ).start()
    for d in range(1, YXS):
        yx = yx_peer(d)
        got = rcopy(kc.at[yx], kc.at[yx], k_s.at[2, d], k_r.at[2, yx], yx_device(yx))
        got.wait_recv()
        got.wait_send()
    for yx in range(YXS):
        gram_ref[yx * 8 : yx * 8 + 8, 0:128] = kc[yx, 0:8]
        gram_ref[yx * 8 : yx * 8 + 8, 128:256] = kc[yx, 8:16]


def shards(
    blocks, connectivity, basal_map, friction, elem_counts, obs_weight, sign_bits, cluster_ids
):
    vmem = pl.BlockSpec(memory_space=pltpu.VMEM)
    here = pl.BlockSpec(memory_space=pltpu.HBM)
    dma = pltpu.SemaphoreType.DMA
    samp, refd, gram = pl.pallas_call(
        kernel,
        out_shape=(
            jax.ShapeDtypeStruct((8, 384), F32),
            jax.ShapeDtypeStruct((8, 384), F32),
            jax.ShapeDtypeStruct((64, 256), F32),
        ),
        in_specs=[here] * 4 + [pl.BlockSpec(memory_space=pltpu.SMEM)] + [here] * 3,
        out_specs=(vmem, vmem, vmem),
        scratch_shapes=[
            pltpu.VMEM((ELEMS, 64), I32),
            pltpu.VMEM((ELEMS, 64), I32),
            pltpu.VMEM((3, ELEMS, 64), F32),
            pltpu.VMEM((3, 4096), F32),
            pltpu.VMEM((8, 256), I32),
            pltpu.VMEM((1, 256), I32),
            pltpu.VMEM((ELEMS, 128), I32),
            pltpu.VMEM((16, 384), F32),
            pltpu.VMEM((ELEMS, DOF, DOF), BF16),
            pltpu.VMEM((256, 4096), BF16),
            pltpu.VMEM((128, 4096), BF16),
            pltpu.VMEM((128, 256), I32),
            pltpu.VMEM((128, 256), I32),
            pltpu.VMEM((256, 512), F32),
            pltpu.VMEM((128, 512), BF16),
            pltpu.VMEM((512, 128), BF16),
            pltpu.VMEM((384, 512), BF16),
            pltpu.VMEM((512, 384), BF16),
            pltpu.VMEM((256, 128), BF16),
            pltpu.VMEM((256, 128), BF16),
            pltpu.VMEM((256, 512), BF16),
            pltpu.VMEM((256, 512), BF16),
            pltpu.VMEM((256, 384), F32),
            pltpu.VMEM((96, 256), F32),
            pltpu.VMEM((336, 256), F32),
            pltpu.VMEM((96, 256), BF16),
            pltpu.VMEM((336, 256), BF16),
            pltpu.VMEM((256, 384), F32),
            pltpu.VMEM((256, 384), BF16),
            pltpu.VMEM((256, 512), BF16),
            pltpu.VMEM((256, 512), BF16),
            pltpu.VMEM((256, 512), BF16),
            pltpu.VMEM((256, 128), F32),
            pltpu.VMEM((3, 512), F32),
            pltpu.VMEM((16, 128), F32),
            pltpu.VMEM((16, 128), F32),
            pltpu.VMEM((ROUNDS, 96, 256), BF16),
            pltpu.VMEM((ROUNDS, 48, 256), BF16),
            pltpu.VMEM((ROUNDS, 48, 256), BF16),
            pltpu.VMEM((ROUNDS, 2, 8, 128), F32),
            pltpu.VMEM((ROUNDS, 8, 128), F32),
            pltpu.VMEM((ROUNDS, 8, 128), F32),
            pltpu.VMEM((POWER, ZS, 8, 128), F32),
            pltpu.VMEM((POWER, YXS, 8, 128), F32),
            pltpu.VMEM((GROUPS, 8, 384), F32),
            pltpu.VMEM((GROUPS, 8, 128), F32),
            pltpu.VMEM((GROUPS, 8, 128), F32),
            pltpu.VMEM((YXS, 16, 128), BF16),
            pltpu.VMEM((YXS, 16, 128), BF16),
            pltpu.VMEM((ZS, 16, 128), BF16),
            pltpu.VMEM((YXS, 16, 128), F32),
            dma,
            dma((6,)),
            dma((3,)),
            dma((3,)),
            dma((ROUNDS, 2)),
            dma((ROUNDS, 2)),
            dma((ROUNDS, 2)),
            dma((ROUNDS, 2)),
            dma((POWER, 2, 8)),
            dma((POWER, 2, 8)),
            dma((3, GROUPS)),
            dma((3, GROUPS)),
            dma((3, 8)),
            dma((3, 8)),
        ],
        compiler_params=pltpu.CompilerParams(
            collective_id=0, has_side_effects=True, vmem_limit_bytes=48 * 1024 * 1024
        ),
    )(
        blocks, connectivity, basal_map, friction.transpose(2, 0, 1), elem_counts,
        obs_weight.T, sign_bits.T, cluster_ids[None, :],
    )
    samples = samp[:, RIM : RIM + 256].T
    refined = refd[:, RIM : RIM + 256].T
    return samples, refined, gram.reshape(64, 8, 32)


def solution(mesh):
    in_specs = (
        P("tiles", None, None),
        P("tiles", None),
        P("tiles", None),
        P("tiles", None, None),
        P("tiles"),
        P("tiles", None),
        P("tiles", "probes"),
        P("tiles"),
    )
    out_specs = (P("tiles", "probes"), P("tiles", "probes"), P(None, "probes", None))
    return jax.shard_map(shards, mesh=mesh, in_specs=in_specs, out_specs=out_specs, check_vma=False)
```

```python
import functools

import jax
import jax.numpy as jnp
from jax import lax
from jax.experimental import pallas as pl
from jax.experimental.pallas import tpu as pltpu
from jax.sharding import PartitionSpec as P

F32 = jnp.float32
BF16 = jnp.bfloat16
I32 = jnp.int32
POWER = 2
ROUNDS = POWER + 1
RIM = 64
ELEMS = 64
DOF = 192
PAIRS = 32
CHUNKS = 16
U_IN = 16
U_PROD = 16
U_EDGE = 16
U_INNER = 16
U_GET = 8
U_PUT = 16
ZS = 8
YXS = 8
GROUPS = 4
EDGE = (0, 1, 16, 17)
INNER = tuple(range(2, 16))
NT = (((1,), (1,)), ((), ()))
NN = (((1,), (0,)), ((), ()))
MESH = pl.DeviceIdType.MESH


def mo(x, n):
    return pl.multiple_of(x, n)


def each(unroll, body, steps=CHUNKS):
    @pl.loop(0, steps // unroll)
    def _(n):
        for j in range(unroll):
            body(n * unroll + j)


def split(x):
    hi = x.astype(BF16).astype(F32)
    return hi, x - hi


def dot(a, b, dims=NN):
    return lax.dot_general(a, b, dims, preferred_element_type=F32)


def kernel(
    blk_hbm, conn_hbm, cell_hbm, fr_hbm, count_ref, w_hbm, sign_hbm, cl_hbm,
    out_ref, gram_ref,
    conn, cell, fr3, w3, sign, cl_ref, idx_ref, qs_ref,
    blk, ohn, ohnt, ohc, ohct, an8, ac8, fr8, rep, sel, pm, pmt,
    gh, gl, xin, fw, fc, acce, acci, te, ti, ad1, ad, ain, yh, yl, pt,
    wn, qsp, qsn, esend, renext, reprev, bs, rbn, rbp, pa, pb, fp, fpn, fpp, gk, ka, kb, kc,
    blk_sem, in_sem, i_s, i_r, e_s, e_r, b_s, b_r, p_s, p_r, g_s, g_r, k_s, k_r,
):
    tile = lax.axis_index("tiles")
    group = lax.axis_index("probes")
    tiles = lax.axis_size("tiles")
    nxt = lax.rem(tile + 1, tiles)
    prv = lax.rem(tile + tiles - 1, tiles)
    my_z = lax.rem(tile, ZS)
    my_yx = lax.div(tile, ZS)
    has_prev = jnp.where(tile > 0, 1.0, 0.0).astype(F32)
    has_next = jnp.where(tile < tiles - 1, 1.0, 0.0).astype(F32)

    def z_peer(d):
        return lax.rem(my_z + d, ZS)

    def yx_peer(d):
        return lax.rem(my_yx + d, YXS)

    def z_device(z):
        return (my_yx * ZS + z, group)

    def yx_device(yx):
        return (yx * ZS + my_z, group)

    def rcopy(src, dst, ss, rs, dev):
        return pltpu.make_async_remote_copy(
            src_ref=src, dst_ref=dst, send_sem=ss, recv_sem=rs, device_id=dev, device_id_type=MESH
        )

    small = [
        pltpu.make_async_copy(src, dst, in_sem.at[n])
        for n, (src, dst) in enumerate(
            [(sign_hbm, sign), (cl_hbm, cl_ref), (w_hbm, w3), (conn_hbm, conn), (cell_hbm, cell), (fr_hbm, fr3)]
        )
    ]
    for cpy in small:
        cpy.start()
    load = pltpu.make_async_copy(blk_hbm, blk, blk_sem)
    load.start()

    barrier = pltpu.get_barrier_semaphore()

    def greet(dev):
        pl.semaphore_signal(barrier, inc=1, device_id=dev, device_id_type=MESH)

    greet((nxt, group))
    greet((prv, group))
    for d in range(1, ZS):
        greet(z_device(z_peer(d)))
    for d in range(1, YXS):
        greet(yx_device(yx_peer(d)))
    for d in range(1, GROUPS):
        other = lax.rem(group + d, GROUPS)
        greet((tile, other))
        greet((nxt, other))
        greet((prv, other))

    def one(cond):
        return jnp.where(cond, 1.0, 0.0).astype(BF16)

    def pair_col(lane):
        half = lane >> 8
        j = lane & 255
        k = (j * 171) >> 9
        return half, k, j - 3 * k, j < DOF

    r = lax.broadcasted_iota(I32, (128, 512), 0)
    half, k, c, ok = pair_col(lax.broadcasted_iota(I32, (128, 512), 1))
    rep[...] = one((r == half * 64 + k) & ok)
    half, k, c, ok = pair_col(lax.broadcasted_iota(I32, (512, 128), 0))
    r = lax.broadcasted_iota(I32, (512, 128), 1)
    sel[...] = one((r == half * 64 + k) & ok)
    r = lax.broadcasted_iota(I32, (384, 512), 0)
    half, k, c, ok = pair_col(lax.broadcasted_iota(I32, (384, 512), 1))
    pm[...] = one((r == c * 128 + half * 64 + k) & ok)
    half, k, c, ok = pair_col(lax.broadcasted_iota(I32, (512, 384), 0))
    r = lax.broadcasted_iota(I32, (512, 384), 1)
    pmt[...] = one((r == c * 128 + half * 64 + k) & ok)

    fw[...] = jnp.zeros(fw.shape, BF16)
    yh[...] = jnp.zeros(yh.shape, BF16)
    yl[...] = jnp.zeros(yl.shape, BF16)

    for cpy in small:
        cpy.wait()

    same_own = (cl_ref[...] & 1) == (lax.broadcasted_iota(I32, (8, 256), 0) & 1)
    start = jnp.where(same_own, (2 * sign[...] - 1).astype(F32), 0.0)
    both = jnp.concatenate([start, jnp.where(same_own, 1.0, 0.0).astype(F32)], axis=0)
    qs_ref[...] = pltpu.roll(
        jnp.concatenate([both, jnp.zeros((16, 128), F32)], axis=1), RIM, 1
    )
    first = [
        rcopy(qs_ref.at[:, pl.ds(256, 128)], qsp, i_s.at[0], i_r.at[0], (nxt, group)),
        rcopy(qs_ref.at[:, pl.ds(0, 128)], qsn, i_s.at[1], i_r.at[1], (prv, group)),
        rcopy(w3.at[:, pl.ds(0, 512)], wn, i_s.at[2], i_r.at[2], (prv, group)),
    ]
    pl.semaphore_wait(barrier, 2 + ZS - 1 + YXS - 1 + 3 * (GROUPS - 1))
    for cpy in first:
        cpy.start()

    idx_ref[0:PAIRS, :] = jnp.concatenate([conn[0:PAIRS, :], conn[PAIRS:ELEMS, :]], axis=1)
    idx_ref[PAIRS:ELEMS, :] = jnp.concatenate([cell[0:PAIRS, :], cell[PAIRS:ELEMS, :]], axis=1)
    element = lax.broadcasted_iota(I32, (PAIRS, 128), 0) + jnp.where(
        lax.broadcasted_iota(I32, (PAIRS, 128), 1) < 64, 0, PAIRS
    )
    live = element < count_ref[0]
    wide = []
    for c in range(3):
        f = jnp.concatenate([fr3[c, 0:PAIRS, :], fr3[c, PAIRS:ELEMS, :]], axis=1)
        wide.append(jnp.where(live, f, 0.0))
    wide = jnp.concatenate(wide, axis=1)
    hi, rest = split(wide)
    mid, lo = split(rest)
    third = dot(jnp.concatenate([hi, mid, lo], axis=0).astype(BF16), pm[...])
    fr = third[0:PAIRS] + third[PAIRS : 2 * PAIRS] + third[2 * PAIRS :]
    for i in range(PAIRS):
        rows = slice(i * 8, i * 8 + 8)
        fr8[rows, :] = jnp.broadcast_to(fr[i : i + 1, :], (8, 512))
    for i in range(CHUNKS):
        rows = slice(i * 8, i * 8 + 8)
        for j in range(2):
            lanes = slice(j * 128, j * 128 + 128)
            n = 2 * i + j
            an8[rows, lanes] = jnp.broadcast_to(idx_ref[n : n + 1, :] >> 8, (8, 128))
            ac8[rows, lanes] = jnp.broadcast_to(idx_ref[PAIRS + n : PAIRS + n + 1, :] >> 7, (8, 128))

    low = jnp.where(
        lax.broadcasted_iota(I32, (64, 128), 0) < PAIRS, idx_ref[...] & 255, idx_ref[...] & 127
    ).astype(F32)
    cols = jnp.transpose(jnp.concatenate([low, jnp.zeros((64, 128), F32)], axis=0))
    lane_n = lax.broadcasted_iota(I32, (128, 256), 1).astype(F32)
    lane_c = lax.broadcasted_iota(I32, (128, 128), 1).astype(F32)
    sub_n = lax.broadcasted_iota(I32, (256, 128), 0)
    sub_c = lax.broadcasted_iota(I32, (128, 128), 0)
    for i in range(PAIRS):
        span = slice(i * 128, i * 128 + 128)
        ohn[:, span] = one(sub_n == (idx_ref[i : i + 1, :] & 255))
        ohc[:, span] = one(sub_c == (idx_ref[PAIRS + i : PAIRS + i + 1, :] & 127))
        ohnt[span, :] = one(lane_n == cols[:, i : i + 1])
        ohct[span, :] = one(lane_c == cols[:, PAIRS + i : PAIRS + i + 1])

    for cpy in first:
        cpy.wait()
    load.wait()

    lane = lax.broadcasted_iota(I32, (8, 128), 1)
    upper = jnp.where(lane >= RIM, 1.0, 0.0).astype(F32)
    own = [upper, jnp.ones((8, 128), F32), 1.0 - upper]
    exist = [
        upper + (1.0 - upper) * has_prev,
        jnp.ones((8, 128), F32),
        (1.0 - upper) + upper * has_next,
    ]
    q = [
        qs_ref[0:8, 0:128] + qsp[0:8, :] * has_prev,
        qs_ref[0:8, 128:256],
        qs_ref[0:8, 256:384] + qsn[0:8, :] * has_next,
    ]
    same = [
        qs_ref[8:16, 0:128] + qsp[8:16, :] * has_prev,
        qs_ref[8:16, 128:256],
        qs_ref[8:16, 256:384] + qsn[8:16, :] * has_next,
    ]

    def square_start(i, cur):
        total = cur[0] * cur[0] * own[0] + cur[1] * cur[1] + cur[2] * cur[2] * own[2]
        pa[i, my_z] = total
        for d in range(1, ZS):
            rcopy(
                pa.at[i, my_z], pa.at[i, my_z], p_s.at[i, 0, d], p_r.at[i, 0, my_z],
                z_device(z_peer(d)),
            ).start()

    def square_mid(i):
        for d in range(1, ZS):
            z = z_peer(d)
            got = rcopy(pa.at[i, z], pa.at[i, z], p_s.at[i, 0, d], p_r.at[i, 0, z], z_device(z))
            got.wait_recv()
            got.wait_send()
        total = pa[i, 0]
        for z in range(1, ZS):
            total = total + pa[i, z]
        pb[i, my_yx] = total
        for d in range(1, YXS):
            rcopy(
                pb.at[i, my_yx], pb.at[i, my_yx], p_s.at[i, 1, d], p_r.at[i, 1, my_yx],
                yx_device(yx_peer(d)),
            ).start()

    def square_end(i):
        for d in range(1, YXS):
            yx = yx_peer(d)
            got = rcopy(
                pb.at[i, yx], pb.at[i, yx], p_s.at[i, 1, d], p_r.at[i, 1, yx], yx_device(yx)
            )
            got.wait_recv()
            got.wait_send()
        total = pb[i, 0]
        for yx in range(1, YXS):
            total = total + pb[i, yx]
        mean = jnp.sum(total, axis=1, keepdims=True) / (256 * tiles)
        return 1.0 / jnp.sqrt(mean + 1e-06)

    def weight(ref, n):
        c = n % 3
        return ref[c : c + 1, n // 3 * 256 : n // 3 * 256 + 256]

    row16 = lax.broadcasted_iota(I32, (16, DOF), 0) < 8

    def scatter_nodes(n, unroll, levels):
        spreads = []
        for j in range(unroll):
            m = n * unroll + j
            r0 = mo(m * 16, 16)
            parts = []
            for c in range(3):
                span = slice(c * 128, c * 128 + 128)
                parts.append(
                    jnp.concatenate([fc[pl.ds(r0, 8), span], fc[pl.ds(r0 + 8, 8), span]], axis=1)
                )
            a = an8[pl.ds(mo(m * 8, 8), 8), :]
            spread = jnp.concatenate(
                [jnp.where(a == lv, parts[c], 0.0) for lv in levels for c in range(3)], axis=0
            )
            spreads.append(spread.astype(BF16))
        size = unroll * 256
        return dot(jnp.concatenate(spreads, axis=1), ohnt[pl.ds(mo(n * size, size), size), :])

    def gather_nodes(m, table, levels, base):
        got = dot(table[...], ohn[:, pl.ds(mo(m * 512, 512), 512)])
        r = mo(m * 16, 16)
        a = jnp.concatenate([an8[pl.ds(r, 8), :], an8[pl.ds(r + 8, 8), :]], axis=1)
        out = list(base)
        for n, lv in enumerate(levels):
            hit = a == lv
            for c in range(3):
                row = (n * 3 + c) * 8
                out[c] = jnp.where(hit, got[row : row + 8], out[c])
        return out

    def hessian(h, q):
        parts = []
        for b in q:
            parts += list(split(b))
        cells = jnp.concatenate(parts, axis=0).astype(BF16)

        def gather_cells(m):
            got = dot(cells, ohc[:, pl.ds(mo(m * 256, 256), 256)])
            a = ac8[pl.ds(mo(m * 8, 8), 8), :]
            g = jnp.where(
                a == 0,
                got[0:8] + got[8:16],
                jnp.where(a == 1, got[16:24] + got[24:32], got[32:40] + got[40:48]),
            )
            hi, lo = split(g)
            rows = pl.ds(mo(m * 16, 16), 16)
            gh[rows, :] = jnp.concatenate([hi[:, :128], hi[:, 128:]], axis=0).astype(BF16)
            gl[rows, :] = jnp.concatenate([lo[:, :128], lo[:, 128:]], axis=0).astype(BF16)

        each(U_IN, gather_cells)

        for i in range(4):
            rows = slice(i * 64, i * 64 + 64)
            wide = dot(gh[rows, :], rep[...]) + dot(gl[rows, :], rep[...])
            xin[rows, :] = (wide * fr8[rows, :]).astype(BF16)

        def forward(m):
            rows = pl.ds(mo(m * 16, 16), 16)
            for half in range(2):
                span = slice(half * 256, half * 256 + DOF)
                x = xin[rows, span]
                o0 = dot(x, blk[2 * m + PAIRS * half], NT)
                o1 = dot(x, blk[2 * m + 1 + PAIRS * half], NT)
                fw[rows, span] = jnp.where(row16, o0, o1).astype(BF16)

        each(U_PROD, forward)

        for i in range(4):
            rows = slice(i * 64, i * 64 + 64)
            fc[rows, :] = dot(fw[rows, :], pmt[...])

        acce[...] = jnp.zeros(acce.shape, F32)
        acci[...] = jnp.zeros(acci.shape, F32)

        @pl.loop(0, CHUNKS // U_EDGE)
        def _(n):
            acce[...] += scatter_nodes(n, U_EDGE, EDGE)

        esend[h] = acce[...].astype(BF16)
        swap = [
            rcopy(esend.at[h, pl.ds(0, 48), :], renext.at[h], e_s.at[h, 0], e_r.at[h, 0], (prv, group)),
            rcopy(esend.at[h, pl.ds(48, 48), :], reprev.at[h], e_s.at[h, 1], e_r.at[h, 1], (nxt, group)),
        ]
        for cpy in swap:
            cpy.start()

        @pl.loop(0, CHUNKS // U_INNER)
        def _(n):
            acci[...] += scatter_nodes(n, U_INNER, INNER)

        if h > 0:
            square_mid(h - 1)

        for i in range(21):
            pair = []
            for j in range(2):
                n = 2 * i + j
                pair.append(acci[n * 8 : n * 8 + 8, :] * weight(w3, 6 + n))
            ti[i * 16 : i * 16 + 16, :] = jnp.concatenate(pair, axis=0).astype(BF16)

        def gather_inner(m):
            zero = jnp.zeros((8, 512), F32)
            out = gather_nodes(m, ti, INNER, [zero] * 3)
            r0 = mo(m * 32, 32)
            for c in range(3):
                span = slice(c * 128, c * 128 + 128)
                for j in range(4):
                    ad1[pl.ds(r0 + 8 * j, 8), span] = out[c][:, j * 128 : j * 128 + 128]

        each(U_GET, gather_inner, CHUNKS // 2)

        for cpy in swap:
            cpy.wait()
        for i in range(6):
            if i < 3:
                theirs = reprev[h, i * 16 : i * 16 + 16, :].astype(F32) * has_prev
            else:
                theirs = renext[h, i * 16 - 48 : i * 16 - 32, :].astype(F32)
            total = acce[i * 16 : i * 16 + 16, :] + theirs
            pair = []
            for j in range(2):
                n = 2 * i + j
                scale = weight(w3, n) if n < 6 else weight(wn, n - 6) * has_next
                pair.append(total[j * 8 : j * 8 + 8] * scale)
            te[i * 16 : i * 16 + 16, :] = jnp.concatenate(pair, axis=0).astype(BF16)

        def gather_edge(m):
            r0 = mo(m * 32, 32)
            base = []
            for c in range(3):
                span = slice(c * 128, c * 128 + 128)
                base.append(
                    jnp.concatenate([ad1[pl.ds(r0 + 8 * j, 8), span] for j in range(4)], axis=1)
                )
            out = gather_nodes(m, te, EDGE, base)
            for c in range(3):
                span = slice(c * 128, c * 128 + 128)
                ad[pl.ds(r0, 32), span] = jnp.concatenate(
                    [out[c][:, j * 128 : j * 128 + 128] for j in range(4)], axis=0
                ).astype(BF16)

        each(U_GET, gather_edge, CHUNKS // 2)

        for i in range(4):
            rows = slice(i * 64, i * 64 + 64)
            ain[rows, :] = dot(ad[rows, :], pm[...]).astype(BF16)

        def adjoint(m):
            rows = pl.ds(mo(m * 16, 16), 16)
            for half in range(2):
                span = slice(half * 256, half * 256 + DOF)
                x = ain[rows, span]
                o0 = dot(x, blk[2 * m + PAIRS * half])
                o1 = dot(x, blk[2 * m + 1 + PAIRS * half])
                hi, lo = split(jnp.where(row16, o0, o1) * fr8[rows, span])
                yh[rows, span] = hi.astype(BF16)
                yl[rows, span] = lo.astype(BF16)

        each(U_PROD, adjoint)

        for i in range(4):
            rows = slice(i * 64, i * 64 + 64)
            pt[rows, :] = dot(yh[rows, :], sel[...]) + dot(yl[rows, :], sel[...])

        def scatter_cells(n, acc):
            spreads = []
            for j in range(U_PUT):
                m = n * U_PUT + j
                r0 = mo(m * 16, 16)
                v = jnp.concatenate([pt[pl.ds(r0, 8), :], pt[pl.ds(r0 + 8, 8), :]], axis=1)
                a = ac8[pl.ds(mo(m * 8, 8), 8), :]
                spread = jnp.concatenate(
                    [jnp.where(a == lv, s, 0.0) for lv in range(3) for s in split(v)], axis=0
                )
                spreads.append(spread.astype(BF16))
            size = U_PUT * 256
            return acc + dot(
                jnp.concatenate(spreads, axis=1), ohct[pl.ds(mo(n * size, size), size), :]
            )

        acc = lax.fori_loop(0, CHUNKS // U_PUT, scatter_cells, jnp.zeros((48, 128), F32))
        sums = [acc[n * 16 : n * 16 + 8] + acc[n * 16 + 8 : n * 16 + 16] for n in range(3)]
        keep = same if h % 2 == 1 else [exist[n] - same[n] for n in range(3)]
        if h == POWER:
            scale = square_end(h - 1)
            for n in range(3):
                fp[group, :, n * 128 : n * 128 + 128] = sums[n] * keep[n] * scale
            return None
        bs[h, 0] = sums[0]
        bs[h, 1] = sums[2]
        swap = [
            rcopy(bs.at[h, 0], rbn.at[h], b_s.at[h, 0], b_r.at[h, 0], (prv, group)),
            rcopy(bs.at[h, 1], rbp.at[h], b_s.at[h, 1], b_r.at[h, 1], (nxt, group)),
        ]
        for cpy in swap:
            cpy.start()
        scale = square_end(h - 1) if h > 0 else None
        for cpy in swap:
            cpy.wait()
        sums[0] = sums[0] + rbp[h] * has_prev
        sums[2] = sums[2] + rbn[h] * has_next
        out = []
        for n in range(3):
            v = sums[n] * keep[n]
            out.append(v if scale is None else v * scale)
        return out

    for h in range(ROUNDS):
        q = hessian(h, q)
        if h < POWER:
            square_start(h, q)
        if h == 0:
            out_ref[0:8, :] = pltpu.roll(jnp.concatenate(q, axis=1), 384 - RIM, 1)[:, :256]
    def final(kind, d, source):
        other = lax.rem(group + d, GROUPS)
        device, landing, span = (
            ((prv, other), fpn, pl.ds(0, 128)),
            ((nxt, other), fpp, pl.ds(256, 128)),
            ((tile, other), fp, pl.ds(0, 384)),
        )[kind]
        return rcopy(
            fp.at[group, :, span], landing.at[source], g_s.at[kind, d], g_r.at[kind, source], device
        )

    order = [(kind, d) for d in range(GROUPS) for kind in range(3) if kind < 2 or d > 0]
    for kind, d in order:
        final(kind, d, group).start()
    for kind, d in order:
        final(kind, d, lax.rem(group + d, GROUPS)).wait_recv()
    for kind, d in order:
        final(kind, d, group).wait_send()

    def window(g):
        return jnp.concatenate(
            [
                fp[g, :, 0:128] + fpp[g] * has_prev,
                fp[g, :, 128:256],
                fp[g, :, 256:384] + fpn[g] * has_next,
            ],
            axis=1,
        )

    mine = pltpu.roll(window(group), 384 - RIM, 1)[:, :256]
    out_ref[8:16, :] = mine
    every = jnp.concatenate([window(g) for g in range(GROUPS)], axis=0)
    every = pltpu.roll(every, 384 - RIM, 1)[:, :256]
    outer = jnp.concatenate([every * mine[i : i + 1, :] for i in range(8)], axis=0)
    hi, lo = split(outer)
    member = one(lax.broadcasted_iota(I32, (64, 256), 0) == cl_ref[...])
    grams = dot(member, hi.astype(BF16), NT) + dot(member, lo.astype(BF16), NT)
    for yx in range(YXS):
        rows = grams[yx * 8 : yx * 8 + 8]
        gk[yx] = jnp.concatenate([rows[:, :128], rows[:, 128:]], axis=0).astype(BF16)

    for d in range(1, YXS):
        yx = yx_peer(d)
        rcopy(
            gk.at[yx], ka.at[my_yx], k_s.at[0, d], k_r.at[0, my_yx],
            yx_device(yx),
        ).start()
    for d in range(1, YXS):
        yx = yx_peer(d)
        got = rcopy(ka.at[yx], ka.at[yx], k_s.at[0, d], k_r.at[0, yx], yx_device(yx))
        got.wait_recv()
        got.wait_send()
    ka[my_yx] = gk[my_yx]
    total = ka[0].astype(F32)
    for yx in range(1, YXS):
        total = total + ka[yx].astype(F32)
    kb[my_z] = total.astype(BF16)
    for d in range(1, ZS):
        rcopy(
            kb.at[my_z], kb.at[my_z], k_s.at[1, d], k_r.at[1, my_z], z_device(z_peer(d))
        ).start()
    for d in range(1, ZS):
        z = z_peer(d)
        got = rcopy(kb.at[z], kb.at[z], k_s.at[1, d], k_r.at[1, z], z_device(z))
        got.wait_recv()
        got.wait_send()
    total = kb[0].astype(F32)
    for z in range(1, ZS):
        total = total + kb[z].astype(F32)
    kc[my_yx] = total
    for d in range(1, YXS):
        rcopy(
            kc.at[my_yx], kc.at[my_yx], k_s.at[2, d], k_r.at[2, my_yx], yx_device(yx_peer(d))
        ).start()
    for d in range(1, YXS):
        yx = yx_peer(d)
        got = rcopy(kc.at[yx], kc.at[yx], k_s.at[2, d], k_r.at[2, yx], yx_device(yx))
        got.wait_recv()
        got.wait_send()
    for yx in range(YXS):
        gram_ref[yx * 8 : yx * 8 + 8, 0:128] = kc[yx, 0:8]
        gram_ref[yx * 8 : yx * 8 + 8, 128:256] = kc[yx, 8:16]


def shards(
    blocks, connectivity, basal_map, friction, elem_counts, obs_weight, sign_bits, cluster_ids
):
    vmem = pl.BlockSpec(memory_space=pltpu.VMEM)
    here = pl.BlockSpec(memory_space=pl.ANY)
    dma = pltpu.SemaphoreType.DMA
    cells, gram = pl.pallas_call(
        kernel,
        out_shape=(
            jax.ShapeDtypeStruct((16, 256), F32),
            jax.ShapeDtypeStruct((64, 256), F32),
        ),
        in_specs=[here] * 4 + [pl.BlockSpec(memory_space=pltpu.SMEM)] + [here] * 3,
        out_specs=(vmem, vmem),
        scratch_shapes=[
            pltpu.VMEM((ELEMS, 64), I32),
            pltpu.VMEM((ELEMS, 64), I32),
            pltpu.VMEM((3, ELEMS, 64), F32),
            pltpu.VMEM((3, 4096), F32),
            pltpu.VMEM((8, 256), I32),
            pltpu.VMEM((1, 256), I32),
            pltpu.VMEM((ELEMS, 128), I32),
            pltpu.VMEM((16, 384), F32),
            pltpu.VMEM((ELEMS, DOF, DOF), BF16),
            pltpu.VMEM((256, 4096), BF16),
            pltpu.VMEM((4096, 256), BF16),
            pltpu.VMEM((128, 4096), BF16),
            pltpu.VMEM((4096, 128), BF16),
            pltpu.VMEM((128, 256), I32),
            pltpu.VMEM((128, 256), I32),
            pltpu.VMEM((256, 512), F32),
            pltpu.VMEM((128, 512), BF16),
            pltpu.VMEM((512, 128), BF16),
            pltpu.VMEM((384, 512), BF16),
            pltpu.VMEM((512, 384), BF16),
            pltpu.VMEM((256, 128), BF16),
            pltpu.VMEM((256, 128), BF16),
            pltpu.VMEM((256, 512), BF16),
            pltpu.VMEM((256, 512), BF16),
            pltpu.VMEM((256, 384), F32),
            pltpu.VMEM((96, 256), F32),
            pltpu.VMEM((336, 256), F32),
            pltpu.VMEM((96, 256), BF16),
            pltpu.VMEM((336, 256), BF16),
            pltpu.VMEM((256, 384), F32),
            pltpu.VMEM((256, 384), BF16),
            pltpu.VMEM((256, 512), BF16),
            pltpu.VMEM((256, 512), BF16),
            pltpu.VMEM((256, 512), BF16),
            pltpu.VMEM((256, 128), F32),
            pltpu.VMEM((3, 512), F32),
            pltpu.VMEM((16, 128), F32),
            pltpu.VMEM((16, 128), F32),
            pltpu.VMEM((ROUNDS, 96, 256), BF16),
            pltpu.VMEM((ROUNDS, 48, 256), BF16),
            pltpu.VMEM((ROUNDS, 48, 256), BF16),
            pltpu.VMEM((ROUNDS, 2, 8, 128), F32),
            pltpu.VMEM((ROUNDS, 8, 128), F32),
            pltpu.VMEM((ROUNDS, 8, 128), F32),
            pltpu.VMEM((POWER, ZS, 8, 128), F32),
            pltpu.VMEM((POWER, YXS, 8, 128), F32),
            pltpu.VMEM((GROUPS, 8, 384), F32),
            pltpu.VMEM((GROUPS, 8, 128), F32),
            pltpu.VMEM((GROUPS, 8, 128), F32),
            pltpu.VMEM((YXS, 16, 128), BF16),
            pltpu.VMEM((YXS, 16, 128), BF16),
            pltpu.VMEM((ZS, 16, 128), BF16),
            pltpu.VMEM((YXS, 16, 128), F32),
            dma,
            dma((6,)),
            dma((3,)),
            dma((3,)),
            dma((ROUNDS, 2)),
            dma((ROUNDS, 2)),
            dma((ROUNDS, 2)),
            dma((ROUNDS, 2)),
            dma((POWER, 2, 8)),
            dma((POWER, 2, 8)),
            dma((3, GROUPS)),
            dma((3, GROUPS)),
            dma((3, 8)),
            dma((3, 8)),
        ],
        compiler_params=pltpu.CompilerParams(
            collective_id=0, has_side_effects=True, vmem_limit_bytes=63 * 1024 * 1024
        ),
    )(
        blocks, connectivity, basal_map, friction.transpose(2, 0, 1), elem_counts,
        obs_weight.T, sign_bits.T, cluster_ids[None, :],
    )
    return cells[:8].T, cells[8:].T, gram.reshape(64, 8, 32)


def solution(mesh):
    in_specs = (
        P("tiles", None, None),
        P("tiles", None),
        P("tiles", None),
        P("tiles", None, None),
        P("tiles"),
        P("tiles", None),
        P("tiles", "probes"),
        P("tiles"),
    )
    out_specs = (P("tiles", "probes"), P("tiles", "probes"), P(None, "probes", None))
    return jax.shard_map(shards, mesh=mesh, in_specs=in_specs, out_specs=out_specs, check_vma=False)
```

```python
import functools

import jax
import jax.numpy as jnp
from jax import lax
from jax.experimental import pallas as pl
from jax.experimental.pallas import tpu as pltpu
from jax.sharding import PartitionSpec as P

F32 = jnp.float32
BF16 = jnp.bfloat16
I32 = jnp.int32
POWER = 2
ROUNDS = POWER + 1
RIM = 64
ELEMS = 64
DOF = 192
PAIRS = 32
CHUNKS = 16
U_IN = 16
U_PROD = 16
U_EDGE = 8
U_INNER = 8
U_GET = 4
U_PUT = 16
ZS = 8
YXS = 8
GROUPS = 4
EDGE = (0, 1, 16, 17)
INNER = tuple(range(2, 16))
NT = (((1,), (1,)), ((), ()))
NN = (((1,), (0,)), ((), ()))
MESH = pl.DeviceIdType.MESH


def mo(x, n):
    return pl.multiple_of(x, n)


def each(unroll, body, steps=CHUNKS):
    @pl.loop(0, steps // unroll)
    def _(n):
        for j in range(unroll):
            body(n * unroll + j)


def split(x):
    hi = x.astype(BF16).astype(F32)
    return hi, x - hi


def dot(a, b, dims=NN):
    return lax.dot_general(a, b, dims, preferred_element_type=F32)


def kernel(
    blk_hbm, conn_hbm, cell_hbm, fr_hbm, count_ref, w_hbm, sign_hbm, cl_hbm,
    out_ref, gram_ref,
    conn, cell, fr3, w3, sign, cl_ref, idx_ref, qs_ref,
    blk, ohn, ohnt, ohc, ohct, an8, ac8, fr8, rep, sel, pm, pmt,
    gh, gl, xin, fw, fc, acce, acci, te, ti, ad1, ad, ain, yh, yl, pt,
    wn, qsp, qsn, esend, renext, reprev, bs, rbn, rbp, pa, pb, fp, fpn, fpp, gk, ka, kb, kc,
    blk_sem, in_sem, i_s, i_r, e_s, e_r, b_s, b_r, s_s, p_r, g_s, g_r, k_r,
):
    tile = lax.axis_index("tiles")
    group = lax.axis_index("probes")
    tiles = lax.axis_size("tiles")
    nxt = lax.rem(tile + 1, tiles)
    prv = lax.rem(tile + tiles - 1, tiles)
    my_z = lax.rem(tile, ZS)
    my_yx = lax.div(tile, ZS)
    has_prev = jnp.where(tile > 0, 1.0, 0.0).astype(F32)
    has_next = jnp.where(tile < tiles - 1, 1.0, 0.0).astype(F32)

    def z_peer(d):
        return lax.rem(my_z + d, ZS)

    def yx_peer(d):
        return lax.rem(my_yx + d, YXS)

    def z_device(z):
        return (my_yx * ZS + z, group)

    def yx_device(yx):
        return (yx * ZS + my_z, group)

    def rcopy(src, dst, ss, rs, dev):
        return pltpu.make_async_remote_copy(
            src_ref=src, dst_ref=dst, send_sem=ss, recv_sem=rs, device_id=dev, device_id_type=MESH
        )

    small = [
        pltpu.make_async_copy(src, dst, in_sem.at[n])
        for n, (src, dst) in enumerate(
            [(sign_hbm, sign), (cl_hbm, cl_ref), (w_hbm, w3), (conn_hbm, conn), (cell_hbm, cell), (fr_hbm, fr3)]
        )
    ]
    for cpy in small:
        cpy.start()
    load = pltpu.make_async_copy(blk_hbm, blk, blk_sem)
    load.start()

    barrier = pltpu.get_barrier_semaphore()

    def greet(dev):
        pl.semaphore_signal(barrier, inc=1, device_id=dev, device_id_type=MESH)

    greet((nxt, group))
    greet((prv, group))
    for d in range(1, ZS):
        greet(z_device(z_peer(d)))
    for d in range(1, YXS):
        greet(yx_device(yx_peer(d)))
    for d in range(1, GROUPS):
        other = lax.rem(group + d, GROUPS)
        greet((tile, other))
        greet((nxt, other))
        greet((prv, other))

    def one(cond):
        return jnp.where(cond, 1.0, 0.0).astype(BF16)

    def pair_col(lane):
        half = lane >> 8
        j = lane & 255
        k = (j * 171) >> 9
        return half, k, j - 3 * k, j < DOF

    r = lax.broadcasted_iota(I32, (128, 512), 0)
    half, k, c, ok = pair_col(lax.broadcasted_iota(I32, (128, 512), 1))
    rep[...] = one((r == half * 64 + k) & ok)
    half, k, c, ok = pair_col(lax.broadcasted_iota(I32, (512, 128), 0))
    r = lax.broadcasted_iota(I32, (512, 128), 1)
    sel[...] = one((r == half * 64 + k) & ok)
    r = lax.broadcasted_iota(I32, (384, 512), 0)
    half, k, c, ok = pair_col(lax.broadcasted_iota(I32, (384, 512), 1))
    pm[...] = one((r == c * 128 + half * 64 + k) & ok)
    half, k, c, ok = pair_col(lax.broadcasted_iota(I32, (512, 384), 0))
    r = lax.broadcasted_iota(I32, (512, 384), 1)
    pmt[...] = one((r == c * 128 + half * 64 + k) & ok)

    fw[...] = jnp.zeros(fw.shape, BF16)
    yh[...] = jnp.zeros(yh.shape, BF16)
    yl[...] = jnp.zeros(yl.shape, BF16)

    for cpy in small:
        cpy.wait()

    same_own = (cl_ref[...] & 1) == (lax.broadcasted_iota(I32, (8, 256), 0) & 1)
    start = jnp.where(same_own, (2 * sign[...] - 1).astype(F32), 0.0)
    both = jnp.concatenate([start, jnp.where(same_own, 1.0, 0.0).astype(F32)], axis=0)
    qs_ref[...] = pltpu.roll(
        jnp.concatenate([both, jnp.zeros((16, 128), F32)], axis=1), RIM, 1
    )
    first = [
        rcopy(qs_ref.at[:, pl.ds(256, 128)], qsp, i_s.at[0], i_r.at[0], (nxt, group)),
        rcopy(qs_ref.at[:, pl.ds(0, 128)], qsn, i_s.at[1], i_r.at[1], (prv, group)),
        rcopy(w3.at[:, pl.ds(0, 512)], wn, i_s.at[2], i_r.at[2], (prv, group)),
    ]
    pl.semaphore_wait(barrier, 2 + ZS - 1 + YXS - 1 + 3 * (GROUPS - 1))
    for cpy in first:
        cpy.start()

    idx_ref[0:PAIRS, :] = jnp.concatenate([conn[0:PAIRS, :], conn[PAIRS:ELEMS, :]], axis=1)
    idx_ref[PAIRS:ELEMS, :] = jnp.concatenate([cell[0:PAIRS, :], cell[PAIRS:ELEMS, :]], axis=1)
    element = lax.broadcasted_iota(I32, (PAIRS, 128), 0) + jnp.where(
        lax.broadcasted_iota(I32, (PAIRS, 128), 1) < 64, 0, PAIRS
    )
    live = element < count_ref[0]
    wide = []
    for c in range(3):
        f = jnp.concatenate([fr3[c, 0:PAIRS, :], fr3[c, PAIRS:ELEMS, :]], axis=1)
        wide.append(jnp.where(live, f, 0.0))
    wide = jnp.concatenate(wide, axis=1)
    hi, rest = split(wide)
    mid, lo = split(rest)
    third = dot(jnp.concatenate([hi, mid, lo], axis=0).astype(BF16), pm[...])
    fr = third[0:PAIRS] + third[PAIRS : 2 * PAIRS] + third[2 * PAIRS :]
    for i in range(PAIRS):
        rows = slice(i * 8, i * 8 + 8)
        fr8[rows, :] = jnp.broadcast_to(fr[i : i + 1, :], (8, 512))
    for i in range(CHUNKS):
        rows = slice(i * 8, i * 8 + 8)
        for j in range(2):
            lanes = slice(j * 128, j * 128 + 128)
            n = 2 * i + j
            an8[rows, lanes] = jnp.broadcast_to(idx_ref[n : n + 1, :] >> 8, (8, 128))
            ac8[rows, lanes] = jnp.broadcast_to(idx_ref[PAIRS + n : PAIRS + n + 1, :] >> 7, (8, 128))

    low = jnp.where(
        lax.broadcasted_iota(I32, (64, 128), 0) < PAIRS, idx_ref[...] & 255, idx_ref[...] & 127
    ).astype(F32)
    cols = jnp.transpose(jnp.concatenate([low, jnp.zeros((64, 128), F32)], axis=0))
    lane_n = lax.broadcasted_iota(I32, (128, 256), 1).astype(F32)
    lane_c = lax.broadcasted_iota(I32, (128, 128), 1).astype(F32)
    sub_n = lax.broadcasted_iota(I32, (256, 128), 0)
    sub_c = lax.broadcasted_iota(I32, (128, 128), 0)
    for i in range(PAIRS):
        span = slice(i * 128, i * 128 + 128)
        ohn[:, span] = one(sub_n == (idx_ref[i : i + 1, :] & 255))
        ohc[:, span] = one(sub_c == (idx_ref[PAIRS + i : PAIRS + i + 1, :] & 127))
        ohnt[span, :] = one(lane_n == cols[:, i : i + 1])
        ohct[span, :] = one(lane_c == cols[:, PAIRS + i : PAIRS + i + 1])

    for cpy in first:
        cpy.wait()
    load.wait()

    lane = lax.broadcasted_iota(I32, (8, 128), 1)
    upper = jnp.where(lane >= RIM, 1.0, 0.0).astype(F32)
    own = [upper, jnp.ones((8, 128), F32), 1.0 - upper]
    exist = [
        upper + (1.0 - upper) * has_prev,
        jnp.ones((8, 128), F32),
        (1.0 - upper) + upper * has_next,
    ]
    q = [
        qs_ref[0:8, 0:128] + qsp[0:8, :] * has_prev,
        qs_ref[0:8, 128:256],
        qs_ref[0:8, 256:384] + qsn[0:8, :] * has_next,
    ]
    same = [
        qs_ref[8:16, 0:128] + qsp[8:16, :] * has_prev,
        qs_ref[8:16, 128:256],
        qs_ref[8:16, 256:384] + qsn[8:16, :] * has_next,
    ]

    def square_start(i, cur):
        total = cur[0] * cur[0] * own[0] + cur[1] * cur[1] + cur[2] * cur[2] * own[2]
        pa[i, my_z] = total
        for d in range(1, ZS):
            rcopy(
                pa.at[i, my_z], pa.at[i, my_z], s_s.at[d], p_r.at[i, 0, my_z],
                z_device(z_peer(d)),
            ).start()

    def square_mid(i):
        for d in range(1, ZS):
            z = z_peer(d)
            got = rcopy(pa.at[i, z], pa.at[i, z], s_s.at[d], p_r.at[i, 0, z], z_device(z))
            got.wait_recv()
            got.wait_send()
        total = pa[i, 0]
        for z in range(1, ZS):
            total = total + pa[i, z]
        pb[i, my_yx] = total
        for d in range(1, YXS):
            rcopy(
                pb.at[i, my_yx], pb.at[i, my_yx], s_s.at[d], p_r.at[i, 1, my_yx],
                yx_device(yx_peer(d)),
            ).start()

    def square_end(i):
        for d in range(1, YXS):
            yx = yx_peer(d)
            got = rcopy(
                pb.at[i, yx], pb.at[i, yx], s_s.at[d], p_r.at[i, 1, yx], yx_device(yx)
            )
            got.wait_recv()
            got.wait_send()
        total = pb[i, 0]
        for yx in range(1, YXS):
            total = total + pb[i, yx]
        mean = jnp.sum(total, axis=1, keepdims=True) / (256 * tiles)
        return 1.0 / jnp.sqrt(mean + 1e-06)

    def weight(ref, n):
        c = n % 3
        return ref[c : c + 1, n // 3 * 256 : n // 3 * 256 + 256]

    row16 = lax.broadcasted_iota(I32, (16, DOF), 0) < 8

    def scatter_nodes(n, unroll, levels):
        spreads = []
        for j in range(unroll):
            m = n * unroll + j
            r0 = mo(m * 16, 16)
            parts = []
            for c in range(3):
                span = slice(c * 128, c * 128 + 128)
                parts.append(
                    jnp.concatenate([fc[pl.ds(r0, 8), span], fc[pl.ds(r0 + 8, 8), span]], axis=1)
                )
            a = an8[pl.ds(mo(m * 8, 8), 8), :]
            spread = jnp.concatenate(
                [jnp.where(a == lv, parts[c], 0.0) for lv in levels for c in range(3)], axis=0
            )
            spreads.append(spread.astype(BF16))
        size = unroll * 256
        return dot(jnp.concatenate(spreads, axis=1), ohnt[pl.ds(mo(n * size, size), size), :])

    def gather_nodes(m, table, levels, base):
        got = dot(table[...], ohn[:, pl.ds(mo(m * 512, 512), 512)])
        r = mo(m * 16, 16)
        a = jnp.concatenate([an8[pl.ds(r, 8), :], an8[pl.ds(r + 8, 8), :]], axis=1)
        out = list(base)
        for n, lv in enumerate(levels):
            hit = a == lv
            for c in range(3):
                row = (n * 3 + c) * 8
                out[c] = jnp.where(hit, got[row : row + 8], out[c])
        return out

    def hessian(h, q):
        terms = 2 if h > 0 else 1
        parts = []
        for b in q:
            parts += list(split(b))[:terms]
        cells = jnp.concatenate(parts, axis=0).astype(BF16)

        def gather_cells(m):
            got = dot(cells, ohc[:, pl.ds(mo(m * 256, 256), 256)])
            a = ac8[pl.ds(mo(m * 8, 8), 8), :]
            level = []
            for n in range(3):
                r = n * 8 * terms
                level.append(got[r : r + 8] + got[r + 8 : r + 16] if h > 0 else got[r : r + 8])
            g = jnp.where(a == 0, level[0], jnp.where(a == 1, level[1], level[2]))
            hi, lo = split(g)
            rows = pl.ds(mo(m * 16, 16), 16)
            gh[rows, :] = jnp.concatenate([hi[:, :128], hi[:, 128:]], axis=0).astype(BF16)
            if h > 0:
                gl[rows, :] = jnp.concatenate([lo[:, :128], lo[:, 128:]], axis=0).astype(BF16)

        each(U_IN, gather_cells)

        for i in range(4):
            rows = slice(i * 64, i * 64 + 64)
            wide = dot(gh[rows, :], rep[...])
            if h > 0:
                wide = wide + dot(gl[rows, :], rep[...])
            xin[rows, :] = (wide * fr8[rows, :]).astype(BF16)

        def forward(m):
            rows = pl.ds(mo(m * 16, 16), 16)
            for half in range(2):
                span = slice(half * 256, half * 256 + DOF)
                x = xin[rows, span]
                o0 = dot(x, blk[2 * m + PAIRS * half], NT)
                o1 = dot(x, blk[2 * m + 1 + PAIRS * half], NT)
                fw[rows, span] = jnp.where(row16, o0, o1).astype(BF16)

        each(U_PROD, forward)

        for i in range(4):
            rows = slice(i * 64, i * 64 + 64)
            fc[rows, :] = dot(fw[rows, :], pmt[...])

        acce[...] = jnp.zeros(acce.shape, F32)
        acci[...] = jnp.zeros(acci.shape, F32)

        @pl.loop(0, CHUNKS // U_EDGE)
        def _(n):
            acce[...] += scatter_nodes(n, U_EDGE, EDGE)

        esend[h] = acce[...].astype(BF16)
        swap = [
            rcopy(esend.at[h, pl.ds(0, 48), :], renext.at[h], e_s.at[h, 0], e_r.at[h, 0], (prv, group)),
            rcopy(esend.at[h, pl.ds(48, 48), :], reprev.at[h], e_s.at[h, 1], e_r.at[h, 1], (nxt, group)),
        ]
        for cpy in swap:
            cpy.start()

        @pl.loop(0, CHUNKS // U_INNER)
        def _(n):
            acci[...] += scatter_nodes(n, U_INNER, INNER)

        if h > 0:
            square_mid(h - 1)

        for i in range(21):
            pair = []
            for j in range(2):
                n = 2 * i + j
                pair.append(acci[n * 8 : n * 8 + 8, :] * weight(w3, 6 + n))
            ti[i * 16 : i * 16 + 16, :] = jnp.concatenate(pair, axis=0).astype(BF16)

        def gather_inner(m):
            zero = jnp.zeros((8, 512), F32)
            out = gather_nodes(m, ti, INNER, [zero] * 3)
            r0 = mo(m * 32, 32)
            for c in range(3):
                span = slice(c * 128, c * 128 + 128)
                for j in range(4):
                    ad1[pl.ds(r0 + 8 * j, 8), span] = out[c][:, j * 128 : j * 128 + 128]

        each(U_GET, gather_inner, CHUNKS // 2)

        for cpy in swap:
            cpy.wait()
        for i in range(6):
            if i < 3:
                theirs = reprev[h, i * 16 : i * 16 + 16, :].astype(F32) * has_prev
            else:
                theirs = renext[h, i * 16 - 48 : i * 16 - 32, :].astype(F32)
            total = acce[i * 16 : i * 16 + 16, :] + theirs
            pair = []
            for j in range(2):
                n = 2 * i + j
                scale = weight(w3, n) if n < 6 else weight(wn, n - 6) * has_next
                pair.append(total[j * 8 : j * 8 + 8] * scale)
            te[i * 16 : i * 16 + 16, :] = jnp.concatenate(pair, axis=0).astype(BF16)

        def gather_edge(m):
            r0 = mo(m * 32, 32)
            base = []
            for c in range(3):
                span = slice(c * 128, c * 128 + 128)
                base.append(
                    jnp.concatenate([ad1[pl.ds(r0 + 8 * j, 8), span] for j in range(4)], axis=1)
                )
            out = gather_nodes(m, te, EDGE, base)
            for c in range(3):
                span = slice(c * 128, c * 128 + 128)
                ad[pl.ds(r0, 32), span] = jnp.concatenate(
                    [out[c][:, j * 128 : j * 128 + 128] for j in range(4)], axis=0
                ).astype(BF16)

        each(U_GET, gather_edge, CHUNKS // 2)

        for i in range(4):
            rows = slice(i * 64, i * 64 + 64)
            ain[rows, :] = dot(ad[rows, :], pm[...]).astype(BF16)

        def adjoint(m):
            rows = pl.ds(mo(m * 16, 16), 16)
            for half in range(2):
                span = slice(half * 256, half * 256 + DOF)
                x = ain[rows, span]
                o0 = dot(x, blk[2 * m + PAIRS * half])
                o1 = dot(x, blk[2 * m + 1 + PAIRS * half])
                hi, lo = split(jnp.where(row16, o0, o1) * fr8[rows, span])
                yh[rows, span] = hi.astype(BF16)
                yl[rows, span] = lo.astype(BF16)

        each(U_PROD, adjoint)

        for i in range(4):
            rows = slice(i * 64, i * 64 + 64)
            pt[rows, :] = dot(yh[rows, :], sel[...]) + dot(yl[rows, :], sel[...])

        def scatter_cells(n, acc):
            spreads = []
            for j in range(U_PUT):
                m = n * U_PUT + j
                r0 = mo(m * 16, 16)
                v = jnp.concatenate([pt[pl.ds(r0, 8), :], pt[pl.ds(r0 + 8, 8), :]], axis=1)
                a = ac8[pl.ds(mo(m * 8, 8), 8), :]
                spread = jnp.concatenate(
                    [jnp.where(a == lv, s, 0.0) for lv in range(3) for s in split(v)], axis=0
                )
                spreads.append(spread.astype(BF16))
            size = U_PUT * 256
            return acc + dot(
                jnp.concatenate(spreads, axis=1), ohct[pl.ds(mo(n * size, size), size), :]
            )

        acc = lax.fori_loop(0, CHUNKS // U_PUT, scatter_cells, jnp.zeros((48, 128), F32))
        sums = [acc[n * 16 : n * 16 + 8] + acc[n * 16 + 8 : n * 16 + 16] for n in range(3)]
        keep = same if h % 2 == 1 else [exist[n] - same[n] for n in range(3)]
        if h == POWER:
            scale = square_end(h - 1)
            for n in range(3):
                fp[group, :, n * 128 : n * 128 + 128] = sums[n] * keep[n] * scale
            return None
        bs[h, 0] = sums[0]
        bs[h, 1] = sums[2]
        swap = [
            rcopy(bs.at[h, 0], rbn.at[h], b_s.at[h, 0], b_r.at[h, 0], (prv, group)),
            rcopy(bs.at[h, 1], rbp.at[h], b_s.at[h, 1], b_r.at[h, 1], (nxt, group)),
        ]
        for cpy in swap:
            cpy.start()
        scale = square_end(h - 1) if h > 0 else None
        for cpy in swap:
            cpy.wait()
        sums[0] = sums[0] + rbp[h] * has_prev
        sums[2] = sums[2] + rbn[h] * has_next
        out = []
        for n in range(3):
            v = sums[n] * keep[n]
            out.append(v if scale is None else v * scale)
        return out

    for h in range(ROUNDS):
        q = hessian(h, q)
        if h < POWER:
            square_start(h, q)
        if h == 0:
            out_ref[0:8, :] = pltpu.roll(jnp.concatenate(q, axis=1), 384 - RIM, 1)[:, :256]
    def final(kind, d, source):
        other = lax.rem(group + d, GROUPS)
        device, landing, span = (
            ((prv, other), fpn, pl.ds(0, 128)),
            ((nxt, other), fpp, pl.ds(256, 128)),
            ((tile, other), fp, pl.ds(0, 384)),
        )[kind]
        return rcopy(
            fp.at[group, :, span], landing.at[source], g_s.at[kind, d], g_r.at[kind, source], device
        )

    order = [(kind, d) for kind in range(3) for d in range(GROUPS) if kind < 2 or d > 0]
    for kind, d in order:
        final(kind, d, group).start()
    for kind, d in order:
        final(kind, d, lax.rem(group + d, GROUPS)).wait_recv()
    for kind, d in order:
        final(kind, d, group).wait_send()

    def window(g):
        return jnp.concatenate(
            [
                fp[g, :, 0:128] + fpp[g] * has_prev,
                fp[g, :, 128:256],
                fp[g, :, 256:384] + fpn[g] * has_next,
            ],
            axis=1,
        )

    mine = pltpu.roll(window(group), 384 - RIM, 1)[:, :256]
    out_ref[8:16, :] = mine
    every = jnp.concatenate([window(g) for g in range(GROUPS)], axis=0)
    every = pltpu.roll(every, 384 - RIM, 1)[:, :256]
    outer = jnp.concatenate([every * mine[i : i + 1, :] for i in range(8)], axis=0)
    hi, lo = split(outer)
    member = one(lax.broadcasted_iota(I32, (64, 256), 0) == cl_ref[...])
    grams = dot(member, hi.astype(BF16), NT) + dot(member, lo.astype(BF16), NT)
    for yx in range(YXS):
        rows = grams[yx * 8 : yx * 8 + 8]
        gk[yx] = jnp.concatenate([rows[:, :128], rows[:, 128:]], axis=0).astype(BF16)

    for d in range(1, YXS):
        yx = yx_peer(d)
        rcopy(
            gk.at[yx], ka.at[my_yx], s_s.at[d], k_r.at[0, my_yx],
            yx_device(yx),
        ).start()
    for d in range(1, YXS):
        yx = yx_peer(d)
        got = rcopy(ka.at[yx], ka.at[yx], s_s.at[d], k_r.at[0, yx], yx_device(yx))
        got.wait_recv()
        got.wait_send()
    ka[my_yx] = gk[my_yx]
    total = ka[0].astype(F32)
    for yx in range(1, YXS):
        total = total + ka[yx].astype(F32)
    kb[my_z] = total.astype(BF16)
    for d in range(1, ZS):
        rcopy(
            kb.at[my_z], kb.at[my_z], s_s.at[d], k_r.at[1, my_z], z_device(z_peer(d))
        ).start()
    for d in range(1, ZS):
        z = z_peer(d)
        got = rcopy(kb.at[z], kb.at[z], s_s.at[d], k_r.at[1, z], z_device(z))
        got.wait_recv()
        got.wait_send()
    total = kb[0].astype(F32)
    for z in range(1, ZS):
        total = total + kb[z].astype(F32)
    kc[my_yx] = total
    for d in range(1, YXS):
        rcopy(
            kc.at[my_yx], kc.at[my_yx], s_s.at[d], k_r.at[2, my_yx], yx_device(yx_peer(d))
        ).start()
    for d in range(1, YXS):
        yx = yx_peer(d)
        got = rcopy(kc.at[yx], kc.at[yx], s_s.at[d], k_r.at[2, yx], yx_device(yx))
        got.wait_recv()
        got.wait_send()
    for yx in range(YXS):
        gram_ref[yx * 8 : yx * 8 + 8, 0:128] = kc[yx, 0:8]
        gram_ref[yx * 8 : yx * 8 + 8, 128:256] = kc[yx, 8:16]


def finish(cells_ref, sums_ref, samp_ref, refd_ref, gram_ref):
    samp_ref[...] = cells_ref[0:8, :]
    refd_ref[...] = cells_ref[8:16, :]
    for j in range(2):
        gram_ref[j * 128 : j * 128 + 128, :] = jnp.transpose(sums_ref[:, j * 128 : j * 128 + 128])


def shards(
    blocks, connectivity, basal_map, friction, elem_counts, obs_weight, sign_bits, cluster_ids
):
    vmem = pl.BlockSpec(memory_space=pltpu.VMEM)
    here = pl.BlockSpec(memory_space=pl.ANY)
    dma = pltpu.SemaphoreType.DMA
    cells, gram = pl.pallas_call(
        kernel,
        out_shape=(
            jax.ShapeDtypeStruct((16, 256), F32),
            jax.ShapeDtypeStruct((64, 256), F32),
        ),
        in_specs=[here] * 4 + [pl.BlockSpec(memory_space=pltpu.SMEM)] + [here] * 3,
        out_specs=(vmem, vmem),
        scratch_shapes=[
            pltpu.VMEM((ELEMS, 64), I32),
            pltpu.VMEM((ELEMS, 64), I32),
            pltpu.VMEM((3, ELEMS, 64), F32),
            pltpu.VMEM((3, 4096), F32),
            pltpu.VMEM((8, 256), I32),
            pltpu.VMEM((1, 256), I32),
            pltpu.VMEM((ELEMS, 128), I32),
            pltpu.VMEM((16, 384), F32),
            pltpu.VMEM((ELEMS, DOF, DOF), BF16),
            pltpu.VMEM((256, 4096), BF16),
            pltpu.VMEM((4096, 256), BF16),
            pltpu.VMEM((128, 4096), BF16),
            pltpu.VMEM((4096, 128), BF16),
            pltpu.VMEM((128, 256), I32),
            pltpu.VMEM((128, 256), I32),
            pltpu.VMEM((256, 512), F32),
            pltpu.VMEM((128, 512), BF16),
            pltpu.VMEM((512, 128), BF16),
            pltpu.VMEM((384, 512), BF16),
            pltpu.VMEM((512, 384), BF16),
            pltpu.VMEM((256, 128), BF16),
            pltpu.VMEM((256, 128), BF16),
            pltpu.VMEM((256, 512), BF16),
            pltpu.VMEM((256, 512), BF16),
            pltpu.VMEM((256, 384), F32),
            pltpu.VMEM((96, 256), F32),
            pltpu.VMEM((336, 256), F32),
            pltpu.VMEM((96, 256), BF16),
            pltpu.VMEM((336, 256), BF16),
            pltpu.VMEM((256, 384), F32),
            pltpu.VMEM((256, 384), BF16),
            pltpu.VMEM((256, 512), BF16),
            pltpu.VMEM((256, 512), BF16),
            pltpu.VMEM((256, 512), BF16),
            pltpu.VMEM((256, 128), F32),
            pltpu.VMEM((3, 512), F32),
            pltpu.VMEM((16, 128), F32),
            pltpu.VMEM((16, 128), F32),
            pltpu.VMEM((ROUNDS, 96, 256), BF16),
            pltpu.VMEM((ROUNDS, 48, 256), BF16),
            pltpu.VMEM((ROUNDS, 48, 256), BF16),
            pltpu.VMEM((ROUNDS, 2, 8, 128), F32),
            pltpu.VMEM((ROUNDS, 8, 128), F32),
            pltpu.VMEM((ROUNDS, 8, 128), F32),
            pltpu.VMEM((POWER, ZS, 8, 128), F32),
            pltpu.VMEM((POWER, YXS, 8, 128), F32),
            pltpu.VMEM((GROUPS, 8, 384), F32),
            pltpu.VMEM((GROUPS, 8, 128), F32),
            pltpu.VMEM((GROUPS, 8, 128), F32),
            pltpu.VMEM((YXS, 16, 128), BF16),
            pltpu.VMEM((YXS, 16, 128), BF16),
            pltpu.VMEM((ZS, 16, 128), BF16),
            pltpu.VMEM((YXS, 16, 128), F32),
            dma,
            dma((6,)),
            dma((3,)),
            dma((3,)),
            dma((ROUNDS, 2)),
            dma((ROUNDS, 2)),
            dma((ROUNDS, 2)),
            dma((ROUNDS, 2)),
            dma((8,)),
            dma((POWER, 2, 8)),
            dma((3, GROUPS)),
            dma((3, GROUPS)),
            dma((3, 8)),
        ],
        compiler_params=pltpu.CompilerParams(
            collective_id=0, has_side_effects=True, vmem_limit_bytes=63 * 1024 * 1024
        ),
    )(
        blocks, connectivity, basal_map, friction.transpose(2, 0, 1), elem_counts,
        obs_weight.T, sign_bits.T, cluster_ids[None, :],
    )
    samp, refd, gram = pl.pallas_call(
        finish,
        out_shape=(
            jax.ShapeDtypeStruct((8, 256), F32),
            jax.ShapeDtypeStruct((8, 256), F32),
            jax.ShapeDtypeStruct((256, 64), F32),
        ),
        in_specs=[vmem, vmem],
        out_specs=(vmem, vmem, vmem),
    )(cells, gram)
    return samp.T, refd.T, gram.reshape(8, 32, 64).transpose(2, 0, 1)


def solution(mesh):
    in_specs = (
        P("tiles", None, None),
        P("tiles", None),
        P("tiles", None),
        P("tiles", None, None),
        P("tiles"),
        P("tiles", None),
        P("tiles", "probes"),
        P("tiles"),
    )
    out_specs = (P("tiles", "probes"), P("tiles", "probes"), P(None, "probes", None))
    return jax.shard_map(shards, mesh=mesh, in_specs=in_specs, out_specs=out_specs, check_vma=False)
```

```python
import functools

import jax
import jax.numpy as jnp
from jax import lax
from jax.experimental import pallas as pl
from jax.experimental.pallas import tpu as pltpu
from jax.sharding import PartitionSpec as P

F32 = jnp.float32
BF16 = jnp.bfloat16
I32 = jnp.int32
POWER = 2
ROUNDS = POWER + 1
RIM = 64
ELEMS = 64
DOF = 192
PAIRS = 32
CHUNKS = 16
U_IN = 16
U_PROD = 16
U_INNER = 8
U_GET = 4
U_PUT = 16
ZS = 8
YXS = 8
GROUPS = 4
EDGE = (0, 1, 16, 17)
INNER = tuple(range(2, 16))
NT = (((1,), (1,)), ((), ()))
NN = (((1,), (0,)), ((), ()))
MESH = pl.DeviceIdType.MESH


def mo(x, n):
    return x if isinstance(x, int) else pl.multiple_of(x, n)


def each(unroll, body, steps=CHUNKS):
    if unroll == steps:
        for j in range(steps):
            body(j)
        return

    @pl.loop(0, steps // unroll)
    def _(n):
        for j in range(unroll):
            body(n * unroll + j)


def split(x):
    hi = x.astype(BF16).astype(F32)
    return hi, x - hi


def dot(a, b, dims=NN):
    return lax.dot_general(a, b, dims, preferred_element_type=F32)


def kernel(
    blk_hbm, conn_hbm, cell_hbm, fr_hbm, count_ref, w_hbm, sign_hbm, cl_hbm,
    out_ref, gram_ref,
    conn, cell, fr3, w3, sign, cl_ref, idx_ref, qs_ref,
    blk, ohn, ohnt, ohc, ohct, an8, ac8, fr8, rep, sel, pm, pmt,
    gh, gl, xin, fw, fc, acce, acci, te, ti, ad1, ad, ain, yh, yl, pt,
    wn, qsp, qsn, esend, renext, reprev, bs, rbn, rbp, pa, pb, fp, fpn, fpp, gk, ka, kb, kc,
    blk_sem, in_sem, i_s, i_r, e_s, e_r, b_s, b_r, s_s, p_r, g_s, g_r, k_r,
):
    tile = lax.axis_index("tiles")
    group = lax.axis_index("probes")
    tiles = lax.axis_size("tiles")
    nxt = lax.rem(tile + 1, tiles)
    prv = lax.rem(tile + tiles - 1, tiles)
    my_z = lax.rem(tile, ZS)
    my_yx = lax.div(tile, ZS)
    has_prev = jnp.where(tile > 0, 1.0, 0.0).astype(F32)
    has_next = jnp.where(tile < tiles - 1, 1.0, 0.0).astype(F32)

    def z_peer(d):
        return lax.rem(my_z + d, ZS)

    def yx_peer(d):
        return lax.rem(my_yx + d, YXS)

    def z_device(z):
        return (my_yx * ZS + z, group)

    def yx_device(yx):
        return (yx * ZS + my_z, group)

    def rcopy(src, dst, ss, rs, dev):
        return pltpu.make_async_remote_copy(
            src_ref=src, dst_ref=dst, send_sem=ss, recv_sem=rs, device_id=dev, device_id_type=MESH
        )

    small = [
        pltpu.make_async_copy(src, dst, in_sem.at[n])
        for n, (src, dst) in enumerate(
            [(sign_hbm, sign), (cl_hbm, cl_ref), (w_hbm, w3), (conn_hbm, conn), (cell_hbm, cell), (fr_hbm, fr3)]
        )
    ]
    for cpy in small:
        cpy.start()
    load = pltpu.make_async_copy(blk_hbm, blk, blk_sem)
    load.start()

    barrier = pltpu.get_barrier_semaphore()

    def greet(dev):
        pl.semaphore_signal(barrier, inc=1, device_id=dev, device_id_type=MESH)

    greet((nxt, group))
    greet((prv, group))
    for d in range(1, ZS):
        greet(z_device(z_peer(d)))
    for d in range(1, YXS):
        greet(yx_device(yx_peer(d)))
    for d in range(1, GROUPS):
        other = lax.rem(group + d, GROUPS)
        greet((tile, other))
        greet((nxt, other))
        greet((prv, other))

    def one(cond):
        return jnp.where(cond, 1.0, 0.0).astype(BF16)

    def pair_col(lane):
        half = lane >> 8
        j = lane & 255
        k = (j * 171) >> 9
        return half, k, j - 3 * k, j < DOF

    r = lax.broadcasted_iota(I32, (128, 512), 0)
    half, k, c, ok = pair_col(lax.broadcasted_iota(I32, (128, 512), 1))
    rep[...] = one((r == half * 64 + k) & ok)
    half, k, c, ok = pair_col(lax.broadcasted_iota(I32, (512, 128), 0))
    r = lax.broadcasted_iota(I32, (512, 128), 1)
    sel[...] = one((r == half * 64 + k) & ok)
    r = lax.broadcasted_iota(I32, (384, 512), 0)
    half, k, c, ok = pair_col(lax.broadcasted_iota(I32, (384, 512), 1))
    pm[...] = one((r == c * 128 + half * 64 + k) & ok)
    half, k, c, ok = pair_col(lax.broadcasted_iota(I32, (512, 384), 0))
    r = lax.broadcasted_iota(I32, (512, 384), 1)
    pmt[...] = one((r == c * 128 + half * 64 + k) & ok)

    fw[...] = jnp.zeros(fw.shape, BF16)
    yh[...] = jnp.zeros(yh.shape, BF16)
    yl[...] = jnp.zeros(yl.shape, BF16)

    for cpy in small:
        cpy.wait()

    same_own = (cl_ref[...] & 1) == (lax.broadcasted_iota(I32, (8, 256), 0) & 1)
    start = jnp.where(same_own, (2 * sign[...] - 1).astype(F32), 0.0)
    both = jnp.concatenate([start, jnp.where(same_own, 1.0, 0.0).astype(F32)], axis=0)
    qs_ref[...] = pltpu.roll(
        jnp.concatenate([both, jnp.zeros((16, 128), F32)], axis=1), RIM, 1
    )
    first = [
        rcopy(qs_ref.at[:, pl.ds(256, 128)], qsp, i_s.at[0], i_r.at[0], (nxt, group)),
        rcopy(qs_ref.at[:, pl.ds(0, 128)], qsn, i_s.at[1], i_r.at[1], (prv, group)),
        rcopy(w3.at[:, pl.ds(0, 512)], wn, i_s.at[2], i_r.at[2], (prv, group)),
    ]
    pl.semaphore_wait(barrier, 2 + ZS - 1 + YXS - 1 + 3 * (GROUPS - 1))
    for cpy in first:
        cpy.start()

    idx_ref[0:PAIRS, :] = jnp.concatenate([conn[0:PAIRS, :], conn[PAIRS:ELEMS, :]], axis=1)
    idx_ref[PAIRS:ELEMS, :] = jnp.concatenate([cell[0:PAIRS, :], cell[PAIRS:ELEMS, :]], axis=1)
    element = lax.broadcasted_iota(I32, (PAIRS, 128), 0) + jnp.where(
        lax.broadcasted_iota(I32, (PAIRS, 128), 1) < 64, 0, PAIRS
    )
    live = element < count_ref[0]
    wide = []
    for c in range(3):
        f = jnp.concatenate([fr3[c, 0:PAIRS, :], fr3[c, PAIRS:ELEMS, :]], axis=1)
        wide.append(jnp.where(live, f, 0.0))
    wide = jnp.concatenate(wide, axis=1)
    hi, rest = split(wide)
    mid, lo = split(rest)
    third = dot(jnp.concatenate([hi, mid, lo], axis=0).astype(BF16), pm[...])
    fr = third[0:PAIRS] + third[PAIRS : 2 * PAIRS] + third[2 * PAIRS :]
    for i in range(PAIRS):
        rows = slice(i * 8, i * 8 + 8)
        fr8[rows, :] = jnp.broadcast_to(fr[i : i + 1, :], (8, 512))
    for i in range(CHUNKS):
        rows = slice(i * 8, i * 8 + 8)
        for j in range(2):
            lanes = slice(j * 128, j * 128 + 128)
            n = 2 * i + j
            an8[rows, lanes] = jnp.broadcast_to(idx_ref[n : n + 1, :] >> 8, (8, 128))
            ac8[rows, lanes] = jnp.broadcast_to(idx_ref[PAIRS + n : PAIRS + n + 1, :] >> 7, (8, 128))

    low = jnp.where(
        lax.broadcasted_iota(I32, (64, 128), 0) < PAIRS, idx_ref[...] & 255, idx_ref[...] & 127
    ).astype(F32)
    cols = jnp.transpose(jnp.concatenate([low, jnp.zeros((64, 128), F32)], axis=0))
    lane_n = lax.broadcasted_iota(I32, (128, 256), 1).astype(F32)
    lane_c = lax.broadcasted_iota(I32, (128, 128), 1).astype(F32)
    sub_n = lax.broadcasted_iota(I32, (256, 128), 0)
    sub_c = lax.broadcasted_iota(I32, (128, 128), 0)
    for i in range(PAIRS):
        span = slice(i * 128, i * 128 + 128)
        ohn[:, span] = one(sub_n == (idx_ref[i : i + 1, :] & 255))
        ohc[:, span] = one(sub_c == (idx_ref[PAIRS + i : PAIRS + i + 1, :] & 127))
        ohnt[span, :] = one(lane_n == cols[:, i : i + 1])
        ohct[span, :] = one(lane_c == cols[:, PAIRS + i : PAIRS + i + 1])

    for cpy in first:
        cpy.wait()
    load.wait()

    lane = lax.broadcasted_iota(I32, (8, 128), 1)
    upper = jnp.where(lane >= RIM, 1.0, 0.0).astype(F32)
    own = [upper, jnp.ones((8, 128), F32), 1.0 - upper]
    exist = [
        upper + (1.0 - upper) * has_prev,
        jnp.ones((8, 128), F32),
        (1.0 - upper) + upper * has_next,
    ]
    q = [
        qs_ref[0:8, 0:128] + qsp[0:8, :] * has_prev,
        qs_ref[0:8, 128:256],
        qs_ref[0:8, 256:384] + qsn[0:8, :] * has_next,
    ]
    same = [
        qs_ref[8:16, 0:128] + qsp[8:16, :] * has_prev,
        qs_ref[8:16, 128:256],
        qs_ref[8:16, 256:384] + qsn[8:16, :] * has_next,
    ]

    def square_start(i, cur):
        total = cur[0] * cur[0] * own[0] + cur[1] * cur[1] + cur[2] * cur[2] * own[2]
        pa[i, my_z] = total
        for d in range(1, ZS):
            rcopy(
                pa.at[i, my_z], pa.at[i, my_z], s_s.at[d], p_r.at[i, 0, my_z],
                z_device(z_peer(d)),
            ).start()

    def square_mid(i):
        for d in range(1, ZS):
            z = z_peer(d)
            got = rcopy(pa.at[i, z], pa.at[i, z], s_s.at[d], p_r.at[i, 0, z], z_device(z))
            got.wait_recv()
            got.wait_send()
        total = pa[i, 0]
        for z in range(1, ZS):
            total = total + pa[i, z]
        pb[i, my_yx] = total
        for d in range(1, YXS):
            rcopy(
                pb.at[i, my_yx], pb.at[i, my_yx], s_s.at[d], p_r.at[i, 1, my_yx],
                yx_device(yx_peer(d)),
            ).start()

    def square_end(i):
        for d in range(1, YXS):
            yx = yx_peer(d)
            got = rcopy(
                pb.at[i, yx], pb.at[i, yx], s_s.at[d], p_r.at[i, 1, yx], yx_device(yx)
            )
            got.wait_recv()
            got.wait_send()
        total = pb[i, 0]
        for yx in range(1, YXS):
            total = total + pb[i, yx]
        mean = jnp.sum(total, axis=1, keepdims=True) / (256 * tiles)
        return 1.0 / jnp.sqrt(mean + 1e-06)

    def weight(ref, n):
        c = n % 3
        return ref[c : c + 1, n // 3 * 256 : n // 3 * 256 + 256]

    row16 = lax.broadcasted_iota(I32, (16, DOF), 0) < 8

    def scatter_nodes(n, unroll, levels):
        spreads = []
        for j in range(unroll):
            m = n * unroll + j
            r0 = mo(m * 16, 16)
            parts = []
            for c in range(3):
                span = slice(c * 128, c * 128 + 128)
                parts.append(
                    jnp.concatenate([fc[pl.ds(r0, 8), span], fc[pl.ds(r0 + 8, 8), span]], axis=1)
                )
            a = an8[pl.ds(mo(m * 8, 8), 8), :]
            spread = jnp.concatenate(
                [jnp.where(a == lv, parts[c], 0.0) for lv in levels for c in range(3)], axis=0
            )
            spreads.append(spread.astype(BF16))
        size = unroll * 256
        return dot(jnp.concatenate(spreads, axis=1), ohnt[pl.ds(mo(n * size, size), size), :])

    def gather_nodes(m, table, levels, base):
        got = dot(table[...], ohn[:, pl.ds(mo(m * 512, 512), 512)])
        r = mo(m * 16, 16)
        a = jnp.concatenate([an8[pl.ds(r, 8), :], an8[pl.ds(r + 8, 8), :]], axis=1)
        out = list(base)
        for n, lv in enumerate(levels):
            hit = a == lv
            for c in range(3):
                row = (n * 3 + c) * 8
                out[c] = jnp.where(hit, got[row : row + 8], out[c])
        return out

    def hessian(h, q):
        terms = 2 if h > 0 else 1
        parts = []
        for b in q:
            parts += list(split(b))[:terms]
        cells = jnp.concatenate(parts, axis=0).astype(BF16)

        def gather_cells(m):
            got = dot(cells, ohc[:, pl.ds(mo(m * 256, 256), 256)])
            a = ac8[pl.ds(mo(m * 8, 8), 8), :]
            level = []
            for n in range(3):
                r = n * 8 * terms
                level.append(got[r : r + 8] + got[r + 8 : r + 16] if h > 0 else got[r : r + 8])
            g = jnp.where(a == 0, level[0], jnp.where(a == 1, level[1], level[2]))
            hi, lo = split(g)
            rows = pl.ds(mo(m * 16, 16), 16)
            gh[rows, :] = jnp.concatenate([hi[:, :128], hi[:, 128:]], axis=0).astype(BF16)
            if h > 0:
                gl[rows, :] = jnp.concatenate([lo[:, :128], lo[:, 128:]], axis=0).astype(BF16)

        each(U_IN, gather_cells)

        for i in range(4):
            rows = slice(i * 64, i * 64 + 64)
            wide = dot(gh[rows, :], rep[...])
            if h > 0:
                wide = wide + dot(gl[rows, :], rep[...])
            xin[rows, :] = (wide * fr8[rows, :]).astype(BF16)

        def forward(m):
            rows = pl.ds(mo(m * 16, 16), 16)
            for half in range(2):
                span = slice(half * 256, half * 256 + DOF)
                x = xin[rows, span]
                o0 = dot(x, blk[2 * m + PAIRS * half], NT)
                o1 = dot(x, blk[2 * m + 1 + PAIRS * half], NT)
                fw[rows, span] = jnp.where(row16, o0, o1).astype(BF16)

        each(U_PROD, forward)

        for i in range(4):
            rows = slice(i * 64, i * 64 + 64)
            fc[rows, :] = dot(fw[rows, :], pmt[...])

        acci[...] = jnp.zeros(acci.shape, F32)

        edges = scatter_nodes(0, CHUNKS, EDGE)
        acce[...] = edges
        esend[h] = edges.astype(BF16)
        swap = [
            rcopy(esend.at[h, pl.ds(0, 48), :], renext.at[h], e_s.at[h, 0], e_r.at[h, 0], (prv, group)),
            rcopy(esend.at[h, pl.ds(48, 48), :], reprev.at[h], e_s.at[h, 1], e_r.at[h, 1], (nxt, group)),
        ]
        for cpy in swap:
            cpy.start()

        @pl.loop(0, CHUNKS // U_INNER)
        def _(n):
            acci[...] += scatter_nodes(n, U_INNER, INNER)

        if h > 0:
            square_mid(h - 1)

        for i in range(21):
            pair = []
            for j in range(2):
                n = 2 * i + j
                pair.append(acci[n * 8 : n * 8 + 8, :] * weight(w3, 6 + n))
            ti[i * 16 : i * 16 + 16, :] = jnp.concatenate(pair, axis=0).astype(BF16)

        def gather_inner(m):
            zero = jnp.zeros((8, 512), F32)
            out = gather_nodes(m, ti, INNER, [zero] * 3)
            r0 = mo(m * 32, 32)
            for c in range(3):
                span = slice(c * 128, c * 128 + 128)
                for j in range(4):
                    ad1[pl.ds(r0 + 8 * j, 8), span] = out[c][:, j * 128 : j * 128 + 128]

        each(U_GET, gather_inner, CHUNKS // 2)

        for cpy in swap:
            cpy.wait()
        for i in range(6):
            if i < 3:
                theirs = reprev[h, i * 16 : i * 16 + 16, :].astype(F32) * has_prev
            else:
                theirs = renext[h, i * 16 - 48 : i * 16 - 32, :].astype(F32)
            total = acce[i * 16 : i * 16 + 16, :] + theirs
            pair = []
            for j in range(2):
                n = 2 * i + j
                scale = weight(w3, n) if n < 6 else weight(wn, n - 6) * has_next
                pair.append(total[j * 8 : j * 8 + 8] * scale)
            te[i * 16 : i * 16 + 16, :] = jnp.concatenate(pair, axis=0).astype(BF16)

        def gather_edge(m):
            r0 = mo(m * 32, 32)
            base = []
            for c in range(3):
                span = slice(c * 128, c * 128 + 128)
                base.append(
                    jnp.concatenate([ad1[pl.ds(r0 + 8 * j, 8), span] for j in range(4)], axis=1)
                )
            out = gather_nodes(m, te, EDGE, base)
            for c in range(3):
                span = slice(c * 128, c * 128 + 128)
                ad[pl.ds(r0, 32), span] = jnp.concatenate(
                    [out[c][:, j * 128 : j * 128 + 128] for j in range(4)], axis=0
                ).astype(BF16)

        each(CHUNKS // 2, gather_edge, CHUNKS // 2)

        for i in range(4):
            rows = slice(i * 64, i * 64 + 64)
            ain[rows, :] = dot(ad[rows, :], pm[...]).astype(BF16)

        def adjoint(m):
            rows = pl.ds(mo(m * 16, 16), 16)
            for half in range(2):
                span = slice(half * 256, half * 256 + DOF)
                x = ain[rows, span]
                o0 = dot(x, blk[2 * m + PAIRS * half])
                o1 = dot(x, blk[2 * m + 1 + PAIRS * half])
                hi, lo = split(jnp.where(row16, o0, o1) * fr8[rows, span])
                yh[rows, span] = hi.astype(BF16)
                yl[rows, span] = lo.astype(BF16)

        each(U_PROD, adjoint)

        for i in range(4):
            rows = slice(i * 64, i * 64 + 64)
            pt[rows, :] = dot(yh[rows, :], sel[...]) + dot(yl[rows, :], sel[...])

        def scatter_cells(n, acc):
            spreads = []
            for j in range(U_PUT):
                m = n * U_PUT + j
                r0 = mo(m * 16, 16)
                v = jnp.concatenate([pt[pl.ds(r0, 8), :], pt[pl.ds(r0 + 8, 8), :]], axis=1)
                a = ac8[pl.ds(mo(m * 8, 8), 8), :]
                spread = jnp.concatenate(
                    [jnp.where(a == lv, s, 0.0) for lv in range(3) for s in split(v)], axis=0
                )
                spreads.append(spread.astype(BF16))
            size = U_PUT * 256
            return acc + dot(
                jnp.concatenate(spreads, axis=1), ohct[pl.ds(mo(n * size, size), size), :]
            )

        acc = lax.fori_loop(0, CHUNKS // U_PUT, scatter_cells, jnp.zeros((48, 128), F32))
        sums = [acc[n * 16 : n * 16 + 8] + acc[n * 16 + 8 : n * 16 + 16] for n in range(3)]
        keep = same if h % 2 == 1 else [exist[n] - same[n] for n in range(3)]
        if h == POWER:
            scale = square_end(h - 1)
            for n in range(3):
                fp[group, :, n * 128 : n * 128 + 128] = sums[n] * keep[n] * scale
            return None
        bs[h, 0] = sums[0]
        bs[h, 1] = sums[2]
        swap = [
            rcopy(bs.at[h, 0], rbn.at[h], b_s.at[h, 0], b_r.at[h, 0], (prv, group)),
            rcopy(bs.at[h, 1], rbp.at[h], b_s.at[h, 1], b_r.at[h, 1], (nxt, group)),
        ]
        for cpy in swap:
            cpy.start()
        scale = square_end(h - 1) if h > 0 else None
        for cpy in swap:
            cpy.wait()
        sums[0] = sums[0] + rbp[h] * has_prev
        sums[2] = sums[2] + rbn[h] * has_next
        out = []
        for n in range(3):
            v = sums[n] * keep[n]
            out.append(v if scale is None else v * scale)
        return out

    for h in range(ROUNDS):
        q = hessian(h, q)
        if h < POWER:
            square_start(h, q)
        if h == 0:
            out_ref[0:8, :] = pltpu.roll(jnp.concatenate(q, axis=1), 384 - RIM, 1)[:, :256]
    def final(kind, d, source):
        other = lax.rem(group + d, GROUPS)
        device, landing, span = (
            ((prv, other), fpn, pl.ds(0, 128)),
            ((nxt, other), fpp, pl.ds(256, 128)),
            ((tile, other), fp, pl.ds(0, 384)),
        )[kind]
        return rcopy(
            fp.at[group, :, span], landing.at[source], g_s.at[kind, d], g_r.at[kind, source], device
        )

    order = [(kind, d) for kind in range(3) for d in range(GROUPS) if kind < 2 or d > 0]
    for kind, d in order:
        final(kind, d, group).start()
    for kind, d in order:
        final(kind, d, lax.rem(group + d, GROUPS)).wait_recv()
    for kind, d in order:
        final(kind, d, group).wait_send()

    def window(g):
        return jnp.concatenate(
            [
                fp[g, :, 0:128] + fpp[g] * has_prev,
                fp[g, :, 128:256],
                fp[g, :, 256:384] + fpn[g] * has_next,
            ],
            axis=1,
        )

    mine = pltpu.roll(window(group), 384 - RIM, 1)[:, :256]
    out_ref[8:16, :] = mine
    every = jnp.concatenate([window(g) for g in range(GROUPS)], axis=0)
    every = pltpu.roll(every, 384 - RIM, 1)[:, :256]
    outer = jnp.concatenate([every * mine[i : i + 1, :] for i in range(8)], axis=0)
    hi, lo = split(outer)
    member = one(lax.broadcasted_iota(I32, (64, 256), 0) == cl_ref[...])
    grams = dot(member, hi.astype(BF16), NT) + dot(member, lo.astype(BF16), NT)
    for yx in range(YXS):
        rows = grams[yx * 8 : yx * 8 + 8]
        gk[yx] = jnp.concatenate([rows[:, :128], rows[:, 128:]], axis=0).astype(BF16)

    for d in range(1, YXS):
        yx = yx_peer(d)
        rcopy(
            gk.at[yx], ka.at[my_yx], s_s.at[d], k_r.at[0, my_yx],
            yx_device(yx),
        ).start()
    for d in range(1, YXS):
        yx = yx_peer(d)
        got = rcopy(ka.at[yx], ka.at[yx], s_s.at[d], k_r.at[0, yx], yx_device(yx))
        got.wait_recv()
        got.wait_send()
    ka[my_yx] = gk[my_yx]
    total = ka[0].astype(F32)
    for yx in range(1, YXS):
        total = total + ka[yx].astype(F32)
    kb[my_z] = total.astype(BF16)
    for d in range(1, ZS):
        rcopy(
            kb.at[my_z], kb.at[my_z], s_s.at[d], k_r.at[1, my_z], z_device(z_peer(d))
        ).start()
    for d in range(1, ZS):
        z = z_peer(d)
        got = rcopy(kb.at[z], kb.at[z], s_s.at[d], k_r.at[1, z], z_device(z))
        got.wait_recv()
        got.wait_send()
    total = kb[0].astype(F32)
    for z in range(1, ZS):
        total = total + kb[z].astype(F32)
    kc[my_yx] = total
    for d in range(1, YXS):
        rcopy(
            kc.at[my_yx], kc.at[my_yx], s_s.at[d], k_r.at[2, my_yx], yx_device(yx_peer(d))
        ).start()
    for d in range(1, YXS):
        yx = yx_peer(d)
        got = rcopy(kc.at[yx], kc.at[yx], s_s.at[d], k_r.at[2, yx], yx_device(yx))
        got.wait_recv()
        got.wait_send()
    for yx in range(YXS):
        gram_ref[yx * 8 : yx * 8 + 8, 0:128] = kc[yx, 0:8]
        gram_ref[yx * 8 : yx * 8 + 8, 128:256] = kc[yx, 8:16]


def finish(cells_ref, sums_ref, samp_ref, refd_ref, gram_ref):
    samp_ref[...] = cells_ref[0:8, :]
    refd_ref[...] = cells_ref[8:16, :]
    for j in range(2):
        gram_ref[j * 128 : j * 128 + 128, :] = jnp.transpose(sums_ref[:, j * 128 : j * 128 + 128])


def shards(
    blocks, connectivity, basal_map, friction, elem_counts, obs_weight, sign_bits, cluster_ids
):
    vmem = pl.BlockSpec(memory_space=pltpu.VMEM)
    here = pl.BlockSpec(memory_space=pl.ANY)
    dma = pltpu.SemaphoreType.DMA
    cells, gram = pl.pallas_call(
        kernel,
        out_shape=(
            jax.ShapeDtypeStruct((16, 256), F32),
            jax.ShapeDtypeStruct((64, 256), F32),
        ),
        in_specs=[here] * 4 + [pl.BlockSpec(memory_space=pltpu.SMEM)] + [here] * 3,
        out_specs=(vmem, vmem),
        scratch_shapes=[
            pltpu.VMEM((ELEMS, 64), I32),
            pltpu.VMEM((ELEMS, 64), I32),
            pltpu.VMEM((3, ELEMS, 64), F32),
            pltpu.VMEM((3, 4096), F32),
            pltpu.VMEM((8, 256), I32),
            pltpu.VMEM((1, 256), I32),
            pltpu.VMEM((ELEMS, 128), I32),
            pltpu.VMEM((16, 384), F32),
            pltpu.VMEM((ELEMS, DOF, DOF), BF16),
            pltpu.VMEM((256, 4096), BF16),
            pltpu.VMEM((4096, 256), BF16),
            pltpu.VMEM((128, 4096), BF16),
            pltpu.VMEM((4096, 128), BF16),
            pltpu.VMEM((128, 256), I32),
            pltpu.VMEM((128, 256), I32),
            pltpu.VMEM((256, 512), F32),
            pltpu.VMEM((128, 512), BF16),
            pltpu.VMEM((512, 128), BF16),
            pltpu.VMEM((384, 512), BF16),
            pltpu.VMEM((512, 384), BF16),
            pltpu.VMEM((256, 128), BF16),
            pltpu.VMEM((256, 128), BF16),
            pltpu.VMEM((256, 512), BF16),
            pltpu.VMEM((256, 512), BF16),
            pltpu.VMEM((256, 384), F32),
            pltpu.VMEM((96, 256), F32),
            pltpu.VMEM((336, 256), F32),
            pltpu.VMEM((96, 256), BF16),
            pltpu.VMEM((336, 256), BF16),
            pltpu.VMEM((256, 384), F32),
            pltpu.VMEM((256, 384), BF16),
            pltpu.VMEM((256, 512), BF16),
            pltpu.VMEM((256, 512), BF16),
            pltpu.VMEM((256, 512), BF16),
            pltpu.VMEM((256, 128), F32),
            pltpu.VMEM((3, 512), F32),
            pltpu.VMEM((16, 128), F32),
            pltpu.VMEM((16, 128), F32),
            pltpu.VMEM((ROUNDS, 96, 256), BF16),
            pltpu.VMEM((ROUNDS, 48, 256), BF16),
            pltpu.VMEM((ROUNDS, 48, 256), BF16),
            pltpu.VMEM((ROUNDS, 2, 8, 128), F32),
            pltpu.VMEM((ROUNDS, 8, 128), F32),
            pltpu.VMEM((ROUNDS, 8, 128), F32),
            pltpu.VMEM((POWER, ZS, 8, 128), F32),
            pltpu.VMEM((POWER, YXS, 8, 128), F32),
            pltpu.VMEM((GROUPS, 8, 384), F32),
            pltpu.VMEM((GROUPS, 8, 128), F32),
            pltpu.VMEM((GROUPS, 8, 128), F32),
            pltpu.VMEM((YXS, 16, 128), BF16),
            pltpu.VMEM((YXS, 16, 128), BF16),
            pltpu.VMEM((ZS, 16, 128), BF16),
            pltpu.VMEM((YXS, 16, 128), F32),
            dma,
            dma((6,)),
            dma((3,)),
            dma((3,)),
            dma((ROUNDS, 2)),
            dma((ROUNDS, 2)),
            dma((ROUNDS, 2)),
            dma((ROUNDS, 2)),
            dma((8,)),
            dma((POWER, 2, 8)),
            dma((3, GROUPS)),
            dma((3, GROUPS)),
            dma((3, 8)),
        ],
        compiler_params=pltpu.CompilerParams(
            collective_id=0, has_side_effects=True, vmem_limit_bytes=63 * 1024 * 1024
        ),
    )(
        blocks, connectivity, basal_map, friction.transpose(2, 0, 1), elem_counts,
        obs_weight.T, sign_bits.T, cluster_ids[None, :],
    )
    samp, refd, gram = pl.pallas_call(
        finish,
        out_shape=(
            jax.ShapeDtypeStruct((8, 256), F32),
            jax.ShapeDtypeStruct((8, 256), F32),
            jax.ShapeDtypeStruct((256, 64), F32),
        ),
        in_specs=[vmem, vmem],
        out_specs=(vmem, vmem, vmem),
    )(cells, gram)
    return samp.T, refd.T, gram.reshape(8, 32, 64).transpose(2, 0, 1)


def solution(mesh):
    in_specs = (
        P("tiles", None, None),
        P("tiles", None),
        P("tiles", None),
        P("tiles", None, None),
        P("tiles"),
        P("tiles", None),
        P("tiles", "probes"),
        P("tiles"),
    )
    out_specs = (P("tiles", "probes"), P("tiles", "probes"), P(None, "probes", None))
    return jax.shard_map(shards, mesh=mesh, in_specs=in_specs, out_specs=out_specs, check_vma=False)
```

```python
import functools

import jax
import jax.numpy as jnp
from jax import lax
from jax.experimental import pallas as pl
from jax.experimental.pallas import tpu as pltpu
from jax.sharding import PartitionSpec as P

F32 = jnp.float32
BF16 = jnp.bfloat16
I32 = jnp.int32
POWER = 2
ROUNDS = POWER + 1
RIM = 64
ELEMS = 64
DOF = 192
PAIRS = 32
CHUNKS = 16
U_IN = 16
U_PROD = 16
U_INNER = 8
U_GET = 4
U_PUT = 16
ZS = 8
YXS = 8
GROUPS = 4
EDGE = (0, 1, 16, 17)
INNER = tuple(range(2, 16))
NT = (((1,), (1,)), ((), ()))
NN = (((1,), (0,)), ((), ()))
MESH = pl.DeviceIdType.MESH


def mo(x, n):
    return x if isinstance(x, int) else pl.multiple_of(x, n)


def each(unroll, body, steps=CHUNKS):
    if unroll == steps:
        for j in range(steps):
            body(j)
        return

    @pl.loop(0, steps // unroll)
    def _(n):
        for j in range(unroll):
            body(n * unroll + j)


def split(x):
    hi = x.astype(BF16).astype(F32)
    return hi, x - hi


def dot(a, b, dims=NN):
    return lax.dot_general(a, b, dims, preferred_element_type=F32)


def kernel(
    blk_hbm, conn_hbm, cell_hbm, fr_hbm, count_ref, w_hbm, sign_hbm, cl_hbm,
    out_ref, gram_ref,
    conn, cell, fr3, w3, sign, cl_ref, idx_ref, qs_ref,
    blk, ohn, ohnt, ohc, ohct, an8, ac8, fr8, rep, sel, pm, pmt,
    gh, gl, xin, fw, fc, acce, acci, te, ti, ad1, ad, ain, yh, yl, pt,
    wn, qsp, qsn, esend, renext, reprev, bs, rbn, rbp, pa, pb, fp, fpn, fpp, gk, ka, kb, kc, cells_v,
    blk_sem, in_sem, out_sem, i_s, i_r, e_s, e_r, b_s, b_r, s_s, p_r, g_s, g_r, k_r,
):
    tile = lax.axis_index("tiles")
    group = lax.axis_index("probes")
    tiles = lax.axis_size("tiles")
    nxt = lax.rem(tile + 1, tiles)
    prv = lax.rem(tile + tiles - 1, tiles)
    my_z = lax.rem(tile, ZS)
    my_yx = lax.div(tile, ZS)
    has_prev = jnp.where(tile > 0, 1.0, 0.0).astype(F32)
    has_next = jnp.where(tile < tiles - 1, 1.0, 0.0).astype(F32)

    def z_peer(d):
        return lax.rem(my_z + d, ZS)

    def yx_peer(d):
        return lax.rem(my_yx + d, YXS)

    def z_device(z):
        return (my_yx * ZS + z, group)

    def yx_device(yx):
        return (yx * ZS + my_z, group)

    def rcopy(src, dst, ss, rs, dev):
        return pltpu.make_async_remote_copy(
            src_ref=src, dst_ref=dst, send_sem=ss, recv_sem=rs, device_id=dev, device_id_type=MESH
        )

    small = [
        pltpu.make_async_copy(src, dst, in_sem.at[n])
        for n, (src, dst) in enumerate(
            [(sign_hbm, sign), (cl_hbm, cl_ref), (w_hbm, w3), (conn_hbm, conn), (cell_hbm, cell), (fr_hbm, fr3)]
        )
    ]
    for cpy in small:
        cpy.start()
    load = pltpu.make_async_copy(blk_hbm, blk, blk_sem)
    load.start()

    barrier = pltpu.get_barrier_semaphore()

    def greet(dev):
        pl.semaphore_signal(barrier, inc=1, device_id=dev, device_id_type=MESH)

    greet((nxt, group))
    greet((prv, group))
    for d in range(1, ZS):
        greet(z_device(z_peer(d)))
    for d in range(1, YXS):
        greet(yx_device(yx_peer(d)))
    for d in range(1, GROUPS):
        other = lax.rem(group + d, GROUPS)
        greet((tile, other))
        greet((nxt, other))
        greet((prv, other))

    def one(cond):
        return jnp.where(cond, 1.0, 0.0).astype(BF16)

    def pair_col(lane):
        half = lane >> 8
        j = lane & 255
        k = (j * 171) >> 9
        return half, k, j - 3 * k, j < DOF

    r = lax.broadcasted_iota(I32, (128, 512), 0)
    half, k, c, ok = pair_col(lax.broadcasted_iota(I32, (128, 512), 1))
    rep[...] = one((r == half * 64 + k) & ok)
    half, k, c, ok = pair_col(lax.broadcasted_iota(I32, (512, 128), 0))
    r = lax.broadcasted_iota(I32, (512, 128), 1)
    sel[...] = one((r == half * 64 + k) & ok)
    r = lax.broadcasted_iota(I32, (384, 512), 0)
    half, k, c, ok = pair_col(lax.broadcasted_iota(I32, (384, 512), 1))
    pm[...] = one((r == c * 128 + half * 64 + k) & ok)
    half, k, c, ok = pair_col(lax.broadcasted_iota(I32, (512, 384), 0))
    r = lax.broadcasted_iota(I32, (512, 384), 1)
    pmt[...] = one((r == c * 128 + half * 64 + k) & ok)

    fw[...] = jnp.zeros(fw.shape, BF16)
    yh[...] = jnp.zeros(yh.shape, BF16)
    yl[...] = jnp.zeros(yl.shape, BF16)

    for cpy in small:
        cpy.wait()

    same_own = (cl_ref[...] & 1) == (lax.broadcasted_iota(I32, (8, 256), 0) & 1)
    start = jnp.where(same_own, (2 * sign[...] - 1).astype(F32), 0.0)
    both = jnp.concatenate([start, jnp.where(same_own, 1.0, 0.0).astype(F32)], axis=0)
    qs_ref[...] = pltpu.roll(
        jnp.concatenate([both, jnp.zeros((16, 128), F32)], axis=1), RIM, 1
    )
    first = [
        rcopy(qs_ref.at[:, pl.ds(256, 128)], qsp, i_s.at[0], i_r.at[0], (nxt, group)),
        rcopy(qs_ref.at[:, pl.ds(0, 128)], qsn, i_s.at[1], i_r.at[1], (prv, group)),
        rcopy(w3.at[:, pl.ds(0, 512)], wn, i_s.at[2], i_r.at[2], (prv, group)),
    ]
    pl.semaphore_wait(barrier, 2 + ZS - 1 + YXS - 1 + 3 * (GROUPS - 1))
    for cpy in first:
        cpy.start()

    idx_ref[0:PAIRS, :] = jnp.concatenate([conn[0:PAIRS, :], conn[PAIRS:ELEMS, :]], axis=1)
    idx_ref[PAIRS:ELEMS, :] = jnp.concatenate([cell[0:PAIRS, :], cell[PAIRS:ELEMS, :]], axis=1)
    element = lax.broadcasted_iota(I32, (PAIRS, 128), 0) + jnp.where(
        lax.broadcasted_iota(I32, (PAIRS, 128), 1) < 64, 0, PAIRS
    )
    live = element < count_ref[0]
    wide = []
    for c in range(3):
        f = jnp.concatenate([fr3[c, 0:PAIRS, :], fr3[c, PAIRS:ELEMS, :]], axis=1)
        wide.append(jnp.where(live, f, 0.0))
    wide = jnp.concatenate(wide, axis=1)
    hi, rest = split(wide)
    mid, lo = split(rest)
    third = dot(jnp.concatenate([hi, mid, lo], axis=0).astype(BF16), pm[...])
    fr = third[0:PAIRS] + third[PAIRS : 2 * PAIRS] + third[2 * PAIRS :]
    for i in range(PAIRS):
        rows = slice(i * 8, i * 8 + 8)
        fr8[rows, :] = jnp.broadcast_to(fr[i : i + 1, :], (8, 512))
    for i in range(CHUNKS):
        rows = slice(i * 8, i * 8 + 8)
        for j in range(2):
            lanes = slice(j * 128, j * 128 + 128)
            n = 2 * i + j
            an8[rows, lanes] = jnp.broadcast_to(idx_ref[n : n + 1, :] >> 8, (8, 128))
            ac8[rows, lanes] = jnp.broadcast_to(idx_ref[PAIRS + n : PAIRS + n + 1, :] >> 7, (8, 128))

    low = jnp.where(
        lax.broadcasted_iota(I32, (64, 128), 0) < PAIRS, idx_ref[...] & 255, idx_ref[...] & 127
    ).astype(F32)
    cols = jnp.transpose(jnp.concatenate([low, jnp.zeros((64, 128), F32)], axis=0))
    lane_n = lax.broadcasted_iota(I32, (128, 256), 1).astype(F32)
    lane_c = lax.broadcasted_iota(I32, (128, 128), 1).astype(F32)
    sub_n = lax.broadcasted_iota(I32, (256, 128), 0)
    sub_c = lax.broadcasted_iota(I32, (128, 128), 0)
    for i in range(PAIRS):
        span = slice(i * 128, i * 128 + 128)
        ohn[:, span] = one(sub_n == (idx_ref[i : i + 1, :] & 255))
        ohc[:, span] = one(sub_c == (idx_ref[PAIRS + i : PAIRS + i + 1, :] & 127))
        ohnt[span, :] = one(lane_n == cols[:, i : i + 1])
        ohct[span, :] = one(lane_c == cols[:, PAIRS + i : PAIRS + i + 1])

    for cpy in first[:2]:
        cpy.wait()
    load.wait()

    lane = lax.broadcasted_iota(I32, (8, 128), 1)
    upper = jnp.where(lane >= RIM, 1.0, 0.0).astype(F32)
    own = [upper, jnp.ones((8, 128), F32), 1.0 - upper]
    exist = [
        upper + (1.0 - upper) * has_prev,
        jnp.ones((8, 128), F32),
        (1.0 - upper) + upper * has_next,
    ]
    q = [
        qs_ref[0:8, 0:128] + qsp[0:8, :] * has_prev,
        qs_ref[0:8, 128:256],
        qs_ref[0:8, 256:384] + qsn[0:8, :] * has_next,
    ]
    same = [
        qs_ref[8:16, 0:128] + qsp[8:16, :] * has_prev,
        qs_ref[8:16, 128:256],
        qs_ref[8:16, 256:384] + qsn[8:16, :] * has_next,
    ]

    def square_start(i, cur):
        total = cur[0] * cur[0] * own[0] + cur[1] * cur[1] + cur[2] * cur[2] * own[2]
        pa[i, my_z] = total
        for d in range(1, ZS):
            rcopy(
                pa.at[i, my_z], pa.at[i, my_z], s_s.at[d], p_r.at[i, 0, my_z],
                z_device(z_peer(d)),
            ).start()

    def square_mid(i):
        for d in range(1, ZS):
            z = z_peer(d)
            got = rcopy(pa.at[i, z], pa.at[i, z], s_s.at[d], p_r.at[i, 0, z], z_device(z))
            got.wait_recv()
            got.wait_send()
        total = pa[i, 0]
        for z in range(1, ZS):
            total = total + pa[i, z]
        pb[i, my_yx] = total
        for d in range(1, YXS):
            rcopy(
                pb.at[i, my_yx], pb.at[i, my_yx], s_s.at[d], p_r.at[i, 1, my_yx],
                yx_device(yx_peer(d)),
            ).start()

    def square_end(i):
        for d in range(1, YXS):
            yx = yx_peer(d)
            got = rcopy(
                pb.at[i, yx], pb.at[i, yx], s_s.at[d], p_r.at[i, 1, yx], yx_device(yx)
            )
            got.wait_recv()
            got.wait_send()
        total = pb[i, 0]
        for yx in range(1, YXS):
            total = total + pb[i, yx]
        mean = jnp.sum(total, axis=1, keepdims=True) / (256 * tiles)
        return 1.0 / jnp.sqrt(mean + 1e-06)

    def weight(ref, n):
        c = n % 3
        return ref[c : c + 1, n // 3 * 256 : n // 3 * 256 + 256]

    row16 = lax.broadcasted_iota(I32, (16, DOF), 0) < 8

    def scatter_nodes(n, unroll, levels):
        spreads = []
        for j in range(unroll):
            m = n * unroll + j
            r0 = mo(m * 16, 16)
            parts = []
            for c in range(3):
                span = slice(c * 128, c * 128 + 128)
                parts.append(
                    jnp.concatenate([fc[pl.ds(r0, 8), span], fc[pl.ds(r0 + 8, 8), span]], axis=1)
                )
            a = an8[pl.ds(mo(m * 8, 8), 8), :]
            spread = jnp.concatenate(
                [jnp.where(a == lv, parts[c], 0.0) for lv in levels for c in range(3)], axis=0
            )
            spreads.append(spread.astype(BF16))
        size = unroll * 256
        return dot(jnp.concatenate(spreads, axis=1), ohnt[pl.ds(mo(n * size, size), size), :])

    def gather_nodes(m, table, levels, base):
        got = dot(table[...], ohn[:, pl.ds(mo(m * 512, 512), 512)])
        r = mo(m * 16, 16)
        a = jnp.concatenate([an8[pl.ds(r, 8), :], an8[pl.ds(r + 8, 8), :]], axis=1)
        out = list(base)
        for n, lv in enumerate(levels):
            hit = a == lv
            for c in range(3):
                row = (n * 3 + c) * 8
                out[c] = jnp.where(hit, got[row : row + 8], out[c])
        return out

    def hessian(h, q):
        terms = 2 if h > 0 else 1
        parts = []
        for b in q:
            parts += list(split(b))[:terms]
        cells = jnp.concatenate(parts, axis=0).astype(BF16)

        def gather_cells(m):
            got = dot(cells, ohc[:, pl.ds(mo(m * 256, 256), 256)])
            a = ac8[pl.ds(mo(m * 8, 8), 8), :]
            level = []
            for n in range(3):
                r = n * 8 * terms
                level.append(got[r : r + 8] + got[r + 8 : r + 16] if h > 0 else got[r : r + 8])
            g = jnp.where(a == 0, level[0], jnp.where(a == 1, level[1], level[2]))
            hi, lo = split(g)
            rows = pl.ds(mo(m * 16, 16), 16)
            gh[rows, :] = jnp.concatenate([hi[:, :128], hi[:, 128:]], axis=0).astype(BF16)
            if h > 0:
                gl[rows, :] = jnp.concatenate([lo[:, :128], lo[:, 128:]], axis=0).astype(BF16)

        each(U_IN, gather_cells)

        for i in range(4):
            rows = slice(i * 64, i * 64 + 64)
            wide = dot(gh[rows, :], rep[...])
            if h > 0:
                wide = wide + dot(gl[rows, :], rep[...])
            xin[rows, :] = (wide * fr8[rows, :]).astype(BF16)

        def forward(m):
            rows = pl.ds(mo(m * 16, 16), 16)
            for half in range(2):
                span = slice(half * 256, half * 256 + DOF)
                x = xin[rows, span]
                o0 = dot(x, blk[2 * m + PAIRS * half], NT)
                o1 = dot(x, blk[2 * m + 1 + PAIRS * half], NT)
                fw[rows, span] = jnp.where(row16, o0, o1).astype(BF16)

        each(U_PROD, forward)

        for i in range(4):
            rows = slice(i * 64, i * 64 + 64)
            fc[rows, :] = dot(fw[rows, :], pmt[...])

        acci[...] = jnp.zeros(acci.shape, F32)

        edges = scatter_nodes(0, CHUNKS, EDGE)
        acce[...] = edges
        esend[h] = edges.astype(BF16)
        swap = [
            rcopy(esend.at[h, pl.ds(0, 48), :], renext.at[h], e_s.at[h, 0], e_r.at[h, 0], (prv, group)),
            rcopy(esend.at[h, pl.ds(48, 48), :], reprev.at[h], e_s.at[h, 1], e_r.at[h, 1], (nxt, group)),
        ]
        for cpy in swap:
            cpy.start()

        @pl.loop(0, CHUNKS // U_INNER)
        def _(n):
            acci[...] += scatter_nodes(n, U_INNER, INNER)

        if h > 0:
            square_mid(h - 1)

        for i in range(21):
            pair = []
            for j in range(2):
                n = 2 * i + j
                pair.append(acci[n * 8 : n * 8 + 8, :] * weight(w3, 6 + n))
            ti[i * 16 : i * 16 + 16, :] = jnp.concatenate(pair, axis=0).astype(BF16)

        def gather_inner(m):
            zero = jnp.zeros((8, 512), F32)
            out = gather_nodes(m, ti, INNER, [zero] * 3)
            r0 = mo(m * 32, 32)
            for c in range(3):
                span = slice(c * 128, c * 128 + 128)
                for j in range(4):
                    ad1[pl.ds(r0 + 8 * j, 8), span] = out[c][:, j * 128 : j * 128 + 128]

        each(U_GET, gather_inner, CHUNKS // 2)

        for cpy in swap if h > 0 else swap + first[2:]:
            cpy.wait()
        for i in range(6):
            if i < 3:
                theirs = reprev[h, i * 16 : i * 16 + 16, :].astype(F32) * has_prev
            else:
                theirs = renext[h, i * 16 - 48 : i * 16 - 32, :].astype(F32)
            total = acce[i * 16 : i * 16 + 16, :] + theirs
            pair = []
            for j in range(2):
                n = 2 * i + j
                scale = weight(w3, n) if n < 6 else weight(wn, n - 6) * has_next
                pair.append(total[j * 8 : j * 8 + 8] * scale)
            te[i * 16 : i * 16 + 16, :] = jnp.concatenate(pair, axis=0).astype(BF16)

        def gather_edge(m):
            r0 = mo(m * 32, 32)
            base = []
            for c in range(3):
                span = slice(c * 128, c * 128 + 128)
                base.append(
                    jnp.concatenate([ad1[pl.ds(r0 + 8 * j, 8), span] for j in range(4)], axis=1)
                )
            out = gather_nodes(m, te, EDGE, base)
            for c in range(3):
                span = slice(c * 128, c * 128 + 128)
                ad[pl.ds(r0, 32), span] = jnp.concatenate(
                    [out[c][:, j * 128 : j * 128 + 128] for j in range(4)], axis=0
                ).astype(BF16)

        each(CHUNKS // 2, gather_edge, CHUNKS // 2)

        for i in range(4):
            rows = slice(i * 64, i * 64 + 64)
            ain[rows, :] = dot(ad[rows, :], pm[...]).astype(BF16)

        def adjoint(m):
            rows = pl.ds(mo(m * 16, 16), 16)
            for half in range(2):
                span = slice(half * 256, half * 256 + DOF)
                x = ain[rows, span]
                o0 = dot(x, blk[2 * m + PAIRS * half])
                o1 = dot(x, blk[2 * m + 1 + PAIRS * half])
                hi, lo = split(jnp.where(row16, o0, o1) * fr8[rows, span])
                yh[rows, span] = hi.astype(BF16)
                yl[rows, span] = lo.astype(BF16)

        each(U_PROD, adjoint)

        for i in range(4):
            rows = slice(i * 64, i * 64 + 64)
            pt[rows, :] = dot(yh[rows, :], sel[...]) + dot(yl[rows, :], sel[...])

        def scatter_cells(n, acc):
            spreads = []
            for j in range(U_PUT):
                m = n * U_PUT + j
                r0 = mo(m * 16, 16)
                v = jnp.concatenate([pt[pl.ds(r0, 8), :], pt[pl.ds(r0 + 8, 8), :]], axis=1)
                a = ac8[pl.ds(mo(m * 8, 8), 8), :]
                spread = jnp.concatenate(
                    [jnp.where(a == lv, s, 0.0) for lv in range(3) for s in split(v)], axis=0
                )
                spreads.append(spread.astype(BF16))
            size = U_PUT * 256
            return acc + dot(
                jnp.concatenate(spreads, axis=1), ohct[pl.ds(mo(n * size, size), size), :]
            )

        acc = lax.fori_loop(0, CHUNKS // U_PUT, scatter_cells, jnp.zeros((48, 128), F32))
        sums = [acc[n * 16 : n * 16 + 8] + acc[n * 16 + 8 : n * 16 + 16] for n in range(3)]
        keep = same if h % 2 == 1 else [exist[n] - same[n] for n in range(3)]
        if h == POWER:
            scale = square_end(h - 1)
            for n in range(3):
                fp[group, :, n * 128 : n * 128 + 128] = sums[n] * keep[n] * scale
            return None
        bs[h, 0] = sums[0]
        bs[h, 1] = sums[2]
        swap = [
            rcopy(bs.at[h, 0], rbn.at[h], b_s.at[h, 0], b_r.at[h, 0], (prv, group)),
            rcopy(bs.at[h, 1], rbp.at[h], b_s.at[h, 1], b_r.at[h, 1], (nxt, group)),
        ]
        for cpy in swap:
            cpy.start()
        scale = square_end(h - 1) if h > 0 else None
        for cpy in swap:
            cpy.wait()
        sums[0] = sums[0] + rbp[h] * has_prev
        sums[2] = sums[2] + rbn[h] * has_next
        out = []
        for n in range(3):
            v = sums[n] * keep[n]
            out.append(v if scale is None else v * scale)
        return out

    for h in range(ROUNDS):
        q = hessian(h, q)
        if h < POWER:
            square_start(h, q)
        if h == 0:
            cells_v[0:8, :] = pltpu.roll(jnp.concatenate(q, axis=1), 384 - RIM, 1)[:, :256]
    def final(kind, d, source):
        other = lax.rem(group + d, GROUPS)
        device, landing, span = (
            ((prv, other), fpn, pl.ds(0, 128)),
            ((nxt, other), fpp, pl.ds(256, 128)),
            ((tile, other), fp, pl.ds(0, 384)),
        )[kind]
        return rcopy(
            fp.at[group, :, span], landing.at[source], g_s.at[kind, d], g_r.at[kind, source], device
        )

    order = [(kind, d) for kind in range(3) for d in range(GROUPS) if kind < 2 or d > 0]
    for kind, d in order:
        final(kind, d, group).start()
    for kind, d in order:
        final(kind, d, lax.rem(group + d, GROUPS)).wait_recv()
    for kind, d in order:
        final(kind, d, group).wait_send()

    def window(g):
        return jnp.concatenate(
            [
                fp[g, :, 0:128] + fpp[g] * has_prev,
                fp[g, :, 128:256],
                fp[g, :, 256:384] + fpn[g] * has_next,
            ],
            axis=1,
        )

    mine = pltpu.roll(window(group), 384 - RIM, 1)[:, :256]
    cells_v[8:16, :] = mine
    put = pltpu.make_async_copy(cells_v, out_ref, out_sem.at[0])
    put.start()
    every = jnp.concatenate([window(g) for g in range(GROUPS)], axis=0)
    every = pltpu.roll(every, 384 - RIM, 1)[:, :256]
    outer = jnp.concatenate([every * mine[i : i + 1, :] for i in range(8)], axis=0)
    hi, lo = split(outer)
    member = one(lax.broadcasted_iota(I32, (64, 256), 0) == cl_ref[...])
    grams = dot(member, hi.astype(BF16), NT) + dot(member, lo.astype(BF16), NT)
    for yx in range(YXS):
        rows = grams[yx * 8 : yx * 8 + 8]
        gk[yx] = jnp.concatenate([rows[:, :128], rows[:, 128:]], axis=0).astype(BF16)

    for d in range(1, YXS):
        yx = yx_peer(d)
        rcopy(
            gk.at[yx], ka.at[my_yx], s_s.at[d], k_r.at[0, my_yx],
            yx_device(yx),
        ).start()
    for d in range(1, YXS):
        yx = yx_peer(d)
        got = rcopy(ka.at[yx], ka.at[yx], s_s.at[d], k_r.at[0, yx], yx_device(yx))
        got.wait_recv()
        got.wait_send()
    ka[my_yx] = gk[my_yx]
    total = ka[0].astype(F32)
    for yx in range(1, YXS):
        total = total + ka[yx].astype(F32)
    kb[my_z] = total.astype(BF16)
    for d in range(1, ZS):
        rcopy(
            kb.at[my_z], kb.at[my_z], s_s.at[d], k_r.at[1, my_z], z_device(z_peer(d))
        ).start()
    for d in range(1, ZS):
        z = z_peer(d)
        got = rcopy(kb.at[z], kb.at[z], s_s.at[d], k_r.at[1, z], z_device(z))
        got.wait_recv()
        got.wait_send()
    total = kb[0].astype(F32)
    for z in range(1, ZS):
        total = total + kb[z].astype(F32)
    kc[...] = total
    keep = pltpu.make_async_copy(kc, gram_ref.at[my_yx], out_sem.at[1])
    for d in range(1, YXS):
        rcopy(
            kc, gram_ref.at[my_yx], s_s.at[d], k_r.at[2, my_yx], yx_device(yx_peer(d))
        ).start()
    keep.start()
    for d in range(1, YXS):
        yx = yx_peer(d)
        got = rcopy(kc, gram_ref.at[yx], s_s.at[d], k_r.at[2, yx], yx_device(yx))
        got.wait_recv()
        got.wait_send()
    keep.wait()
    put.wait()


def finish(cells_ref, sums_ref, samp_ref, refd_ref, gram_ref):
    samp_ref[...] = cells_ref[0:8, :]
    refd_ref[...] = cells_ref[8:16, :]
    for j in range(2):
        rows = jnp.concatenate([sums_ref[n, j * 8 : j * 8 + 8] for n in range(YXS)], axis=0)
        gram_ref[j * 128 : j * 128 + 128, :] = jnp.transpose(rows)


def shards(
    blocks, connectivity, basal_map, friction, elem_counts, obs_weight, sign_bits, cluster_ids
):
    vmem = pl.BlockSpec(memory_space=pltpu.VMEM)
    here = pl.BlockSpec(memory_space=pl.ANY)
    dma = pltpu.SemaphoreType.DMA
    cells, gram = pl.pallas_call(
        kernel,
        out_shape=(
            jax.ShapeDtypeStruct((16, 256), F32),
            jax.ShapeDtypeStruct((YXS, 16, 128), F32),
        ),
        in_specs=[here] * 4 + [pl.BlockSpec(memory_space=pltpu.SMEM)] + [here] * 3,
        out_specs=(here, here),
        scratch_shapes=[
            pltpu.VMEM((ELEMS, 64), I32),
            pltpu.VMEM((ELEMS, 64), I32),
            pltpu.VMEM((3, ELEMS, 64), F32),
            pltpu.VMEM((3, 4096), F32),
            pltpu.VMEM((8, 256), I32),
            pltpu.VMEM((1, 256), I32),
            pltpu.VMEM((ELEMS, 128), I32),
            pltpu.VMEM((16, 384), F32),
            pltpu.VMEM((ELEMS, DOF, DOF), BF16),
            pltpu.VMEM((256, 4096), BF16),
            pltpu.VMEM((4096, 256), BF16),
            pltpu.VMEM((128, 4096), BF16),
            pltpu.VMEM((4096, 128), BF16),
            pltpu.VMEM((128, 256), I32),
            pltpu.VMEM((128, 256), I32),
            pltpu.VMEM((256, 512), F32),
            pltpu.VMEM((128, 512), BF16),
            pltpu.VMEM((512, 128), BF16),
            pltpu.VMEM((384, 512), BF16),
            pltpu.VMEM((512, 384), BF16),
            pltpu.VMEM((256, 128), BF16),
            pltpu.VMEM((256, 128), BF16),
            pltpu.VMEM((256, 512), BF16),
            pltpu.VMEM((256, 512), BF16),
            pltpu.VMEM((256, 384), F32),
            pltpu.VMEM((96, 256), F32),
            pltpu.VMEM((336, 256), F32),
            pltpu.VMEM((96, 256), BF16),
            pltpu.VMEM((336, 256), BF16),
            pltpu.VMEM((256, 384), F32),
            pltpu.VMEM((256, 384), BF16),
            pltpu.VMEM((256, 512), BF16),
            pltpu.VMEM((256, 512), BF16),
            pltpu.VMEM((256, 512), BF16),
            pltpu.VMEM((256, 128), F32),
            pltpu.VMEM((3, 512), F32),
            pltpu.VMEM((16, 128), F32),
            pltpu.VMEM((16, 128), F32),
            pltpu.VMEM((ROUNDS, 96, 256), BF16),
            pltpu.VMEM((ROUNDS, 48, 256), BF16),
            pltpu.VMEM((ROUNDS, 48, 256), BF16),
            pltpu.VMEM((ROUNDS, 2, 8, 128), F32),
            pltpu.VMEM((ROUNDS, 8, 128), F32),
            pltpu.VMEM((ROUNDS, 8, 128), F32),
            pltpu.VMEM((POWER, ZS, 8, 128), F32),
            pltpu.VMEM((POWER, YXS, 8, 128), F32),
            pltpu.VMEM((GROUPS, 8, 384), F32),
            pltpu.VMEM((GROUPS, 8, 128), F32),
            pltpu.VMEM((GROUPS, 8, 128), F32),
            pltpu.VMEM((YXS, 16, 128), BF16),
            pltpu.VMEM((YXS, 16, 128), BF16),
            pltpu.VMEM((ZS, 16, 128), BF16),
            pltpu.VMEM((16, 128), F32),
            pltpu.VMEM((16, 256), F32),
            dma,
            dma((6,)),
            dma((2,)),
            dma((3,)),
            dma((3,)),
            dma((ROUNDS, 2)),
            dma((ROUNDS, 2)),
            dma((ROUNDS, 2)),
            dma((ROUNDS, 2)),
            dma((8,)),
            dma((POWER, 2, 8)),
            dma((3, GROUPS)),
            dma((3, GROUPS)),
            dma((3, 8)),
        ],
        compiler_params=pltpu.CompilerParams(
            collective_id=0, has_side_effects=True, vmem_limit_bytes=63 * 1024 * 1024
        ),
    )(
        blocks, connectivity, basal_map, friction.transpose(2, 0, 1), elem_counts,
        obs_weight.T, sign_bits.T, cluster_ids[None, :],
    )
    samp, refd, gram = pl.pallas_call(
        finish,
        out_shape=(
            jax.ShapeDtypeStruct((8, 256), F32),
            jax.ShapeDtypeStruct((8, 256), F32),
            jax.ShapeDtypeStruct((256, 64), F32),
        ),
        in_specs=[vmem, vmem],
        out_specs=(vmem, vmem, vmem),
    )(cells, gram)
    return samp.T, refd.T, gram.reshape(8, 32, 64).transpose(2, 0, 1)


def solution(mesh):
    in_specs = (
        P("tiles", None, None),
        P("tiles", None),
        P("tiles", None),
        P("tiles", None, None),
        P("tiles"),
        P("tiles", None),
        P("tiles", "probes"),
        P("tiles"),
    )
    out_specs = (P("tiles", "probes"), P("tiles", "probes"), P(None, "probes", None))
    return jax.shard_map(shards, mesh=mesh, in_specs=in_specs, out_specs=out_specs, check_vma=False)
```

```python
import functools

import jax
import jax.numpy as jnp
from jax import lax
from jax.experimental import pallas as pl
from jax.experimental.pallas import tpu as pltpu
from jax.sharding import PartitionSpec as P

F32 = jnp.float32
BF16 = jnp.bfloat16
I32 = jnp.int32
POWER = 2
ROUNDS = POWER + 1
RIM = 64
ELEMS = 64
DOF = 192
PAIRS = 32
CHUNKS = 16
U_IN = 16
U_PROD = 16
U_INNER = 8
U_GET = 4
ZS = 8
YXS = 8
GROUPS = 4
EDGE = (0, 1, 16, 17)
INNER = tuple(range(2, 16))
NT = (((1,), (1,)), ((), ()))
NN = (((1,), (0,)), ((), ()))
MESH = pl.DeviceIdType.MESH


def mo(x, n):
    return x if isinstance(x, int) else pl.multiple_of(x, n)


def each(unroll, body, steps=CHUNKS):
    if unroll == steps:
        for j in range(steps):
            body(j)
        return

    @pl.loop(0, steps // unroll)
    def _(n):
        for j in range(unroll):
            body(n * unroll + j)


def split(x):
    hi = x.astype(BF16).astype(F32)
    return hi, x - hi


def dot(a, b, dims=NN):
    return lax.dot_general(a, b, dims, preferred_element_type=F32)


def kernel(
    blk_hbm, conn_hbm, cell_hbm, fr_hbm, count_ref, w_hbm, sign_hbm, cl_hbm,
    out_ref, gram_ref,
    conn, cell, fr3, w3, sign, cl_ref, idx_ref, qs_ref,
    blk, ohn, ohnt, ohc, ohct, an8, ac8, fr8, rep, sel, pm, pmt,
    gh, gl, xin, fw, fc, acce, acci, te, ti, ad1, ad, ain, yh, yl, pt,
    wn, qsp, qsn, esend, renext, reprev, bs, rbn, rbp, pa, pb, fp, fpn, fpp, gk, ka, kb, kc, cells_v,
    blk_sem, in_sem, out_sem, i_s, i_r, e_s, e_r, b_s, b_r, s_s, p_r, g_s, g_r, k_r,
):
    tile = lax.axis_index("tiles")
    group = lax.axis_index("probes")
    tiles = lax.axis_size("tiles")
    nxt = lax.rem(tile + 1, tiles)
    prv = lax.rem(tile + tiles - 1, tiles)
    my_z = lax.rem(tile, ZS)
    my_yx = lax.div(tile, ZS)
    has_prev = jnp.where(tile > 0, 1.0, 0.0).astype(F32)
    has_next = jnp.where(tile < tiles - 1, 1.0, 0.0).astype(F32)

    def z_peer(d):
        return lax.rem(my_z + d, ZS)

    def yx_peer(d):
        return lax.rem(my_yx + d, YXS)

    def z_device(z):
        return (my_yx * ZS + z, group)

    def yx_device(yx):
        return (yx * ZS + my_z, group)

    def rcopy(src, dst, ss, rs, dev):
        return pltpu.make_async_remote_copy(
            src_ref=src, dst_ref=dst, send_sem=ss, recv_sem=rs, device_id=dev, device_id_type=MESH
        )

    small = [
        pltpu.make_async_copy(src, dst, in_sem.at[n])
        for n, (src, dst) in enumerate(
            [(sign_hbm, sign), (cl_hbm, cl_ref), (w_hbm, w3), (conn_hbm, conn), (cell_hbm, cell), (fr_hbm, fr3)]
        )
    ]
    for cpy in small:
        cpy.start()
    load = pltpu.make_async_copy(blk_hbm, blk, blk_sem)
    load.start()

    barrier = pltpu.get_barrier_semaphore()

    def greet(dev):
        pl.semaphore_signal(barrier, inc=1, device_id=dev, device_id_type=MESH)

    greet((nxt, group))
    greet((prv, group))
    for d in range(1, ZS):
        greet(z_device(z_peer(d)))
    for d in range(1, YXS):
        greet(yx_device(yx_peer(d)))
    for d in range(1, GROUPS):
        other = lax.rem(group + d, GROUPS)
        greet((tile, other))
        greet((nxt, other))
        greet((prv, other))

    def one(cond):
        return jnp.where(cond, 1.0, 0.0).astype(BF16)

    def pair_col(lane):
        half = lane >> 8
        j = lane & 255
        k = (j * 171) >> 9
        return half, k, j - 3 * k, j < DOF

    r = lax.broadcasted_iota(I32, (128, 512), 0)
    half, k, c, ok = pair_col(lax.broadcasted_iota(I32, (128, 512), 1))
    rep[...] = one((r == half * 64 + k) & ok)
    half, k, c, ok = pair_col(lax.broadcasted_iota(I32, (512, 128), 0))
    r = lax.broadcasted_iota(I32, (512, 128), 1)
    sel[...] = one((r == half * 64 + k) & ok)
    r = lax.broadcasted_iota(I32, (384, 512), 0)
    half, k, c, ok = pair_col(lax.broadcasted_iota(I32, (384, 512), 1))
    pm[...] = one((r == c * 128 + half * 64 + k) & ok)
    half, k, c, ok = pair_col(lax.broadcasted_iota(I32, (512, 384), 0))
    r = lax.broadcasted_iota(I32, (512, 384), 1)
    pmt[...] = one((r == c * 128 + half * 64 + k) & ok)

    fw[...] = jnp.zeros(fw.shape, BF16)
    yh[...] = jnp.zeros(yh.shape, BF16)
    yl[...] = jnp.zeros(yl.shape, BF16)

    for cpy in small:
        cpy.wait()

    same_own = (cl_ref[...] & 1) == (lax.broadcasted_iota(I32, (8, 256), 0) & 1)
    start = jnp.where(same_own, (2 * sign[...] - 1).astype(F32), 0.0)
    both = jnp.concatenate([start, jnp.where(same_own, 1.0, 0.0).astype(F32)], axis=0)
    qs_ref[...] = pltpu.roll(
        jnp.concatenate([both, jnp.zeros((16, 128), F32)], axis=1), RIM, 1
    )
    first = [
        rcopy(qs_ref.at[:, pl.ds(256, 128)], qsp, i_s.at[0], i_r.at[0], (nxt, group)),
        rcopy(qs_ref.at[:, pl.ds(0, 128)], qsn, i_s.at[1], i_r.at[1], (prv, group)),
        rcopy(w3.at[:, pl.ds(0, 512)], wn, i_s.at[2], i_r.at[2], (prv, group)),
    ]
    pl.semaphore_wait(barrier, 2 + ZS - 1 + YXS - 1 + 3 * (GROUPS - 1))
    for cpy in first:
        cpy.start()

    idx_ref[0:PAIRS, :] = jnp.concatenate([conn[0:PAIRS, :], conn[PAIRS:ELEMS, :]], axis=1)
    idx_ref[PAIRS:ELEMS, :] = jnp.concatenate([cell[0:PAIRS, :], cell[PAIRS:ELEMS, :]], axis=1)
    element = lax.broadcasted_iota(I32, (PAIRS, 128), 0) + jnp.where(
        lax.broadcasted_iota(I32, (PAIRS, 128), 1) < 64, 0, PAIRS
    )
    live = element < count_ref[0]
    wide = []
    for c in range(3):
        f = jnp.concatenate([fr3[c, 0:PAIRS, :], fr3[c, PAIRS:ELEMS, :]], axis=1)
        wide.append(jnp.where(live, f, 0.0))
    wide = jnp.concatenate(wide, axis=1)
    hi, rest = split(wide)
    mid, lo = split(rest)
    third = dot(jnp.concatenate([hi, mid, lo], axis=0).astype(BF16), pm[...])
    fr = third[0:PAIRS] + third[PAIRS : 2 * PAIRS] + third[2 * PAIRS :]
    for i in range(PAIRS):
        rows = slice(i * 8, i * 8 + 8)
        fr8[rows, :] = jnp.broadcast_to(fr[i : i + 1, :], (8, 512))
    for i in range(CHUNKS):
        rows = slice(i * 8, i * 8 + 8)
        for j in range(2):
            lanes = slice(j * 128, j * 128 + 128)
            n = 2 * i + j
            an8[rows, lanes] = jnp.broadcast_to(idx_ref[n : n + 1, :] >> 8, (8, 128))
            ac8[rows, lanes] = jnp.broadcast_to(idx_ref[PAIRS + n : PAIRS + n + 1, :] >> 7, (8, 128))

    low = jnp.where(
        lax.broadcasted_iota(I32, (64, 128), 0) < PAIRS, idx_ref[...] & 255, idx_ref[...] & 127
    ).astype(F32)
    cols = jnp.transpose(jnp.concatenate([low, jnp.zeros((64, 128), F32)], axis=0))
    lane_n = lax.broadcasted_iota(I32, (128, 256), 1).astype(F32)
    lane_c = lax.broadcasted_iota(I32, (128, 128), 1).astype(F32)
    sub_n = lax.broadcasted_iota(I32, (256, 128), 0)
    sub_c = lax.broadcasted_iota(I32, (128, 128), 0)
    for i in range(PAIRS):
        span = slice(i * 128, i * 128 + 128)
        ohn[:, span] = one(sub_n == (idx_ref[i : i + 1, :] & 255))
        ohc[:, span] = one(sub_c == (idx_ref[PAIRS + i : PAIRS + i + 1, :] & 127))
        ohnt[span, :] = one(lane_n == cols[:, i : i + 1])
        ohct[span, :] = one(lane_c == cols[:, PAIRS + i : PAIRS + i + 1])

    for cpy in first[:2]:
        cpy.wait()
    load.wait()

    lane = lax.broadcasted_iota(I32, (8, 128), 1)
    upper = jnp.where(lane >= RIM, 1.0, 0.0).astype(F32)
    own = [upper, jnp.ones((8, 128), F32), 1.0 - upper]
    exist = [
        upper + (1.0 - upper) * has_prev,
        jnp.ones((8, 128), F32),
        (1.0 - upper) + upper * has_next,
    ]
    q = [
        qs_ref[0:8, 0:128] + qsp[0:8, :] * has_prev,
        qs_ref[0:8, 128:256],
        qs_ref[0:8, 256:384] + qsn[0:8, :] * has_next,
    ]
    same = [
        qs_ref[8:16, 0:128] + qsp[8:16, :] * has_prev,
        qs_ref[8:16, 128:256],
        qs_ref[8:16, 256:384] + qsn[8:16, :] * has_next,
    ]

    def square_start(i, cur):
        total = cur[0] * cur[0] * own[0] + cur[1] * cur[1] + cur[2] * cur[2] * own[2]
        pa[i, my_z] = total
        for d in range(1, ZS):
            rcopy(
                pa.at[i, my_z], pa.at[i, my_z], s_s.at[d], p_r.at[i, 0, my_z],
                z_device(z_peer(d)),
            ).start()

    def square_mid(i):
        for d in range(1, ZS):
            z = z_peer(d)
            got = rcopy(pa.at[i, z], pa.at[i, z], s_s.at[d], p_r.at[i, 0, z], z_device(z))
            got.wait_recv()
            got.wait_send()
        total = pa[i, 0]
        for z in range(1, ZS):
            total = total + pa[i, z]
        pb[i, my_yx] = total
        for d in range(1, YXS):
            rcopy(
                pb.at[i, my_yx], pb.at[i, my_yx], s_s.at[d], p_r.at[i, 1, my_yx],
                yx_device(yx_peer(d)),
            ).start()

    def square_end(i):
        for d in range(1, YXS):
            yx = yx_peer(d)
            got = rcopy(
                pb.at[i, yx], pb.at[i, yx], s_s.at[d], p_r.at[i, 1, yx], yx_device(yx)
            )
            got.wait_recv()
            got.wait_send()
        total = pb[i, 0]
        for yx in range(1, YXS):
            total = total + pb[i, yx]
        mean = jnp.sum(total, axis=1, keepdims=True) / (256 * tiles)
        return 1.0 / jnp.sqrt(mean + 1e-06)

    def weight(ref, n):
        c = n % 3
        return ref[c : c + 1, n // 3 * 256 : n // 3 * 256 + 256]

    row16 = lax.broadcasted_iota(I32, (16, DOF), 0) < 8

    def scatter_nodes(n, unroll, levels):
        spreads = []
        for j in range(unroll):
            m = n * unroll + j
            r0 = mo(m * 16, 16)
            parts = []
            for c in range(3):
                span = slice(c * 128, c * 128 + 128)
                parts.append(
                    jnp.concatenate([fc[pl.ds(r0, 8), span], fc[pl.ds(r0 + 8, 8), span]], axis=1)
                )
            a = an8[pl.ds(mo(m * 8, 8), 8), :]
            spread = jnp.concatenate(
                [jnp.where(a == lv, parts[c], 0.0) for lv in levels for c in range(3)], axis=0
            )
            spreads.append(spread.astype(BF16))
        size = unroll * 256
        return dot(jnp.concatenate(spreads, axis=1), ohnt[pl.ds(mo(n * size, size), size), :])

    def gather_nodes(m, table, levels, base):
        got = dot(table[...], ohn[:, pl.ds(mo(m * 512, 512), 512)])
        r = mo(m * 16, 16)
        a = jnp.concatenate([an8[pl.ds(r, 8), :], an8[pl.ds(r + 8, 8), :]], axis=1)
        out = list(base)
        for n, lv in enumerate(levels):
            hit = a == lv
            for c in range(3):
                row = (n * 3 + c) * 8
                out[c] = jnp.where(hit, got[row : row + 8], out[c])
        return out

    def hessian(h, q):
        terms = 2 if h > 0 else 1
        parts = []
        for b in q:
            parts += list(split(b))[:terms]
        cells = jnp.concatenate(parts, axis=0).astype(BF16)

        def gather_cells(m):
            got = dot(cells, ohc[:, pl.ds(mo(m * 256, 256), 256)])
            a = ac8[pl.ds(mo(m * 8, 8), 8), :]
            level = []
            for n in range(3):
                r = n * 8 * terms
                level.append(got[r : r + 8] + got[r + 8 : r + 16] if h > 0 else got[r : r + 8])
            g = jnp.where(a == 0, level[0], jnp.where(a == 1, level[1], level[2]))
            hi, lo = split(g)
            rows = pl.ds(mo(m * 16, 16), 16)
            gh[rows, :] = jnp.concatenate([hi[:, :128], hi[:, 128:]], axis=0).astype(BF16)
            if h > 0:
                gl[rows, :] = jnp.concatenate([lo[:, :128], lo[:, 128:]], axis=0).astype(BF16)

        each(U_IN, gather_cells)

        for i in range(4):
            rows = slice(i * 64, i * 64 + 64)
            wide = dot(gh[rows, :], rep[...])
            if h > 0:
                wide = wide + dot(gl[rows, :], rep[...])
            xin[rows, :] = (wide * fr8[rows, :]).astype(BF16)

        def forward(m):
            rows = pl.ds(mo(m * 16, 16), 16)
            for half in range(2):
                span = slice(half * 256, half * 256 + DOF)
                x = xin[rows, span]
                o0 = dot(x, blk[2 * m + PAIRS * half], NT)
                o1 = dot(x, blk[2 * m + 1 + PAIRS * half], NT)
                fw[rows, span] = jnp.where(row16, o0, o1).astype(BF16)

        each(U_PROD, forward)

        for i in range(4):
            rows = slice(i * 64, i * 64 + 64)
            fc[rows, :] = dot(fw[rows, :], pmt[...])

        acci[...] = jnp.zeros(acci.shape, F32)

        edges = scatter_nodes(0, CHUNKS, EDGE)
        acce[...] = edges
        esend[h] = edges.astype(BF16)
        swap = [
            rcopy(esend.at[h, pl.ds(0, 48), :], renext.at[h], e_s.at[h, 0], e_r.at[h, 0], (prv, group)),
            rcopy(esend.at[h, pl.ds(48, 48), :], reprev.at[h], e_s.at[h, 1], e_r.at[h, 1], (nxt, group)),
        ]
        for cpy in swap:
            cpy.start()

        @pl.loop(0, CHUNKS // U_INNER)
        def _(n):
            acci[...] += scatter_nodes(n, U_INNER, INNER)

        if h > 0:
            square_mid(h - 1)

        for i in range(21):
            pair = []
            for j in range(2):
                n = 2 * i + j
                pair.append(acci[n * 8 : n * 8 + 8, :] * weight(w3, 6 + n))
            ti[i * 16 : i * 16 + 16, :] = jnp.concatenate(pair, axis=0).astype(BF16)

        def gather_inner(m):
            zero = jnp.zeros((8, 512), F32)
            out = gather_nodes(m, ti, INNER, [zero] * 3)
            r0 = mo(m * 32, 32)
            for c in range(3):
                span = slice(c * 128, c * 128 + 128)
                for j in range(4):
                    ad1[pl.ds(r0 + 8 * j, 8), span] = out[c][:, j * 128 : j * 128 + 128]

        each(U_GET, gather_inner, CHUNKS // 2)

        for cpy in swap if h > 0 else swap + first[2:]:
            cpy.wait()
        for i in range(6):
            if i < 3:
                theirs = reprev[h, i * 16 : i * 16 + 16, :].astype(F32) * has_prev
            else:
                theirs = renext[h, i * 16 - 48 : i * 16 - 32, :].astype(F32)
            total = acce[i * 16 : i * 16 + 16, :] + theirs
            pair = []
            for j in range(2):
                n = 2 * i + j
                scale = weight(w3, n) if n < 6 else weight(wn, n - 6) * has_next
                pair.append(total[j * 8 : j * 8 + 8] * scale)
            te[i * 16 : i * 16 + 16, :] = jnp.concatenate(pair, axis=0).astype(BF16)

        def gather_edge(m):
            r0 = mo(m * 32, 32)
            base = []
            for c in range(3):
                span = slice(c * 128, c * 128 + 128)
                base.append(
                    jnp.concatenate([ad1[pl.ds(r0 + 8 * j, 8), span] for j in range(4)], axis=1)
                )
            out = gather_nodes(m, te, EDGE, base)
            for c in range(3):
                span = slice(c * 128, c * 128 + 128)
                ad[pl.ds(r0, 32), span] = jnp.concatenate(
                    [out[c][:, j * 128 : j * 128 + 128] for j in range(4)], axis=0
                ).astype(BF16)

        each(CHUNKS // 2, gather_edge, CHUNKS // 2)

        for i in range(4):
            rows = slice(i * 64, i * 64 + 64)
            ain[rows, :] = dot(ad[rows, :], pm[...]).astype(BF16)

        def adjoint(m):
            rows = pl.ds(mo(m * 16, 16), 16)
            for half in range(2):
                span = slice(half * 256, half * 256 + DOF)
                x = ain[rows, span]
                o0 = dot(x, blk[2 * m + PAIRS * half])
                o1 = dot(x, blk[2 * m + 1 + PAIRS * half])
                hi, lo = split(jnp.where(row16, o0, o1) * fr8[rows, span])
                yh[rows, span] = hi.astype(BF16)
                yl[rows, span] = lo.astype(BF16)

        each(U_PROD, adjoint)

        for i in range(4):
            rows = slice(i * 64, i * 64 + 64)
            pt[rows, :] = dot(yh[rows, :], sel[...]) + dot(yl[rows, :], sel[...])

        def scatter_cells(levels):
            spreads = []
            for m in range(CHUNKS):
                r0 = m * 16
                v = jnp.concatenate([pt[r0 : r0 + 8, :], pt[r0 + 8 : r0 + 16, :]], axis=1)
                a = ac8[m * 8 : m * 8 + 8, :]
                spread = jnp.concatenate(
                    [jnp.where(a == lv, s, 0.0) for lv in levels for s in split(v)], axis=0
                )
                spreads.append(spread.astype(BF16))
            acc = dot(jnp.concatenate(spreads, axis=1), ohct[...])
            return [acc[n * 16 : n * 16 + 8] + acc[n * 16 + 8 : n * 16 + 16] for n in range(len(levels))]

        if h == POWER:
            sums = scatter_cells((0, 1, 2))
        else:
            before, after = scatter_cells((0, 2))
            sums = [before, None, after]
        keep = same if h % 2 == 1 else [exist[n] - same[n] for n in range(3)]
        if h == POWER:
            scale = square_end(h - 1)
            for n in range(3):
                fp[group, :, n * 128 : n * 128 + 128] = sums[n] * keep[n] * scale
            return None
        bs[h, 0] = sums[0]
        bs[h, 1] = sums[2]
        swap = [
            rcopy(bs.at[h, 0], rbn.at[h], b_s.at[h, 0], b_r.at[h, 0], (prv, group)),
            rcopy(bs.at[h, 1], rbp.at[h], b_s.at[h, 1], b_r.at[h, 1], (nxt, group)),
        ]
        for cpy in swap:
            cpy.start()
        sums[1] = scatter_cells((1,))[0]
        scale = square_end(h - 1) if h > 0 else None
        for cpy in swap:
            cpy.wait()
        sums[0] = sums[0] + rbp[h] * has_prev
        sums[2] = sums[2] + rbn[h] * has_next
        out = []
        for n in range(3):
            v = sums[n] * keep[n]
            out.append(v if scale is None else v * scale)
        return out

    for h in range(ROUNDS):
        q = hessian(h, q)
        if h < POWER:
            square_start(h, q)
        if h == 0:
            cells_v[0:8, :] = pltpu.roll(jnp.concatenate(q, axis=1), 384 - RIM, 1)[:, :256]
    def final(kind, d, source):
        other = lax.rem(group + d, GROUPS)
        device, landing, span = (
            ((prv, other), fpn, pl.ds(0, 128)),
            ((nxt, other), fpp, pl.ds(256, 128)),
            ((tile, other), fp, pl.ds(0, 384)),
        )[kind]
        return rcopy(
            fp.at[group, :, span], landing.at[source], g_s.at[kind, d], g_r.at[kind, source], device
        )

    order = [(kind, d) for kind in range(3) for d in range(GROUPS) if kind < 2 or d > 0]
    for kind, d in order:
        final(kind, d, group).start()
    for kind, d in order:
        final(kind, d, lax.rem(group + d, GROUPS)).wait_recv()
    for kind, d in order:
        final(kind, d, group).wait_send()

    def window(g):
        return jnp.concatenate(
            [
                fp[g, :, 0:128] + fpp[g] * has_prev,
                fp[g, :, 128:256],
                fp[g, :, 256:384] + fpn[g] * has_next,
            ],
            axis=1,
        )

    mine = pltpu.roll(window(group), 384 - RIM, 1)[:, :256]
    cells_v[8:16, :] = mine
    put = pltpu.make_async_copy(cells_v, out_ref, out_sem.at[0])
    put.start()
    every = jnp.concatenate([window(g) for g in range(GROUPS)], axis=0)
    every = pltpu.roll(every, 384 - RIM, 1)[:, :256]
    outer = jnp.concatenate([every * mine[i : i + 1, :] for i in range(8)], axis=0)
    member = one(lax.broadcasted_iota(I32, (64, 256), 0) == cl_ref[...])
    grams = dot(member, outer.astype(BF16), NT)
    for yx in range(YXS):
        rows = grams[yx * 8 : yx * 8 + 8]
        gk[yx] = jnp.concatenate([rows[:, :128], rows[:, 128:]], axis=0).astype(BF16)

    for d in range(1, YXS):
        yx = yx_peer(d)
        rcopy(
            gk.at[yx], ka.at[my_yx], s_s.at[d], k_r.at[0, my_yx],
            yx_device(yx),
        ).start()
    for d in range(1, YXS):
        yx = yx_peer(d)
        got = rcopy(ka.at[yx], ka.at[yx], s_s.at[d], k_r.at[0, yx], yx_device(yx))
        got.wait_recv()
        got.wait_send()
    ka[my_yx] = gk[my_yx]
    total = ka[0].astype(F32)
    for yx in range(1, YXS):
        total = total + ka[yx].astype(F32)
    kb[my_z] = total.astype(BF16)
    for d in range(1, ZS):
        rcopy(
            kb.at[my_z], kb.at[my_z], s_s.at[d], k_r.at[1, my_z], z_device(z_peer(d))
        ).start()
    for d in range(1, ZS):
        z = z_peer(d)
        got = rcopy(kb.at[z], kb.at[z], s_s.at[d], k_r.at[1, z], z_device(z))
        got.wait_recv()
        got.wait_send()
    total = kb[0].astype(F32)
    for z in range(1, ZS):
        total = total + kb[z].astype(F32)
    kc[...] = total
    keep = pltpu.make_async_copy(kc, gram_ref.at[my_yx], out_sem.at[1])
    for d in range(1, YXS):
        rcopy(
            kc, gram_ref.at[my_yx], s_s.at[d], k_r.at[2, my_yx], yx_device(yx_peer(d))
        ).start()
    keep.start()
    for d in range(1, YXS):
        yx = yx_peer(d)
        got = rcopy(kc, gram_ref.at[yx], s_s.at[d], k_r.at[2, yx], yx_device(yx))
        got.wait_recv()
        got.wait_send()
    keep.wait()
    put.wait()


def finish(cells_ref, sums_ref, samp_ref, refd_ref, gram_ref):
    samp_ref[...] = cells_ref[0:8, :]
    refd_ref[...] = cells_ref[8:16, :]
    for j in range(2):
        rows = jnp.concatenate([sums_ref[n, j * 8 : j * 8 + 8] for n in range(YXS)], axis=0)
        gram_ref[j * 128 : j * 128 + 128, :] = jnp.transpose(rows)


def shards(
    blocks, connectivity, basal_map, friction, elem_counts, obs_weight, sign_bits, cluster_ids
):
    vmem = pl.BlockSpec(memory_space=pltpu.VMEM)
    here = pl.BlockSpec(memory_space=pl.ANY)
    dma = pltpu.SemaphoreType.DMA
    cells, gram = pl.pallas_call(
        kernel,
        out_shape=(
            jax.ShapeDtypeStruct((16, 256), F32),
            jax.ShapeDtypeStruct((YXS, 16, 128), F32),
        ),
        in_specs=[here] * 4 + [pl.BlockSpec(memory_space=pltpu.SMEM)] + [here] * 3,
        out_specs=(here, here),
        scratch_shapes=[
            pltpu.VMEM((ELEMS, 64), I32),
            pltpu.VMEM((ELEMS, 64), I32),
            pltpu.VMEM((3, ELEMS, 64), F32),
            pltpu.VMEM((3, 4096), F32),
            pltpu.VMEM((8, 256), I32),
            pltpu.VMEM((1, 256), I32),
            pltpu.VMEM((ELEMS, 128), I32),
            pltpu.VMEM((16, 384), F32),
            pltpu.VMEM((ELEMS, DOF, DOF), BF16),
            pltpu.VMEM((256, 4096), BF16),
            pltpu.VMEM((4096, 256), BF16),
            pltpu.VMEM((128, 4096), BF16),
            pltpu.VMEM((4096, 128), BF16),
            pltpu.VMEM((128, 256), I32),
            pltpu.VMEM((128, 256), I32),
            pltpu.VMEM((256, 512), F32),
            pltpu.VMEM((128, 512), BF16),
            pltpu.VMEM((512, 128), BF16),
            pltpu.VMEM((384, 512), BF16),
            pltpu.VMEM((512, 384), BF16),
            pltpu.VMEM((256, 128), BF16),
            pltpu.VMEM((256, 128), BF16),
            pltpu.VMEM((256, 512), BF16),
            pltpu.VMEM((256, 512), BF16),
            pltpu.VMEM((256, 384), F32),
            pltpu.VMEM((96, 256), F32),
            pltpu.VMEM((336, 256), F32),
            pltpu.VMEM((96, 256), BF16),
            pltpu.VMEM((336, 256), BF16),
            pltpu.VMEM((256, 384), F32),
            pltpu.VMEM((256, 384), BF16),
            pltpu.VMEM((256, 512), BF16),
            pltpu.VMEM((256, 512), BF16),
            pltpu.VMEM((256, 512), BF16),
            pltpu.VMEM((256, 128), F32),
            pltpu.VMEM((3, 512), F32),
            pltpu.VMEM((16, 128), F32),
            pltpu.VMEM((16, 128), F32),
            pltpu.VMEM((ROUNDS, 96, 256), BF16),
            pltpu.VMEM((ROUNDS, 48, 256), BF16),
            pltpu.VMEM((ROUNDS, 48, 256), BF16),
            pltpu.VMEM((ROUNDS, 2, 8, 128), F32),
            pltpu.VMEM((ROUNDS, 8, 128), F32),
            pltpu.VMEM((ROUNDS, 8, 128), F32),
            pltpu.VMEM((POWER, ZS, 8, 128), F32),
            pltpu.VMEM((POWER, YXS, 8, 128), F32),
            pltpu.VMEM((GROUPS, 8, 384), F32),
            pltpu.VMEM((GROUPS, 8, 128), F32),
            pltpu.VMEM((GROUPS, 8, 128), F32),
            pltpu.VMEM((YXS, 16, 128), BF16),
            pltpu.VMEM((YXS, 16, 128), BF16),
            pltpu.VMEM((ZS, 16, 128), BF16),
            pltpu.VMEM((16, 128), F32),
            pltpu.VMEM((16, 256), F32),
            dma,
            dma((6,)),
            dma((2,)),
            dma((3,)),
            dma((3,)),
            dma((ROUNDS, 2)),
            dma((ROUNDS, 2)),
            dma((ROUNDS, 2)),
            dma((ROUNDS, 2)),
            dma((8,)),
            dma((POWER, 2, 8)),
            dma((3, GROUPS)),
            dma((3, GROUPS)),
            dma((3, 8)),
        ],
        compiler_params=pltpu.CompilerParams(
            collective_id=0, has_side_effects=True, vmem_limit_bytes=63 * 1024 * 1024
        ),
    )(
        blocks, connectivity, basal_map, friction.transpose(2, 0, 1), elem_counts,
        obs_weight.T, sign_bits.T, cluster_ids[None, :],
    )
    samp, refd, gram = pl.pallas_call(
        finish,
        out_shape=(
            jax.ShapeDtypeStruct((8, 256), F32),
            jax.ShapeDtypeStruct((8, 256), F32),
            jax.ShapeDtypeStruct((256, 64), F32),
        ),
        in_specs=[vmem, vmem],
        out_specs=(vmem, vmem, vmem),
    )(cells, gram)
    return samp.T, refd.T, gram.reshape(8, 32, 64).transpose(2, 0, 1)


def solution(mesh):
    in_specs = (
        P("tiles", None, None),
        P("tiles", None),
        P("tiles", None),
        P("tiles", None, None),
        P("tiles"),
        P("tiles", None),
        P("tiles", "probes"),
        P("tiles"),
    )
    out_specs = (P("tiles", "probes"), P("tiles", "probes"), P(None, "probes", None))
    return jax.shard_map(shards, mesh=mesh, in_specs=in_specs, out_specs=out_specs, check_vma=False)
```
